32 devices in a mesh: dp: 4 (over z), mp: 8 (over y, x, core).
Axes of the slice: x: 2, y: 2, z: 4, core: 2. Of those that a mesh axis runs over, the one named last changes fastest.
Arguments:
- tokens: bfloat16 [32768, 1024], P(('dp', 'mp')), may hold values from -6 to 6
- segment_ids: int32 [32, 1024], P(('dp', 'mp')), may hold values from 0 to 7, never falling along the last dimension, each value on 1 to 512 neighbouring positions
- pad_mask: int32 [32, 1024], P(('dp', 'mp')), may hold values 0 or 1
- cotangent: bfloat16 [32768, 1024], P(('dp', 'mp')), may hold values from -6 to 6
- w_query: bfloat16 [1024, 1024], replicated, may hold values from -0.1875 to 0.1875
- w_key: bfloat16 [1024, 1024], replicated, may hold values from -0.1875 to 0.1875
- w_value: bfloat16 [1024, 1024], replicated, may hold values from -0.1875 to 0.1875
- w_out: bfloat16 [1024, 1024], replicated, may hold values from -1 to 1
- w_in: bfloat16 [1024, 4096], P(None, 'mp'), may hold values from -0.1875 to 0.1875
- w_back: bfloat16 [4096, 1024], P('mp'), may hold values from -0.125 to 0.125
- params_main: float32 [8, 1024], replicated, as said below
- params_hidden: float32 [4096], P('mp'), may hold values from -3 to 3
- first_main: float32 [8, 1024], replicated, may hold values from -10 to 10
- second_main: float32 [8, 1024], replicated, may hold values from 3.2768 to 13.1072
- first_hidden: float32 [4096], P('mp'), may hold values from -10 to 10
- second_hidden: float32 [4096], P('mp'), may hold values from 3.2768 to 13.1072
- average_main: float32 [8, 1024], replicated, as said below
- average_hidden: float32 [4096], P('mp'), may hold values from -3 to 3
Outputs:
- activations: float32 [32768, 1024], P(('dp', 'mp'))
- input_grad: float32 [32768, 1024], P(('dp', 'mp'))
- grad_norm: float32 [], replicated
- grads_main: float32 [8, 1024], replicated
- grads_hidden: float32 [4096], P('mp')
- first_main_new: float32 [8, 1024], replicated
- second_main_new: float32 [8, 1024], replicated
- first_hidden_new: float32 [4096], P('mp')
- second_hidden_new: float32 [4096], P('mp')
- params_main_new: float32 [8, 1024], replicated
- params_hidden_new: float32 [4096], P('mp')
- copy_main: bfloat16 [8, 1024], replicated
- copy_hidden: bfloat16 [4096], P('mp')
- average_main_new: float32 [8, 1024], replicated
- average_hidden_new: float32 [4096], P('mp')
The draws below stay inside these ranges and needn't reach their ends.
Inputs may be any that keep to these rules, and one draw needn't show every extreme that they name: `segment_ids`: each row is one packed sequence; its segment numbers never fall along the row and it holds 8 segments. `params_main`: rows 3 and 6 are gains near 1, the others biases of both signs. `average_main`: rows 3 and 6 are gains near 1, the others biases of both signs.
All inputs are finite; a program needn't handle non-finite values. No bound on the sum of `pad_mask` on one device may be relied on, other than what follows from the above.
Results may differ from the reference program's by a relative error of at most 0.017.
Values may be sent and summed in bfloat16 or wider, within the bound.
No kernel may reach another device: no remote copies, remote signals or barrier semaphores. Data moves between devices by JAX's collectives and lax.ppermute only.
A program may use at most 320 MiB of HBM per device.

```python
import math
import jax
import jax.numpy as jnp
import numpy as np
from jax import lax

D = 1024
HEADS = 16
HEAD = 64
FF = 4096
LEN = 1024
SEGS = 8
STEP = 5
SEQ_DEV = 1
SEQS = 32
TOKENS = 32768


def bias_table(key):
    rows = jnp.arange(8)[:, None]
    gain_rows = (rows == 3) | (rows == 6)
    biases = 0.5 * jax.random.normal(jax.random.fold_in(key, 1), (8, D), jnp.float32)
    gains = jax.random.uniform(jax.random.fold_in(key, 2), (8, D), jnp.float32, 0.7, 1.3)
    return jnp.where(gain_rows, gains, biases)


def draw_params_main(key, part):
    return bias_table(jax.random.fold_in(key, 11))


def draw_average_main(key, part):
    return bias_table(jax.random.fold_in(key, 12))


def set_ends(result, rng, smallest, high):
    spot = [jax.random.randint(jax.random.fold_in(rng, axis), (), 0, length) for axis, length in enumerate(result.shape)]
    longest = result.shape.index(max(result.shape))
    neighbour = spot[:longest] + [(spot[longest] + 1) % result.shape[longest]] + spot[longest + 1:]
    return result.at[tuple(spot)].set(smallest).at[tuple(neighbour)].set(high)


def block_scale(own_key, shape, pieces, least, largest):
    gain, own = 1.0, jax.random.fold_in(own_key, 6)
    for axis_at, parts in pieces:
        heights = jnp.exp(jax.random.uniform(jax.random.fold_in(own, axis_at), (parts,), jnp.float32, least / len(pieces), largest / len(pieces)))
        gain = gain * jnp.repeat(heights, shape[axis_at] // parts).reshape([-1 if axis == axis_at else 1 for axis in range(len(shape))])
    return gain


def profile(number_of, total, bound, skew):
    weights = [(1 << 20) // math.isqrt(rank ** skew) + 1 for rank in range(2, number_of + 1)]
    spare, counts = total - bound - (number_of - 1), [1] * (number_of - 1)
    while spare > 0:
        free = [i for i in range(number_of - 1) if counts[i] < bound]
        mass, left = sum([weights[i] for i in free]), spare
        for i in free:
            extra = min(bound - counts[i], max(1, left * weights[i] // mass), spare)
            counts[i] = counts[i] + extra
            spare = spare - extra
    return np.array([bound] + counts)


def ragged(key, number_of, total, reach, lean):
    if number_of == 2:
        one = jax.random.randint(key, (), max(1, total - reach), min(reach, total - 1) + 1)
        return jnp.stack([one, total - one])
    tallies = jnp.asarray(profile(number_of, total, reach, lean), jnp.int32)
    twos = (number_of - 1) // 2
    donor, taker = tallies[1:1 + 2 * twos:2], tallies[2:2 + 2 * twos:2]
    slack = jnp.minimum(donor - 1, reach - taker)
    passed = jax.random.randint(jax.random.fold_in(key, 1), (twos,), 0, 1 << 20) % (slack + 1)
    tallies = tallies.at[1:1 + 2 * twos:2].set(donor - passed).at[2:2 + 2 * twos:2].set(taker + passed)
    return tallies[jax.random.permutation(jax.random.fold_in(key, 2), number_of)]


def scatter_about(own_key, shape, scale, most, pieces=(), kind=jnp.bfloat16):
    values = jax.random.normal(own_key, shape, jnp.float32) * scale
    if len(pieces) > 0:
        values = block_scale(own_key, shape, pieces, -0.22, 0.18) * values
    return jnp.clip(values, min=-most, max=most).astype(kind)


def setup_inputs(seed: int = 0) -> dict:
    streams_of = jax.random.split(jax.random.key(seed), 19)
    return {
        "tokens": scatter_about(streams_of[0], (TOKENS, D), 1.0, 6.0, ((0, 32),)),
        "segment_ids": jax.vmap(lambda own: jnp.searchsorted(jnp.cumsum(ragged(own, SEGS, LEN, LEN // 2, 1)), jnp.arange(LEN), side="right"))(jax.random.split(streams_of[1], SEQS)).reshape((SEQS, LEN)).astype(jnp.int32),
        "pad_mask": set_ends((jax.random.randint(streams_of[2], (SEQS, LEN), 0, 8) < 7).astype(jnp.int32), jax.random.fold_in(streams_of[2], 1), 0, 1),
        "cotangent": scatter_about(streams_of[3], (TOKENS, D), 1.0, 6.0, ((0, 32),)),
        "w_query": scatter_about(streams_of[4], (D, D), D ** -0.5, 0.1875),
        "w_key": scatter_about(streams_of[5], (D, D), D ** -0.5, 0.1875),
        "w_value": scatter_about(streams_of[6], (D, D), D ** -0.5, 0.1875),
        "w_out": scatter_about(streams_of[7], (D, D), (D * SEGS * 4 // LEN) ** -0.5, 1.0),
        "w_in": scatter_about(streams_of[8], (D, FF), D ** -0.5, 0.1875, ((1, 8),)),
        "w_back": scatter_about(streams_of[9], (FF, D), (FF // 2) ** -0.5, 0.125, ((0, 8),)),
        "params_main": draw_params_main(jax.random.fold_in(streams_of[18], 71), 0),
        "params_hidden": scatter_about(streams_of[11], (FF,), 0.5, 3.0, ((0, 8),), jnp.float32),
        "first_main": scatter_about(streams_of[12], (8, D), (0.01 * TOKENS ** 0.5), 10.0, (), jnp.float32),
        "second_main": jnp.clip(jnp.exp(jax.random.uniform(streams_of[13], (8, D), jnp.float32, math.log(3.2768), math.log(13.1072))), 3.2768, 13.1072),
        "first_hidden": scatter_about(streams_of[14], (FF,), (0.01 * TOKENS ** 0.5), 10.0, ((0, 8),), jnp.float32),
        "second_hidden": jnp.clip(jnp.exp(math.log(13.1072) - 1.3862944 * jax.random.uniform(streams_of[15], (FF,), jnp.float32) ** block_scale(streams_of[15], (FF,), ((0, 8),), -0.2, 0.2)), 3.2768, 13.1072),
        "average_main": draw_average_main(jax.random.fold_in(streams_of[18], 71), 0),
        "average_hidden": scatter_about(streams_of[17], (FF,), 0.5, 3.0, ((0, 8),), jnp.float32),
    }


@jax.custom_vjp
def low(v):
    return lax.optimization_barrier(v.astype(jnp.bfloat16)).astype(jnp.float32)

@jax.custom_vjp
def low_back(v):
    return v

def low_keep(v):
    return (low(v), None)

def low_pass(kept, grad):
    return (grad,)

def back_keep(v):
    return (v, None)

def back_low(kept, grad):
    return (low(grad),)
low.defvjp(low_keep, low_pass)
low_back.defvjp(back_keep, back_low)

def matmul(left, right):
    return jnp.dot(left, right, precision=lax.Precision.HIGHEST, preferred_element_type=jnp.float32)

def normed(resid):
    center = resid - lax.optimization_barrier(jnp.mean(resid, axis=-1, keepdims=True))
    return center * lax.rsqrt(lax.optimization_barrier(jnp.mean(center * center, axis=-1, keepdims=True)) + 1e-05)

def attend(args):
    query, keys, values, vis = args
    scores = jnp.einsum('qhd,khd->hqk', query, keys, precision=lax.Precision.HIGHEST) * 0.125
    scores = jnp.where(vis[None], low_back(scores), -1000000000.0)
    probs = jax.nn.softmax(scores, axis=-1)
    mixed = jnp.einsum('hqk,khd->qhd', low(probs), values, precision=lax.Precision.HIGHEST)
    return mixed.reshape(LEN, D)

def forward(xin, vis, pmain, phid, weights):
    w_query, w_key, w_value, w_out, w_in, w_back = weights
    rows = xin.shape[0]
    query = low(low_back(matmul(xin, w_query)) + pmain[0])
    keys = low(low_back(matmul(xin, w_key)))
    values = low(low_back(matmul(xin, w_value)) + pmain[1])
    group = rows // LEN
    shape = (group, LEN, HEADS, HEAD)
    mixed = lax.map(jax.checkpoint(attend), (query.reshape(shape), keys.reshape(shape), values.reshape(shape), vis))
    mixed = low(low_back(mixed.reshape(rows, D)))
    resid = xin + low_back(matmul(mixed, w_out)) + pmain[2]
    hidden_in = normed(resid) * pmain[3] + pmain[4]
    zeta = low_back(matmul(low(hidden_in), w_in)) + phid
    upper = low(jax.nn.gelu(zeta, approximate=False))
    ffn = low_back(matmul(upper, w_back)) + pmain[5]
    return normed(hidden_in + ffn) * pmain[6] + pmain[7]

def adam_step(grad, first, second, param, average):
    first_new = 0.5 * first + 0.5 * grad
    second_new = 0.5 * second + 0.5 * grad * grad
    corr = 1.0 - 0.5 ** STEP
    param_new = param - 0.25 * (first_new / corr / (jnp.sqrt(second_new / corr) + 1e-08) + 0.01 * param)
    return (first_new, second_new, param_new, param_new.astype(jnp.bfloat16), 0.8 * average + 0.2 * param_new)

def reference(tokens, segment_ids, pad_mask, cotangent, w_query, w_key, w_value, w_out, w_in, w_back, params_main, params_hidden, first_main, second_main, first_hidden, second_hidden, average_main, average_hidden):
    weights = tuple((w.astype(jnp.float32) for w in (w_query, w_key, w_value, w_out, w_in, w_back)))
    groups = SEQS // SEQ_DEV
    xs = tokens.astype(jnp.float32).reshape(groups, SEQ_DEV * LEN, D)
    cots = cotangent.astype(jnp.float32).reshape(groups, SEQ_DEV * LEN, D)
    segs = segment_ids.reshape(groups, SEQ_DEV, LEN)
    pads = pad_mask.reshape(groups, SEQ_DEV, LEN)
    diag = jnp.eye(LEN, dtype=jnp.bool_)

    def one_group(carry, item):
        xin, cot, seg, pad = item
        vis = (seg[:, :, None] == seg[:, None, :]) & ((pad[:, None, :] == 1) | diag[None])

        def run(xval, pmain, phid):
            return forward(xval, vis, pmain, phid, weights)
        outv, pull = jax.vjp(run, xin, params_main, params_hidden)
        cot = cot * pad.reshape(SEQ_DEV * LEN)[:, None].astype(jnp.float32)
        dx, dmain, dhid = pull(cot)
        return ((carry[0] + dmain, carry[1] + dhid), (outv, dx))
    init = (jnp.zeros((8, D), jnp.float32), jnp.zeros((FF,), jnp.float32))
    (gmain, ghid), (outs, dxs) = lax.scan(one_group, init, (xs, cots, segs, pads))
    grad_norm = jnp.sqrt(jnp.sum(gmain * gmain) + jnp.sum(ghid * ghid))
    limit = 0.01 * jnp.sqrt(jnp.float32(TOKENS * (8 * D + FF)))
    factor = jnp.minimum(1.0, limit / (grad_norm + 1e-06))
    gmain = gmain * factor
    ghid = ghid * factor
    fm, sm, pm, cm, am = adam_step(gmain, first_main, second_main, params_main, average_main)
    fh, sh, ph, ch, ah = adam_step(ghid, first_hidden, second_hidden, params_hidden, average_hidden)
    return (outs.reshape(TOKENS, D), dxs.reshape(TOKENS, D), grad_norm, gmain, ghid, fm, sm, fh, sh, pm, ph, cm, ch, am, ah)
```

```python
import math

import jax
import jax.numpy as jnp
from jax import lax
from jax.sharding import PartitionSpec as P

D = 1024
HEADS = 16
HEAD = 64
QBLOCK = 512
STEP = 5


def product(left, right):
    return jnp.dot(left, right, preferred_element_type=jnp.float32)


def normed(resid):
    center = resid - jnp.mean(resid, axis=-1, keepdims=True)
    factor = lax.rsqrt(jnp.mean(center * center, axis=-1, keepdims=True) + 1e-05)
    return (center * factor, factor)


def norm_back(normal, factor, dnorm):
    return factor * (
        dnorm
        - jnp.mean(dnorm, axis=-1, keepdims=True)
        - normal * jnp.mean(dnorm * normal, axis=-1, keepdims=True)
    )


def adam_step(grad, first, second, param, average):
    first_new = 0.5 * first + 0.5 * grad
    second_new = 0.5 * second + 0.5 * grad * grad
    corr = 1.0 - 0.5**STEP
    param_new = param - 0.25 * (
        first_new / corr / (jnp.sqrt(second_new / corr) + 1e-08) + 0.01 * param
    )
    return (
        first_new,
        second_new,
        param_new,
        param_new.astype(jnp.bfloat16),
        0.8 * average + 0.2 * param_new,
    )


def gelu_exact(value):
    return jax.nn.gelu(value, approximate=False)


def on_device(
    tokens,
    segment_ids,
    pad_mask,
    cotangent,
    w_query,
    w_key,
    w_value,
    w_out,
    w_in,
    w_back,
    params_main,
    params_hidden,
    first_main,
    second_main,
    first_hidden,
    second_hidden,
    average_main,
    average_hidden,
):
    rows_all = tokens.shape[0]
    seqs = segment_ids.shape[0]
    length = segment_ids.shape[1]
    block = QBLOCK
    nblock = length // block
    positions = jnp.arange(length)
    width = params_hidden.shape[0]
    total_hidden = width * lax.axis_size("mp")
    query = (product(tokens, w_query) + params_main[0]).astype(jnp.bfloat16)
    keys = product(tokens, w_key).astype(jnp.bfloat16)
    values = (product(tokens, w_value) + params_main[1]).astype(jnp.bfloat16)
    q_blocks = query.reshape(seqs, nblock, block, HEADS, HEAD)
    k_seqs = keys.reshape(seqs, length, HEADS, HEAD)
    v_seqs = values.reshape(seqs, length, HEADS, HEAD)

    def visible(seg_row, pad_row, index):
        seg_query = lax.dynamic_slice_in_dim(seg_row, index * block, block)
        query_pos = index * block + jnp.arange(block)
        return (seg_query[:, None] == seg_row[None, :]) & (
            (pad_row[None, :] == 1) | (query_pos[:, None] == positions[None, :])
        )

    def scores_of(q_blk, k_seq, vis):
        scores = (
            jnp.einsum("qhd,khd->hqk", q_blk, k_seq, preferred_element_type=jnp.float32) * 0.125
        )
        return jnp.where(vis[None], scores, -1000000000.0)

    def attend_seq(args):
        q_seq, k_seq, v_seq, seg_row, pad_row = args

        def one_block(index):
            scores = scores_of(q_seq[index], k_seq, visible(seg_row, pad_row, index))
            top = jnp.max(scores, axis=-1, keepdims=True)
            expd = jnp.exp(scores - top)
            total = jnp.sum(expd, axis=-1, keepdims=True)
            probs = (expd / total).astype(jnp.bfloat16)
            mixed = jnp.einsum("hqk,khd->qhd", probs, v_seq, preferred_element_type=jnp.float32)
            return (mixed, (top + jnp.log(total))[..., 0])

        return lax.map(one_block, jnp.arange(nblock))

    mixed, lse = lax.map(attend_seq, (q_blocks, k_seqs, v_seqs, segment_ids, pad_mask))
    mixed_low = mixed.reshape(rows_all, D).astype(jnp.bfloat16)
    resid_one = tokens.astype(jnp.float32) + product(mixed_low, w_out) + params_main[2]
    normal_one, factor_one = normed(resid_one)
    hidden_in = normal_one * params_main[3] + params_main[4]
    hidden_low = hidden_in.astype(jnp.bfloat16)
    dy = cotangent.astype(jnp.float32) * pad_mask.reshape(rows_all)[:, None].astype(jnp.float32)
    in_all = lax.all_gather(w_in, "mp", axis=0, tiled=False)
    back_all = lax.all_gather(w_back, "mp", axis=0, tiled=False)
    bias_all = lax.all_gather(params_hidden, "mp", axis=0, tiled=False)
    zeta = jnp.einsum("td,jdh->jth", hidden_low, in_all, preferred_element_type=jnp.float32) + bias_all[:, None, :]
    upper, gelu_pull = jax.vjp(gelu_exact, zeta)
    upper_low = upper.astype(jnp.bfloat16)
    ffn = (
        jnp.einsum("jth,jhd->td", upper_low, back_all, preferred_element_type=jnp.float32)
        + params_main[5]
    )
    normal_two, factor_two = normed(hidden_in + ffn)
    dresid_two = norm_back(normal_two, factor_two, dy * params_main[6])
    dupper = jnp.einsum(
        "td,jhd->jth", dresid_two.astype(jnp.bfloat16), back_all, preferred_element_type=jnp.float32
    )
    dzeta = gelu_pull(dupper)[0]
    dzeta_low = dzeta.astype(jnp.bfloat16)
    dhidden = dresid_two + jnp.einsum(
        "jth,jdh->td", dzeta_low, in_all, preferred_element_type=jnp.float32
    )
    hidden_vec = jnp.sum(dzeta, axis=1).reshape(total_hidden)
    activations = normal_two * params_main[6] + params_main[7]
    grad_gain_two = jnp.sum(dy * normal_two, axis=0)
    grad_shift_two = jnp.sum(dy, axis=0)
    grad_bias_two = jnp.sum(dresid_two, axis=0)
    grad_gain_one = jnp.sum(dhidden * normal_one, axis=0)
    grad_shift_one = jnp.sum(dhidden, axis=0)
    dresid_one = norm_back(normal_one, factor_one, dhidden * params_main[3])
    grad_bias_out = jnp.sum(dresid_one, axis=0)
    dmixed = product(dresid_one.astype(jnp.bfloat16), w_out.T).astype(jnp.bfloat16)
    d_blocks = dmixed.reshape(seqs, nblock, block, HEADS, HEAD)

    def back_seq(args):
        q_seq, k_seq, v_seq, d_seq, l_seq, seg_row, pad_row = args

        def one_step(carry, index):
            dkeys, dvalues = carry
            q_blk = q_seq[index]
            d_blk = d_seq[index]
            scores = scores_of(q_blk, k_seq, visible(seg_row, pad_row, index))
            probs = jnp.exp(scores - l_seq[index][..., None])
            dprobs = jnp.einsum("qhd,khd->hqk", d_blk, v_seq, preferred_element_type=jnp.float32)
            delta = jnp.sum(probs * dprobs, axis=-1, keepdims=True)
            dscores = (probs * (dprobs - delta)).astype(jnp.bfloat16)
            dquery = 0.125 * jnp.einsum(
                "hqk,khd->qhd", dscores, k_seq, preferred_element_type=jnp.float32
            )
            dkeys = dkeys + 0.125 * jnp.einsum(
                "hqk,qhd->khd", dscores, q_blk, preferred_element_type=jnp.float32
            )
            dvalues = dvalues + jnp.einsum(
                "hqk,qhd->khd",
                probs.astype(jnp.bfloat16),
                d_blk,
                preferred_element_type=jnp.float32,
            )
            return ((dkeys, dvalues), dquery)

        empty = jnp.zeros((length, HEADS, HEAD), jnp.float32)
        (dkeys, dvalues), dquery = lax.scan(one_step, (empty, empty), jnp.arange(nblock))
        return (dquery, dkeys, dvalues)

    dquery, dkeys, dvalues = lax.map(
        back_seq, (q_blocks, k_seqs, v_seqs, d_blocks, lse, segment_ids, pad_mask)
    )
    dquery = dquery.reshape(rows_all, D)
    dkeys = dkeys.reshape(rows_all, D)
    dvalues = dvalues.reshape(rows_all, D)
    input_grad = dresid_one + product(dquery.astype(jnp.bfloat16), w_query.T)
    input_grad = input_grad + product(dkeys.astype(jnp.bfloat16), w_key.T)
    input_grad = input_grad + product(dvalues.astype(jnp.bfloat16), w_value.T)
    local_main = jnp.stack(
        [
            jnp.sum(dquery, axis=0),
            jnp.sum(dvalues, axis=0),
            grad_bias_out,
            grad_gain_one,
            grad_shift_one,
            grad_bias_two,
            grad_gain_two,
            grad_shift_two,
        ]
    )
    grad_main, hidden_total = lax.psum((local_main, hidden_vec), ("dp", "mp"))
    grad_hid = lax.dynamic_slice_in_dim(hidden_total, lax.axis_index("mp") * width, width, 0)
    grad_norm = jnp.sqrt(jnp.sum(grad_main * grad_main) + jnp.sum(hidden_total * hidden_total))
    tokens_all = rows_all * lax.axis_size("dp") * lax.axis_size("mp")
    limit = 0.01 * math.sqrt(tokens_all * (8 * D + total_hidden))
    scale_factor = jnp.minimum(1.0, limit / (grad_norm + 1e-06))
    grad_main = grad_main * scale_factor
    grad_hid = grad_hid * scale_factor
    fm, sm, pm, cm, am = adam_step(grad_main, first_main, second_main, params_main, average_main)
    fh, sh, ph, ch, ah = adam_step(
        grad_hid, first_hidden, second_hidden, params_hidden, average_hidden
    )
    return (
        activations,
        input_grad,
        grad_norm,
        grad_main,
        grad_hid,
        fm,
        sm,
        fh,
        sh,
        pm,
        ph,
        cm,
        ch,
        am,
        ah,
    )


def solution(mesh):
    placed = (
        P(("dp", "mp"), None),
        P(("dp", "mp"), None),
        P(("dp", "mp"), None),
        P(("dp", "mp"), None),
        P(),
        P(),
        P(),
        P(),
        P(None, "mp"),
        P("mp", None),
        P(),
        P("mp"),
        P(),
        P(),
        P("mp"),
        P("mp"),
        P(),
        P("mp"),
    )
    return jax.shard_map(
        on_device,
        mesh=mesh,
        in_specs=placed,
        out_specs=(
            P(("dp", "mp"), None),
            P(("dp", "mp"), None),
            P(),
            P(),
            P("mp"),
            P(),
            P(),
            P("mp"),
            P("mp"),
            P(),
            P("mp"),
            P(),
            P("mp"),
            P(),
            P("mp"),
        ),
        check_vma=False,
    )
```

```python
import functools
import math

import jax
import jax.numpy as jnp
from jax import lax
from jax.experimental import pallas as pl
from jax.experimental.pallas import tpu as pltpu
from jax.sharding import PartitionSpec as P

STEP = 5
f32, bf16 = jnp.float32, jnp.bfloat16
NN = (((1,), (0,)), ((), ()))
NT = (((1,), (1,)), ((), ()))
DN_NT = NT

BLK = 128
PAIR = 128
NEG = -1e9
ALLOWED = (2, 3, 4, 5, 6, 8)


def windows(seg_row, blk, allowed):
    length = seg_row.shape[0]
    nb = length // blk
    first = seg_row[::blk]
    last = seg_row[blk - 1 :: blk]
    lo = jnp.sum(seg_row[None, :] < first[:, None], axis=1)
    hi = jnp.sum(seg_row[None, :] <= last[:, None], axis=1)
    start = lo // blk
    count = (hi + blk - 1) // blk - start
    allowed_arr = jnp.array(allowed)
    variant = jnp.sum(allowed_arr[None, :] < count[:, None], axis=1)
    size = allowed_arr[variant]
    start = jnp.minimum(start, nb - size)
    return jnp.stack([start, variant]).astype(jnp.int32)


def halves(x):
    lane = lax.broadcasted_iota(jnp.int32, x.shape, 1)
    zero = jnp.zeros_like(x)
    return jnp.concatenate([jnp.where(lane < 64, x, zero), jnp.where(lane >= 64, x, zero)], axis=0)


def fill_bias(bias_ref, segcol_ref, segrow_ref, i, start, width):
    rows = pl.ds(start * BLK, width)
    kcode = segcol_ref[rows, :]
    qseg = segrow_ref[:, pl.ds(pl.multiple_of(i * BLK, BLK), BLK)]
    kpos = start * BLK + lax.broadcasted_iota(jnp.int32, (width, BLK), 0)
    qpos = i * BLK + lax.broadcasted_iota(jnp.int32, (width, BLK), 1)
    vis = (kcode == qseg) | (kpos == qpos)
    bias_ref[pl.ds(0, width), :] = jnp.where(vis, 0.0, NEG).astype(f32)


def fwd_kernel(allowed, npair, unroll, win_ref, q_ref, k_ref, v_ref, segcol_ref, segrow_ref, o_ref, lse_ref, vt_ref, bias_ref):
    i = pl.program_id(0)

    @pl.when(i == 0)
    def _():
        for h in range(npair):
            vt_ref[h * PAIR : (h + 1) * PAIR, :] = v_ref[:, h * PAIR : (h + 1) * PAIR].T

    start = win_ref[0, i]
    variant = win_ref[1, i]
    for n, size in enumerate(allowed):
        width = size * BLK

        @pl.when(variant == n)
        def _(width=width):
            fill_bias(bias_ref, segcol_ref, segrow_ref, i, start, width)
            rows = pl.ds(pl.multiple_of(start * BLK, BLK), width)

            def pair(h):
                cols = pl.ds(pl.multiple_of(h * PAIR, PAIR), PAIR)
                qbd = halves(q_ref[:, cols])
                s = lax.dot_general(k_ref[rows, cols], qbd, DN_NT, preferred_element_type=f32)
                b = bias_ref[pl.ds(0, width), :]
                s = s * 0.125 + jnp.concatenate([b, b], axis=1)
                top = jnp.max(s, axis=0, keepdims=True)
                p = jnp.exp(s - top)
                tot = jnp.sum(p, axis=0, keepdims=True)
                ot = lax.dot_general(
                    vt_ref[cols, rows], p.astype(bf16), (((1,), (0,)), ((), ())), preferred_element_type=f32
                )
                ot = ot * (1.0 / tot)
                ot = jnp.concatenate([ot[:64, :BLK], ot[64:, BLK:]], axis=0)
                o_ref[:, cols] = ot.T.astype(bf16)
                lse_ref[0, pl.ds(h, 1), :] = top + jnp.log(tot)

            def body(t, c):
                for u in range(unroll):
                    pair(t * unroll + u)
                return c

            lax.fori_loop(0, npair // unroll, body, 0)


def attn_fwd(q, k, v, seg, pad, allowed=(1, 2, 3, 4, 5, 6, 7, 8), unroll=1):
    length, d = q.shape
    nb, npair = length // BLK, d // PAIR
    win = windows(seg, BLK, allowed)
    segcol = jnp.where(pad == 1, seg, -1)[:, None]
    full = lambda: pl.BlockSpec((length, d), lambda i, w: (0, 0))
    return pl.pallas_call(
        functools.partial(fwd_kernel, allowed, npair, unroll),
        out_shape=(jax.ShapeDtypeStruct((length, d), bf16), jax.ShapeDtypeStruct((nb, npair, 2 * BLK), f32)),
        grid_spec=pltpu.PrefetchScalarGridSpec(
            num_scalar_prefetch=1, grid=(nb,),
            in_specs=[pl.BlockSpec((BLK, d), lambda i, w: (i, 0)), full(), full(),
                      pl.BlockSpec((length, 1), lambda i, w: (0, 0)), pl.BlockSpec((1, length), lambda i, w: (0, 0))],
            out_specs=[pl.BlockSpec((BLK, d), lambda i, w: (i, 0)), pl.BlockSpec((1, npair, 2 * BLK), lambda i, w: (i, 0, 0))],
            scratch_shapes=[pltpu.VMEM((d, length), bf16), pltpu.VMEM((length, BLK), f32)]),
        compiler_params=pltpu.CompilerParams(vmem_limit_bytes=48 << 20),
        name="attend",
    )(win, q, k, v, segcol, seg[None, :])


def bwd_kernel(allowed, npair, unroll, win_ref, q_ref, k_ref, v_ref, do_ref, lse_ref, segcol_ref, segrow_ref,
               dq_ref, dk_ref, dv_ref, kt_ref, bias_ref):
    i = pl.program_id(0)

    @pl.when(i == 0)
    def _():
        for h in range(npair):
            kt_ref[h * PAIR : (h + 1) * PAIR, :] = k_ref[:, h * PAIR : (h + 1) * PAIR].T
        dk_ref[...] = jnp.zeros_like(dk_ref)
        dv_ref[...] = jnp.zeros_like(dv_ref)

    start = win_ref[0, i]
    variant = win_ref[1, i]
    for n, size in enumerate(allowed):
        width = size * BLK

        @pl.when(variant == n)
        def _(width=width):
            fill_bias(bias_ref, segcol_ref, segrow_ref, i, start, width)
            rows = pl.ds(pl.multiple_of(start * BLK, BLK), width)

            def pair(h):
                cols = pl.ds(pl.multiple_of(h * PAIR, PAIR), PAIR)
                qbd = halves(q_ref[:, cols])
                dobd = halves(do_ref[:, cols])
                s = lax.dot_general(k_ref[rows, cols], qbd, DN_NT, preferred_element_type=f32)
                dp = lax.dot_general(v_ref[rows, cols], dobd, DN_NT, preferred_element_type=f32)
                b = bias_ref[pl.ds(0, width), :]
                lse = lse_ref[0, pl.ds(h, 1), :]
                p = jnp.exp(s * 0.125 + jnp.concatenate([b, b], axis=1) - lse)
                t = p * dp
                delta = jnp.sum(t, axis=0, keepdims=True)
                ds = (t - p * delta).astype(bf16)
                nn = (((1,), (0,)), ((), ()))
                dv_ref[rows, cols] += lax.dot_general(p.astype(bf16), dobd, nn, preferred_element_type=f32)
                dk_ref[rows, cols] += 0.125 * lax.dot_general(ds, qbd, nn, preferred_element_type=f32)
                dqt = lax.dot_general(kt_ref[cols, rows], ds, nn, preferred_element_type=f32)
                dqt = jnp.concatenate([dqt[:64, :BLK], dqt[64:, BLK:]], axis=0)
                dq_ref[:, cols] = 0.125 * dqt.T

            def body(t, c):
                for u in range(unroll):
                    pair(t * unroll + u)
                return c

            lax.fori_loop(0, npair // unroll, body, 0)


def attn_bwd(q, k, v, do, lse, seg, pad, allowed=(1, 2, 3, 4, 5, 6, 7, 8), unroll=1):
    length, d = q.shape
    nb, npair = length // BLK, d // PAIR
    win = windows(seg, BLK, allowed)
    segcol = jnp.where(pad == 1, seg, -1)[:, None]
    full = lambda: pl.BlockSpec((length, d), lambda i, w: (0, 0))
    row = lambda: pl.BlockSpec((BLK, d), lambda i, w: (i, 0))
    return pl.pallas_call(
        functools.partial(bwd_kernel, allowed, npair, unroll),
        out_shape=tuple(jax.ShapeDtypeStruct((length, d), f32) for _ in range(3)),
        grid_spec=pltpu.PrefetchScalarGridSpec(
            num_scalar_prefetch=1, grid=(nb,),
            in_specs=[row(), full(), full(), row(), pl.BlockSpec((1, npair, 2 * BLK), lambda i, w: (i, 0, 0)),
                      pl.BlockSpec((length, 1), lambda i, w: (0, 0)), pl.BlockSpec((1, length), lambda i, w: (0, 0))],
            out_specs=[row(), full(), full()],
            scratch_shapes=[pltpu.VMEM((d, length), bf16), pltpu.VMEM((length, BLK), f32)]),
        compiler_params=pltpu.CompilerParams(vmem_limit_bytes=56 << 20),
        name="attend_back",
    )(win, q, k, v, do, lse, segcol, seg[None, :])


def dot(a, b, dims=NN):
    return lax.dot_general(a, b, dims, preferred_element_type=f32)


def gelu_both(z):
    x = jnp.abs(z) * 0.7071067811865476
    e = jnp.exp(-0.5 * z * z)
    t = 1.0 / (1.0 + 0.3275911 * x)
    poly = t * (0.254829592 + t * (-0.284496736 + t * (1.421413741 + t * (-1.453152027 + t * 1.061405429))))
    tail = 0.5 * poly * e
    phi = jnp.where(z >= 0, 1.0 - tail, tail)
    return z * phi, phi + z * (0.3989422804014327 * e)


def normed(r):
    center = r - jnp.mean(r, axis=-1, keepdims=True)
    factor = lax.rsqrt(jnp.mean(center * center, axis=-1, keepdims=True) + 1e-05)
    return center * factor, factor


def norm_back(normal, factor, dn):
    return factor * (
        dn - jnp.mean(dn, axis=-1, keepdims=True) - normal * jnp.mean(dn * normal, axis=-1, keepdims=True)
    )


def mid_kernel(rchunk, sub, a_ref, x_ref, cot_ref, pad_ref, wout_ref, win_hbm, wback_hbm, b1_ref, pm_ref,
               act_ref, dr1_ref, da_ref, stat_ref, db1_ref,
               win_ref, wback_ref, sem, slope_ref, n1_ref, rs1_ref, low_ref, sum_ref):
    i = pl.program_id(0)
    nchunk, _, width = win_ref.shape
    rows_all = x_ref.shape[0]
    steps = rows_all // rchunk

    def copy_in(j):
        return pltpu.make_async_copy(win_hbm.at[j], win_ref.at[j], sem.at[0, j])

    def copy_back(j):
        return pltpu.make_async_copy(wback_hbm.at[j], wback_ref.at[j], sem.at[1, j])

    @pl.when(i == 0)
    def _():
        for j in range(nchunk):
            copy_in(j).start()
            copy_back(j).start()
        stat_ref[...] = jnp.zeros_like(stat_ref)
        db1_ref[...] = jnp.zeros_like(db1_ref)

    row = lambda n: pm_ref[n : n + 1, :]

    def add_stat(n, v):
        stat_ref[n : n + 1, :] += jnp.sum(v, axis=0, keepdims=True)

    def first(c, t):
        rows = pl.ds(pl.multiple_of(c * rchunk, rchunk), rchunk)
        r = x_ref[rows, :].astype(f32) + dot(a_ref[rows, :], wout_ref[...]) + row(2)
        n1, rs1 = normed(r)
        n1_ref[rows, :] = n1
        rs1_ref[rows, :] = rs1
        low_ref[rows, :] = (n1 * row(3) + row(4)).astype(bf16)
        sum_ref[rows, :] = jnp.zeros_like(n1)
        return t

    lax.fori_loop(0, steps, first, 0)

    def up(j, t):
        @pl.when(i == 0)
        def _():
            copy_in(j).wait()
            copy_back(j).wait()

        for c in range(width // sub):
            cols = slice(c * sub, (c + 1) * sub)
            z = dot(low_ref[...], win_ref[j, :, cols]) + b1_ref[j, :, cols]
            u, slope = gelu_both(z)
            slope_ref[j, :, cols] = slope.astype(bf16)
            sum_ref[...] += dot(u.astype(bf16), wback_ref[j, cols, :])
        return t

    lax.fori_loop(0, nchunk, up, 0)

    def middle(c, t):
        rows = pl.ds(pl.multiple_of(c * rchunk, rchunk), rchunk)
        h1 = n1_ref[rows, :] * row(3) + row(4)
        n2, rs2 = normed(h1 + (sum_ref[rows, :] + row(5)))
        act_ref[rows, :] = n2 * row(6) + row(7)
        dy = cot_ref[rows, :].astype(f32) * pad_ref[rows, :]
        add_stat(6, dy * n2)
        add_stat(7, dy)
        dr2 = norm_back(n2, rs2, dy * row(6))
        add_stat(5, dr2)
        sum_ref[rows, :] = dr2
        low_ref[rows, :] = dr2.astype(bf16)
        return t

    lax.fori_loop(0, steps, middle, 0)

    def down(j, t):
        for c in range(width // sub):
            cols = slice(c * sub, (c + 1) * sub)
            dz = dot(low_ref[...], wback_ref[j, cols, :], NT) * slope_ref[j, :, cols].astype(f32)
            db1_ref[j, :, cols] += jnp.sum(dz, axis=0, keepdims=True)
            sum_ref[...] += dot(dz.astype(bf16), win_ref[j, :, cols], NT)
        return t

    lax.fori_loop(0, nchunk, down, 0)

    def last(c, t):
        rows = pl.ds(pl.multiple_of(c * rchunk, rchunk), rchunk)
        n1 = n1_ref[rows, :]
        dh1 = sum_ref[rows, :]
        add_stat(3, dh1 * n1)
        add_stat(4, dh1)
        dr1 = norm_back(n1, rs1_ref[rows, :], dh1 * row(3))
        add_stat(2, dr1)
        dr1_ref[rows, :] = dr1
        da = dot(dr1.astype(bf16), wout_ref[...], NT).astype(bf16)
        da_ref[rows, :] = da
        add_stat(1, da.astype(f32))
        return t

    lax.fori_loop(0, steps, last, 0)


def mid(a, x, cot, padcol, wout, win_all, wback_all, b1, pm, block=512, rchunk=128, sub=512):
    rows, d = x.shape
    nchunk, _, width = win_all.shape
    block = min(block, rows)
    sub = min(sub, width)
    nb = rows // block
    r = lambda: pl.BlockSpec((block, d), lambda i: (i, 0))
    once = lambda s: pl.BlockSpec(s, lambda i: (0,) * len(s), pipeline_mode=pl.Buffered(1))
    flops = 2 * rows * d * (4 * nchunk * width + 2 * d)
    return pl.pallas_call(
        functools.partial(mid_kernel, rchunk, sub),
        out_shape=(jax.ShapeDtypeStruct((rows, d), f32), jax.ShapeDtypeStruct((rows, d), f32),
                   jax.ShapeDtypeStruct((rows, d), bf16), jax.ShapeDtypeStruct((8, d), f32),
                   jax.ShapeDtypeStruct((nchunk, 1, width), f32)),
        grid_spec=pltpu.PrefetchScalarGridSpec(
            num_scalar_prefetch=0, grid=(nb,),
            in_specs=[r(), r(), r(), pl.BlockSpec((block, 1), lambda i: (i, 0)), once((d, d)),
                      pl.BlockSpec(memory_space=pl.ANY), pl.BlockSpec(memory_space=pl.ANY),
                      once((nchunk, 1, width)), once((8, d))],
            out_specs=[r(), r(), r(), pl.BlockSpec((8, d), lambda i: (0, 0)),
                       pl.BlockSpec((nchunk, 1, width), lambda i: (0, 0, 0))],
            scratch_shapes=[pltpu.VMEM((nchunk, d, width), bf16), pltpu.VMEM((nchunk, width, d), bf16),
                            pltpu.SemaphoreType.DMA((2, nchunk)), pltpu.VMEM((nchunk, block, width), bf16),
                            pltpu.VMEM((block, d), f32), pltpu.VMEM((block, 1), f32),
                            pltpu.VMEM((block, d), bf16), pltpu.VMEM((block, d), f32)]),
        compiler_params=pltpu.CompilerParams(vmem_limit_bytes=60 << 20),
        cost_estimate=pl.CostEstimate(flops=flops, bytes_accessed=40 << 20, transcendentals=2 * rows * nchunk * width),
        name="feed",
    )(a, x, cot, padcol, wout, win_all, wback_all, b1, pm)


def adam_step(grad, first, second, param, average):
    first_new = 0.5 * first + 0.5 * grad
    second_new = 0.5 * second + 0.5 * grad * grad
    corr = 1.0 - 0.5**STEP
    param_new = param - 0.25 * (
        first_new / corr / (jnp.sqrt(second_new / corr) + 1e-08) + 0.01 * param
    )
    return (
        first_new,
        second_new,
        param_new,
        param_new.astype(jnp.bfloat16),
        0.8 * average + 0.2 * param_new,
    )


def on_device(
    tokens,
    segment_ids,
    pad_mask,
    cotangent,
    w_query,
    w_key,
    w_value,
    w_out,
    w_in,
    w_back,
    params_main,
    params_hidden,
    first_main,
    second_main,
    first_hidden,
    second_hidden,
    average_main,
    average_hidden,
):
    rows_all, d = tokens.shape
    width = params_hidden.shape[0]
    total_hidden = width * lax.axis_size("mp")
    seg, pad = segment_ids[0], pad_mask[0]
    in_all = lax.all_gather(w_in, "mp", axis=0, tiled=False)
    back_all = lax.all_gather(w_back, "mp", axis=0, tiled=False)
    bias_all = lax.all_gather(params_hidden, "mp", axis=0, tiled=False)[:, None, :]
    query = (dot(tokens, w_query) + params_main[0]).astype(bf16)
    keys = dot(tokens, w_key).astype(bf16)
    values = (dot(tokens, w_value) + params_main[1]).astype(bf16)
    mixed, lse = attn_fwd(query, keys, values, seg, pad, ALLOWED, 4)
    padcol = pad.astype(f32)[:, None]
    activations, dresid_one, dmixed, stats, hidden_grad = mid(
        mixed, tokens, cotangent, padcol, w_out, in_all, back_all, bias_all, params_main
    )
    dquery, dkeys, dvalues = attn_bwd(query, keys, values, dmixed, lse, seg, pad, ALLOWED, 4)
    input_grad = dresid_one + dot(dquery.astype(bf16), w_query, NT)
    input_grad = input_grad + dot(dkeys.astype(bf16), w_key, NT)
    input_grad = input_grad + dot(dvalues.astype(bf16), w_value, NT)
    local_main = stats.at[0].set(jnp.sum(dquery, axis=0))
    grad_main, hidden_total = lax.psum((local_main, hidden_grad.reshape(total_hidden)), ("dp", "mp"))
    grad_hid = lax.dynamic_slice_in_dim(hidden_total, lax.axis_index("mp") * width, width, 0)
    grad_norm = jnp.sqrt(jnp.sum(grad_main * grad_main) + jnp.sum(hidden_total * hidden_total))
    tokens_all = rows_all * lax.axis_size("dp") * lax.axis_size("mp")
    limit = 0.01 * math.sqrt(tokens_all * (8 * d + total_hidden))
    scale_factor = jnp.minimum(1.0, limit / (grad_norm + 1e-06))
    grad_main = grad_main * scale_factor
    grad_hid = grad_hid * scale_factor
    fm, sm, pm, cm, am = adam_step(grad_main, first_main, second_main, params_main, average_main)
    fh, sh, ph, ch, ah = adam_step(grad_hid, first_hidden, second_hidden, params_hidden, average_hidden)
    return (
        activations,
        input_grad,
        grad_norm,
        grad_main,
        grad_hid,
        fm,
        sm,
        fh,
        sh,
        pm,
        ph,
        cm,
        ch,
        am,
        ah,
    )


def solution(mesh):
    placed = (
        P(("dp", "mp"), None),
        P(("dp", "mp"), None),
        P(("dp", "mp"), None),
        P(("dp", "mp"), None),
        P(),
        P(),
        P(),
        P(),
        P(None, "mp"),
        P("mp", None),
        P(),
        P("mp"),
        P(),
        P(),
        P("mp"),
        P("mp"),
        P(),
        P("mp"),
    )
    return jax.shard_map(
        on_device,
        mesh=mesh,
        in_specs=placed,
        out_specs=(
            P(("dp", "mp"), None),
            P(("dp", "mp"), None),
            P(),
            P(),
            P("mp"),
            P(),
            P(),
            P("mp"),
            P("mp"),
            P(),
            P("mp"),
            P(),
            P("mp"),
            P(),
            P("mp"),
        ),
        check_vma=False,
    )
```

```python
import functools
import math

import jax
import jax.numpy as jnp
from jax import lax
from jax.experimental import pallas as pl
from jax.experimental.pallas import tpu as pltpu
from jax.sharding import PartitionSpec as P

STEP = 5
f32, bf16 = jnp.float32, jnp.bfloat16
NN = (((1,), (0,)), ((), ()))
NT = (((1,), (1,)), ((), ()))
DN_NT = NT
DN_TN = (((0,), (0,)), ((), ()))

BLK = 128
PAIR = 128
CH = 128
NEG = -1e9
ALLOWED = (2, 3, 4, 5, 6, 8)


def windows(seg_row, blk, allowed):
    length = seg_row.shape[0]
    nb = length // blk
    first = seg_row[::blk]
    last = seg_row[blk - 1 :: blk]
    lo = jnp.sum(seg_row[None, :] < first[:, None], axis=1)
    hi = jnp.sum(seg_row[None, :] <= last[:, None], axis=1)
    start = lo // blk
    count = (hi + blk - 1) // blk - start
    allowed_arr = jnp.array(allowed)
    variant = jnp.sum(allowed_arr[None, :] < count[:, None], axis=1)
    size = allowed_arr[variant]
    start = jnp.minimum(start, nb - size)
    return jnp.stack([start, variant]).astype(jnp.int32)


def halves(x):
    lane = lax.broadcasted_iota(jnp.int32, x.shape, 1)
    zero = jnp.zeros_like(x)
    return jnp.concatenate([jnp.where(lane < 64, x, zero), jnp.where(lane >= 64, x, zero)], axis=0)


def fill_bias(bias_ref, segcol_ref, segrow_ref, i, start, width):
    rows = pl.ds(start * BLK, width)
    kcode = segcol_ref[rows, :]
    qseg = segrow_ref[:, pl.ds(pl.multiple_of(i * BLK, BLK), BLK)]
    kpos = start * BLK + lax.broadcasted_iota(jnp.int32, (width, BLK), 0)
    qpos = i * BLK + lax.broadcasted_iota(jnp.int32, (width, BLK), 1)
    vis = (kcode == qseg) | (kpos == qpos)
    bias_ref[pl.ds(0, width), :] = jnp.where(vis, 0.0, NEG).astype(f32)


def fwd_kernel(allowed, npair, unroll, win_ref, q_ref, k_ref, v_ref, segcol_ref, segrow_ref, o_ref, lse_ref, bias_ref):
    i = pl.program_id(0)
    start = win_ref[0, i]
    variant = win_ref[1, i]
    for n, size in enumerate(allowed):
        width = size * BLK

        @pl.when(variant == n)
        def _(width=width):
            fill_bias(bias_ref, segcol_ref, segrow_ref, i, start, width)
            rows = pl.ds(pl.multiple_of(start * BLK, BLK), width)

            def pair(h):
                cols = pl.ds(pl.multiple_of(h * PAIR, PAIR), PAIR)
                qbd = halves(q_ref[:, cols])
                s = lax.dot_general(k_ref[rows, cols], qbd, DN_NT, preferred_element_type=f32)
                b = bias_ref[pl.ds(0, width), :]
                s = s + jnp.concatenate([b, b], axis=1)
                top = jnp.max(s, axis=0, keepdims=True)
                p = jnp.exp(s - top)
                tot = jnp.sum(p, axis=0, keepdims=True)
                o = lax.dot_general(p.astype(bf16), v_ref[rows, cols], DN_TN, preferred_element_type=f32)
                inv = jnp.broadcast_to(1.0 / tot, (8, 2 * BLK)).T[:, :1]
                o = o * inv
                lane = lax.broadcasted_iota(jnp.int32, (BLK, PAIR), 1)
                o_ref[:, cols] = jnp.where(lane < 64, o[:BLK], o[BLK:]).astype(bf16)
                lse_ref[0, pl.ds(h, 1), :] = top + jnp.log(tot)

            def body(t, c):
                for u in range(unroll):
                    pair(t * unroll + u)
                return c

            lax.fori_loop(0, npair // unroll, body, 0)


def attn_fwd(q, k, v, win, segcol, segrow, pairs, allowed=ALLOWED, unroll=8):
    length = q.shape[0]
    npair = pairs[1] - pairs[0]
    d, part = npair * PAIR, pairs[0] // npair
    nb = length // BLK
    unroll = min(unroll, npair)
    full = lambda: pl.BlockSpec((length, d), lambda i, w: (0, part))
    return pl.pallas_call(
        functools.partial(fwd_kernel, allowed, npair, unroll),
        out_shape=(jax.ShapeDtypeStruct((length, d), bf16), jax.ShapeDtypeStruct((nb, npair, 2 * BLK), f32)),
        grid_spec=pltpu.PrefetchScalarGridSpec(
            num_scalar_prefetch=1, grid=(nb,),
            in_specs=[pl.BlockSpec((BLK, d), lambda i, w: (i, part)), full(), full(),
                      pl.BlockSpec((length, 1), lambda i, w: (0, 0)), pl.BlockSpec((1, length), lambda i, w: (0, 0))],
            out_specs=[pl.BlockSpec((BLK, d), lambda i, w: (i, 0)), pl.BlockSpec((1, npair, 2 * BLK), lambda i, w: (i, 0, 0))],
            scratch_shapes=[pltpu.VMEM((length, BLK), f32)]),
        compiler_params=pltpu.CompilerParams(vmem_limit_bytes=48 << 20),
        cost_estimate=pl.CostEstimate(flops=length * d, bytes_accessed=8 * d, transcendentals=0),
        name="attend",
    )(win, q, k, v, segcol, segrow)


def bwd_kernel(allowed, npair, unroll, win_ref, q_ref, k_ref, v_ref, o_ref, do_ref, lse_ref, segcol_ref, segrow_ref,
               dr1_ref, wq_hbm, wk_hbm, wv_hbm, grad_ref, qsum_ref,
               bias_ref, p_ref, ds_ref, delta_ref, dq_ref, dk_ref, dv_ref, w_ref, sem):
    i = pl.program_id(0)
    nblock = k_ref.shape[0] // BLK
    loads = [pltpu.make_async_copy(w, w_ref.at[n], sem.at[n]) for n, w in enumerate((wq_hbm, wk_hbm, wv_hbm))]

    @pl.when(i == 0)
    def _():
        for load in loads:
            load.start()
        dk_ref[...] = jnp.zeros_like(dk_ref)
        dv_ref[...] = jnp.zeros_like(dv_ref)
        qsum_ref[...] = jnp.zeros_like(qsum_ref)

    @pl.when(i < nblock)
    def _():
        prod = do_ref[...].astype(f32) * o_ref[...].astype(f32)
        high = prod.astype(bf16)
        low = (prod - high.astype(f32)).astype(bf16)
        head = lax.broadcasted_iota(jnp.int32, (2 * npair, npair * PAIR), 0)
        lanes = lax.broadcasted_iota(jnp.int32, (2 * npair, npair * PAIR), 1)
        pick = jnp.where(lanes // 64 == head, 1.0, 0.0).astype(bf16)
        delta_ref[...] = lax.dot_general(pick, high, DN_NT, preferred_element_type=f32) + lax.dot_general(
            pick, low, DN_NT, preferred_element_type=f32
        )

    block = jnp.minimum(i, nblock - 1)
    start = win_ref[0, block]
    variant = jnp.where(i < nblock, win_ref[1, block], -1)
    for n, size in enumerate(allowed):
        width = size * BLK

        @pl.when(variant == n)
        def _(width=width):
            fill_bias(bias_ref, segcol_ref, segrow_ref, i, start, width)
            rows = pl.ds(pl.multiple_of(start * BLK, BLK), width)

            def pair(h, u):
                cols = pl.ds(pl.multiple_of(h * PAIR, PAIR), PAIR)
                qbd = halves(q_ref[:, cols])
                dobd = halves(do_ref[:, cols])
                lse = lse_ref[0, pl.ds(h, 1), :]
                delta = jnp.concatenate([delta_ref[pl.ds(2 * h, 1), :], delta_ref[pl.ds(2 * h + 1, 1), :]], axis=1)
                for c in range(width // CH):
                    crow = pl.ds(pl.multiple_of(start * BLK + c * CH, CH), CH)
                    span = slice(c * CH, (c + 1) * CH)
                    s = lax.dot_general(k_ref[crow, cols], qbd, DN_NT, preferred_element_type=f32)
                    dp = lax.dot_general(v_ref[crow, cols], dobd, DN_NT, preferred_element_type=f32)
                    b = bias_ref[span, :]
                    p = jnp.exp(s + jnp.concatenate([b, b], axis=1) - lse)
                    p_ref[u, span, :] = p.astype(bf16)
                    ds_ref[u, span, :] = (p * (dp - delta)).astype(bf16)
                nn = (((1,), (0,)), ((), ()))
                dv_ref[rows, cols] += lax.dot_general(p_ref[u, :width, :], dobd, nn, preferred_element_type=f32)
                dk_ref[rows, cols] += lax.dot_general(ds_ref[u, :width, :], qbd, nn, preferred_element_type=f32)
                dq = lax.dot_general(ds_ref[u, :width, :], k_ref[rows, cols], DN_TN, preferred_element_type=f32)
                lane = lax.broadcasted_iota(jnp.int32, (BLK, PAIR), 1)
                dq = 0.125 * jnp.where(lane < 64, dq[:BLK], dq[BLK:])
                dq_ref[pl.ds(pl.multiple_of(i * BLK, BLK), BLK), cols] = dq.astype(bf16)
                qsum_ref[:, cols] += jnp.sum(dq.reshape(BLK // 8, 8, PAIR), axis=0)

            def body(t, c):
                for u in range(unroll):
                    pair(t * unroll + u, u)
                return c

            lax.fori_loop(0, npair // unroll, body, 0)

    @pl.when(i == nblock)
    def _():
        for load in loads:
            load.wait()

    @pl.when(i >= nblock)
    def _():
        span = grad_ref.shape[0]
        rows = pl.ds(pl.multiple_of((i - nblock) * span, span), span)
        total = lax.dot_general(dq_ref[rows, :], w_ref[0], DN_NT, preferred_element_type=f32)
        total += lax.dot_general(dk_ref[rows, :].astype(bf16), w_ref[1], DN_NT, preferred_element_type=f32)
        total += lax.dot_general(dv_ref[rows, :].astype(bf16), w_ref[2], DN_NT, preferred_element_type=f32)
        grad_ref[...] = dr1_ref[...] + total


def attn_bwd(q, k, v, o, do, lse, win, segcol, segrow, dr1, wq, wk, wv, allowed=ALLOWED, unroll=8, span=512):
    length, d = q.shape
    nb, npair = length // BLK, d // PAIR
    one = pl.Buffered(1)
    full = lambda: pl.BlockSpec((length, d), lambda i, w: (0, 0), pipeline_mode=one)
    row = lambda: pl.BlockSpec((BLK, d), lambda i, w: (jnp.minimum(i, nb - 1), 0))
    wide = lambda: pl.BlockSpec((span, d), lambda i, w: (jnp.maximum(i - nb, 0), 0))
    hbm = lambda: pl.BlockSpec(memory_space=pl.ANY)
    return pl.pallas_call(
        functools.partial(bwd_kernel, allowed, npair, unroll),
        out_shape=(jax.ShapeDtypeStruct((length, d), f32), jax.ShapeDtypeStruct((8, d), f32)),
        grid_spec=pltpu.PrefetchScalarGridSpec(
            num_scalar_prefetch=1, grid=(nb + length // span,),
            in_specs=[row(), full(), full(), row(), row(),
                      pl.BlockSpec((1, npair, 2 * BLK), lambda i, w: (jnp.minimum(i, nb - 1), 0, 0)),
                      pl.BlockSpec((length, 1), lambda i, w: (0, 0)), pl.BlockSpec((1, length), lambda i, w: (0, 0)),
                      wide(), hbm(), hbm(), hbm()],
            out_specs=[wide(), pl.BlockSpec((8, d), lambda i, w: (0, 0))],
            scratch_shapes=[pltpu.VMEM((length, BLK), f32), pltpu.VMEM((unroll, length, 2 * BLK), bf16),
                            pltpu.VMEM((unroll, length, 2 * BLK), bf16), pltpu.VMEM((2 * npair, BLK), f32),
                            pltpu.VMEM((length, d), bf16), pltpu.VMEM((length, d), f32), pltpu.VMEM((length, d), f32),
                            pltpu.VMEM((3, d, d), bf16), pltpu.SemaphoreType.DMA((3,))]),
        compiler_params=pltpu.CompilerParams(vmem_limit_bytes=58 << 20),
        cost_estimate=pl.CostEstimate(flops=5 * length * length * d, bytes_accessed=14 * length * d, transcendentals=length * length * npair),
        name="attend_back",
    )(win, q, k, v, o, do, lse, segcol, segrow, dr1, wq, wk, wv)


def dot(a, b, dims=NN):
    return lax.dot_general(a, b, dims, preferred_element_type=f32)


def gelu_both(z):
    x = jnp.abs(z) * 0.7071067811865476
    e = jnp.exp(-0.5 * z * z)
    t = 1.0 / (1.0 + 0.3275911 * x)
    poly = t * (0.254829592 + t * (-0.284496736 + t * (1.421413741 + t * (-1.453152027 + t * 1.061405429))))
    tail = 0.5 * poly * e
    phi = jnp.where(z >= 0, 1.0 - tail, tail)
    return z * phi, phi + z * (0.3989422804014327 * e)


def normed(r):
    center = r - jnp.mean(r, axis=-1, keepdims=True)
    factor = lax.rsqrt(jnp.mean(center * center, axis=-1, keepdims=True) + 1e-05)
    return center * factor, factor


def norm_back(normal, factor, dn):
    return factor * (
        dn - jnp.mean(dn, axis=-1, keepdims=True) - normal * jnp.mean(dn * normal, axis=-1, keepdims=True)
    )


def mid_kernel(plan, rchunk, sub, nsrc, *refs):
    a_ref, x_ref, cot_ref, pad_ref, wout_ref, pm_ref = refs[:6]
    src = refs[6 : 6 + nsrc]
    (act_ref, dr1_ref, da_ref, stat_ref, db1_ref,
     win_ref, wback_ref, sem, slope_ref, n1_ref, rs1_ref, low_ref, sum_ref) = refs[6 + nsrc :]
    i = pl.program_id(0)
    nchunk, _, width = win_ref.shape
    rows_all = x_ref.shape[0]
    steps = rows_all // rchunk

    def copies(j):
        (a_in, i_in), (a_back, i_back) = plan[j]
        return (
            pltpu.make_async_copy(src[a_in].at[i_in], win_ref.at[j], sem.at[0, j]),
            pltpu.make_async_copy(src[a_back].at[i_back], wback_ref.at[j], sem.at[1, j]),
        )

    @pl.when(i == 0)
    def _():
        for j in range(nchunk):
            for copy in copies(j):
                copy.start()
        stat_ref[...] = jnp.zeros_like(stat_ref)
        db1_ref[...] = jnp.zeros_like(db1_ref)

    row = lambda n: pm_ref[n : n + 1, :]

    def add_stat(n, v):
        stat_ref[n : n + 1, :] += jnp.sum(v, axis=0, keepdims=True)

    def first(c, t):
        rows = pl.ds(pl.multiple_of(c * rchunk, rchunk), rchunk)
        r = x_ref[rows, :].astype(f32) + sum_ref[rows, :] + row(2)
        n1, rs1 = normed(r)
        n1_ref[rows, :] = n1
        rs1_ref[rows, :] = rs1
        low_ref[rows, :] = (n1 * row(3) + row(4)).astype(bf16)
        sum_ref[rows, :] = jnp.zeros_like(n1)
        return t

    sum_ref[...] = dot(a_ref[...], wout_ref[...])
    lax.fori_loop(0, steps, first, 0)

    def up(j, t):
        @pl.when(i == 0)
        def _():
            pltpu.make_async_copy(src[plan[0][0][0]].at[0], win_ref.at[j], sem.at[0, j]).wait()
            pltpu.make_async_copy(src[plan[0][1][0]].at[0], wback_ref.at[j], sem.at[1, j]).wait()

        parts = wback_ref[j, width : width + 16, :width].astype(f32)
        bias = parts[0:1] + parts[1:2] + parts[2:3]

        for c in range(width // sub):
            cols = slice(c * sub, (c + 1) * sub)
            z = dot(low_ref[...], win_ref[j, :, cols]) + bias[:, cols]
            u, slope = gelu_both(z)
            slope_ref[j, :, cols] = slope.astype(bf16)
            sum_ref[...] += dot(u.astype(bf16), wback_ref[j, cols, :])
        return t

    lax.fori_loop(0, nchunk, up, 0)

    def middle(c, t):
        rows = pl.ds(pl.multiple_of(c * rchunk, rchunk), rchunk)
        h1 = n1_ref[rows, :] * row(3) + row(4)
        n2, rs2 = normed(h1 + (sum_ref[rows, :] + row(5)))
        act_ref[rows, :] = n2 * row(6) + row(7)
        dy = cot_ref[rows, :].astype(f32) * pad_ref[rows, :]
        add_stat(6, dy * n2)
        add_stat(7, dy)
        dr2 = norm_back(n2, rs2, dy * row(6))
        add_stat(5, dr2)
        sum_ref[rows, :] = dr2
        low_ref[rows, :] = dr2.astype(bf16)
        return t

    lax.fori_loop(0, steps, middle, 0)

    def down(j, t):
        for c in range(width // sub):
            cols = slice(c * sub, (c + 1) * sub)
            dz = dot(low_ref[...], wback_ref[j, cols, :], NT) * slope_ref[j, :, cols].astype(f32)
            db1_ref[j, :, cols] += jnp.sum(dz, axis=0, keepdims=True)
            sum_ref[...] += dot(dz.astype(bf16), win_ref[j, :, cols], NT)
        return t

    lax.fori_loop(0, nchunk, down, 0)

    def last(c, t):
        rows = pl.ds(pl.multiple_of(c * rchunk, rchunk), rchunk)
        n1 = n1_ref[rows, :]
        dh1 = sum_ref[rows, :]
        add_stat(3, dh1 * n1)
        add_stat(4, dh1)
        dr1 = norm_back(n1, rs1_ref[rows, :], dh1 * row(3))
        add_stat(2, dr1)
        dr1_ref[rows, :] = dr1
        low_ref[rows, :] = dr1.astype(bf16)
        return t

    lax.fori_loop(0, steps, last, 0)
    da = dot(low_ref[...], wout_ref[...], NT).astype(bf16)
    da_ref[...] = da
    add_stat(1, da.astype(f32))


def mid(a, x, cot, padcol, wout, pm, src, plan, width, block=512, rchunk=128, sub=512):
    rows, d = x.shape
    nchunk = len(plan)
    block = min(block, rows)
    sub = min(sub, width)
    nb = rows // block
    r = lambda: pl.BlockSpec((block, d), lambda i: (i, 0))
    once = lambda s: pl.BlockSpec(s, lambda i: (0,) * len(s), pipeline_mode=pl.Buffered(1))
    flops = 2 * rows * d * (4 * nchunk * width + 2 * d)
    return pl.pallas_call(
        functools.partial(mid_kernel, plan, rchunk, sub, len(src)),
        out_shape=(jax.ShapeDtypeStruct((rows, d), f32), jax.ShapeDtypeStruct((rows, d), f32),
                   jax.ShapeDtypeStruct((rows, d), bf16), jax.ShapeDtypeStruct((8, d), f32),
                   jax.ShapeDtypeStruct((nchunk, 1, width), f32)),
        grid_spec=pltpu.PrefetchScalarGridSpec(
            num_scalar_prefetch=0, grid=(nb,),
            in_specs=[r(), r(), r(), pl.BlockSpec((block, 1), lambda i: (i, 0)), once((d, d)), once((8, d))]
            + [pl.BlockSpec(memory_space=pl.ANY) for _ in src],
            out_specs=[r(), r(), r(), pl.BlockSpec((8, d), lambda i: (0, 0)),
                       pl.BlockSpec((nchunk, 1, width), lambda i: (0, 0, 0))],
            scratch_shapes=[pltpu.VMEM((nchunk, d, width), bf16), pltpu.VMEM((nchunk, width + 16, d), bf16),
                            pltpu.SemaphoreType.DMA((2, nchunk)), pltpu.VMEM((nchunk, block, width), bf16),
                            pltpu.VMEM((block, d), f32), pltpu.VMEM((block, 1), f32),
                            pltpu.VMEM((block, d), bf16), pltpu.VMEM((block, d), f32)]),
        compiler_params=pltpu.CompilerParams(vmem_limit_bytes=60 << 20),
        cost_estimate=pl.CostEstimate(flops=flops, bytes_accessed=40 << 20, transcendentals=2 * rows * nchunk * width),
        name="feed",
    )(a, x, cot, padcol, wout, pm, *src)


def adam_step(grad, first, second, param, average):
    first_new = 0.5 * first + 0.5 * grad
    second_new = 0.5 * second + 0.5 * grad * grad
    corr = 1.0 - 0.5**STEP
    param_new = param - 0.25 * (
        first_new / corr / (jnp.sqrt(second_new / corr) + 1e-08) + 0.01 * param
    )
    return (
        first_new,
        second_new,
        param_new,
        param_new.astype(jnp.bfloat16),
        0.8 * average + 0.2 * param_new,
    )


def exchange(v, axis, bit):
    size = lax.axis_size(axis)
    return lax.ppermute(v, axis, [(i, i ^ bit) for i in range(size)])


def bits(size):
    return [1 << b for b in range(size.bit_length() - 1)]


def gather_cube(part_in, part_back, early, late):
    core, along_x, along_y = 1, 2, 4
    xb = exchange(part_back, "mp", along_x)
    ya = exchange(part_in, "mp", along_y)
    core_in, core_back = exchange(part_in, "mp", core), exchange(part_back, "mp", core)
    xb, ya, core_in, core_back, own_in, own_back, early = lax.optimization_barrier(
        (xb, ya, core_in, core_back, part_in, part_back, early)
    )
    far_in = exchange(ya, "mp", along_x)
    far_back = exchange(xb, "mp", along_y)
    xa = exchange(own_in, "mp", along_x)
    yb = exchange(own_back, "mp", along_y)
    core_ya = exchange(ya, "mp", core)
    xa, yb, far_in, far_back, core_ya, xb, late = lax.optimization_barrier(
        (xa, yb, far_in, far_back, core_ya, xb, late(early))
    )
    pieces = [own_in, own_back, xa, xb, ya, yb, far_in, far_back, core_in, core_back]
    pieces += [exchange(xa, "mp", core), exchange(xb, "mp", core), core_ya]
    pieces += [exchange(p, "mp", core) for p in (yb, far_in, far_back)]
    order = (0, 8, 2, 10, 4, 12, 6, 14)
    return [p[None] for p in pieces], tuple(((j, 0), (j + 1, 0)) for j in order), early, late


def total_sum(v):
    if lax.axis_size("mp") == 8 and lax.axis_size("dp") == 4:
        v = v + exchange(v, "mp", 1)
        v = (v + exchange(v, "mp", 2)) + (exchange(v, "mp", 4) + exchange(v, "mp", 6))
        return (v + exchange(v, "dp", 1)) + (exchange(v, "dp", 2) + exchange(v, "dp", 3))
    for axis in ("mp", "dp"):
        for bit in bits(lax.axis_size(axis)):
            v = v + exchange(v, axis, bit)
    return v


def on_device(
    tokens,
    segment_ids,
    pad_mask,
    cotangent,
    w_query,
    w_key,
    w_value,
    w_out,
    w_in,
    w_back,
    params_main,
    params_hidden,
    first_main,
    second_main,
    first_hidden,
    second_hidden,
    average_main,
    average_hidden,
):
    rows_all, d = tokens.shape
    width = params_hidden.shape[0]
    devices = lax.axis_size("mp")
    me = lax.axis_index("mp")
    total_hidden = width * devices
    seg, pad = segment_ids[0], pad_mask[0]

    rounded = lambda v: lax.reduce_precision(v, 8, 7)
    high = rounded(params_hidden)
    middle = rounded(params_hidden - high)
    rows = jnp.stack([high, middle, rounded(params_hidden - high - middle)]).astype(bf16)
    part_back = jnp.concatenate([w_back, jnp.pad(rows, ((0, 13), (0, d - width)))], axis=0)
    win = windows(seg, BLK, ALLOWED)
    segcol = jnp.where(pad == 1, seg, -1)[:, None]
    segrow = seg[None, :]
    query = (0.125 * (dot(tokens, w_query) + params_main[0])).astype(bf16)
    keys = dot(tokens, w_key).astype(bf16)
    values = (dot(tokens, w_value) + params_main[1]).astype(bf16)
    cube = devices == 8
    attend = lambda qkv: attn_fwd(*qkv, win, segcol, segrow, (0, d // PAIR))
    if cube:
        sources, plan, (query, keys, values), (mixed, lse) = gather_cube(
            w_in, part_back, (query, keys, values), attend
        )
    else:
        sources = [lax.all_gather(w_in, "mp", axis=0), lax.all_gather(part_back, "mp", axis=0)]
        plan = tuple(((0, j), (1, j)) for j in range(devices))
        mixed, lse = attend((query, keys, values))
    padcol = pad.astype(f32)[:, None]
    activations, dresid_one, dmixed, stats, hidden_grad = mid(
        mixed, tokens, cotangent, padcol, w_out, params_main, sources, plan, width
    )
    input_grad, query_sum = attn_bwd(
        query, keys, values, mixed, dmixed, lse, win, segcol, segrow, dresid_one, w_query, w_key, w_value
    )
    if cube:
        hidden_grad = hidden_grad.reshape(2, 2, 2, width)
        for n in range(3):
            hidden_grad = jnp.where((me & (4 >> n)) > 0, jnp.flip(hidden_grad, n), hidden_grad)
    local = jnp.concatenate(
        [jnp.sum(query_sum, axis=0)[None], stats[1:], hidden_grad.reshape(total_hidden // d, d)], axis=0
    )
    total = total_sum(local)
    grad_norm = jnp.sqrt(jnp.sum(total * total))
    grad_main = total[:8]
    grad_hid = lax.dynamic_slice_in_dim(total[8:].reshape(total_hidden), me * width, width, 0)
    tokens_all = rows_all * lax.axis_size("dp") * devices
    limit = 0.01 * math.sqrt(tokens_all * (8 * d + total_hidden))
    scale_factor = jnp.minimum(1.0, limit / (grad_norm + 1e-06))
    grad_main = grad_main * scale_factor
    grad_hid = grad_hid * scale_factor
    fm, sm, pm, cm, am = adam_step(grad_main, first_main, second_main, params_main, average_main)
    fh, sh, ph, ch, ah = adam_step(grad_hid, first_hidden, second_hidden, params_hidden, average_hidden)
    return (
        activations,
        input_grad,
        grad_norm,
        grad_main,
        grad_hid,
        fm,
        sm,
        fh,
        sh,
        pm,
        ph,
        cm,
        ch,
        am,
        ah,
    )


def solution(mesh):
    placed = (
        P(("dp", "mp"), None),
        P(("dp", "mp"), None),
        P(("dp", "mp"), None),
        P(("dp", "mp"), None),
        P(),
        P(),
        P(),
        P(),
        P(None, "mp"),
        P("mp", None),
        P(),
        P("mp"),
        P(),
        P(),
        P("mp"),
        P("mp"),
        P(),
        P("mp"),
    )
    return jax.shard_map(
        on_device,
        mesh=mesh,
        in_specs=placed,
        out_specs=(
            P(("dp", "mp"), None),
            P(("dp", "mp"), None),
            P(),
            P(),
            P("mp"),
            P(),
            P(),
            P("mp"),
            P("mp"),
            P(),
            P("mp"),
            P(),
            P("mp"),
            P(),
            P("mp"),
        ),
        check_vma=False,
    )
```

```python
import functools
import math

import jax
import jax.numpy as jnp
from jax import lax
from jax.experimental import pallas as pl
from jax.experimental.pallas import tpu as pltpu
from jax.sharding import PartitionSpec as P

STEP = 5
f32, bf16 = jnp.float32, jnp.bfloat16
NN = (((1,), (0,)), ((), ()))
NT = (((1,), (1,)), ((), ()))
DN_NT = NT
DN_TN = (((0,), (0,)), ((), ()))

BLK = 128
PAIR = 128
CH = 128
NEG = -1e9
ALLOWED = (2, 3, 4, 5, 6, 8)


def windows(seg_row, blk, allowed):
    length = seg_row.shape[0]
    nb = length // blk
    first = seg_row[::blk]
    last = seg_row[blk - 1 :: blk]
    lo = jnp.sum(seg_row[None, :] < first[:, None], axis=1)
    hi = jnp.sum(seg_row[None, :] <= last[:, None], axis=1)
    start = lo // blk
    count = (hi + blk - 1) // blk - start
    allowed_arr = jnp.array(allowed)
    variant = jnp.sum(allowed_arr[None, :] < count[:, None], axis=1)
    size = allowed_arr[variant]
    start = jnp.minimum(start, nb - size)
    return jnp.stack([start, variant]).astype(jnp.int32)


def halves(x):
    lane = lax.broadcasted_iota(jnp.int32, x.shape, 1)
    zero = jnp.zeros_like(x)
    return jnp.concatenate([jnp.where(lane < 64, x, zero), jnp.where(lane >= 64, x, zero)], axis=0)


def fill_bias(bias_ref, segcol_ref, segrow_ref, i, start, width):
    rows = pl.ds(start * BLK, width)
    kcode = segcol_ref[rows, :]
    qseg = segrow_ref[:, pl.ds(pl.multiple_of(i * BLK, BLK), BLK)]
    kpos = start * BLK + lax.broadcasted_iota(jnp.int32, (width, BLK), 0)
    qpos = i * BLK + lax.broadcasted_iota(jnp.int32, (width, BLK), 1)
    vis = (kcode == qseg) | (kpos == qpos)
    bias_ref[pl.ds(0, width), :] = jnp.where(vis, 0.0, NEG).astype(f32)


def fwd_kernel(allowed, npair, unroll, win_ref, q_ref, k_ref, v_ref, segcol_ref, segrow_ref, o_ref, lse_ref, bias_ref):
    i = pl.program_id(0)
    start = win_ref[0, i]
    variant = win_ref[1, i]
    for n, size in enumerate(allowed):
        width = size * BLK

        @pl.when(variant == n)
        def _(width=width):
            fill_bias(bias_ref, segcol_ref, segrow_ref, i, start, width)
            rows = pl.ds(pl.multiple_of(start * BLK, BLK), width)

            def pair(h):
                cols = pl.ds(pl.multiple_of(h * PAIR, PAIR), PAIR)
                qbd = halves(q_ref[:, cols])
                s = lax.dot_general(k_ref[rows, cols], qbd, DN_NT, preferred_element_type=f32)
                b = bias_ref[pl.ds(0, width), :]
                s = s + jnp.concatenate([b, b], axis=1)
                top = jnp.max(s, axis=0, keepdims=True)
                p = jnp.exp(s - top)
                tot = jnp.sum(p, axis=0, keepdims=True)
                o = lax.dot_general(p.astype(bf16), v_ref[rows, cols], DN_TN, preferred_element_type=f32)
                inv = jnp.broadcast_to(1.0 / tot, (8, 2 * BLK)).T[:, :1]
                o = o * inv
                lane = lax.broadcasted_iota(jnp.int32, (BLK, PAIR), 1)
                o_ref[:, cols] = jnp.where(lane < 64, o[:BLK], o[BLK:]).astype(bf16)
                lse_ref[0, pl.ds(h, 1), :] = top + jnp.log(tot)

            def body(t, c):
                for u in range(unroll):
                    pair(t * unroll + u)
                return c

            lax.fori_loop(0, npair // unroll, body, 0)


def attn_fwd(q, k, v, win, segcol, segrow, pairs, allowed=ALLOWED, unroll=8):
    length = q.shape[0]
    npair = pairs[1] - pairs[0]
    d, part = npair * PAIR, pairs[0] // npair
    nb = length // BLK
    unroll = min(unroll, npair)
    full = lambda: pl.BlockSpec((length, d), lambda i, w: (0, part))
    return pl.pallas_call(
        functools.partial(fwd_kernel, allowed, npair, unroll),
        out_shape=(jax.ShapeDtypeStruct((length, d), bf16), jax.ShapeDtypeStruct((nb, npair, 2 * BLK), f32)),
        grid_spec=pltpu.PrefetchScalarGridSpec(
            num_scalar_prefetch=1, grid=(nb,),
            in_specs=[pl.BlockSpec((BLK, d), lambda i, w: (i, part)), full(), full(),
                      pl.BlockSpec((length, 1), lambda i, w: (0, 0)), pl.BlockSpec((1, length), lambda i, w: (0, 0))],
            out_specs=[pl.BlockSpec((BLK, d), lambda i, w: (i, 0)), pl.BlockSpec((1, npair, 2 * BLK), lambda i, w: (i, 0, 0))],
            scratch_shapes=[pltpu.VMEM((length, BLK), f32)]),
        compiler_params=pltpu.CompilerParams(vmem_limit_bytes=60 << 20),
        cost_estimate=pl.CostEstimate(flops=length * d, bytes_accessed=8 * d, transcendentals=0),
        name="attend",
    )(win, q, k, v, segcol, segrow)


def bwd_kernel(allowed, npair, unroll, win_ref, q_ref, k_ref, v_ref, o_ref, do_ref, lse_ref, segcol_ref, segrow_ref,
               dr1_ref, wq_hbm, wk_hbm, wv_hbm, grad_ref, qsum_ref,
               bias_ref, p_ref, ds_ref, delta_ref, dq_ref, dk_ref, dv_ref, w_ref, sem):
    i = pl.program_id(0)
    nblock = k_ref.shape[0] // BLK
    loads = [pltpu.make_async_copy(w, w_ref.at[n], sem.at[n]) for n, w in enumerate((wq_hbm, wk_hbm, wv_hbm))]

    @pl.when(i == 0)
    def _():
        for load in loads:
            load.start()
        dk_ref[...] = jnp.zeros_like(dk_ref)
        dv_ref[...] = jnp.zeros_like(dv_ref)
        qsum_ref[...] = jnp.zeros_like(qsum_ref)

    @pl.when(i < nblock)
    def _():
        prod = do_ref[...].astype(f32) * o_ref[...].astype(f32)
        high = prod.astype(bf16)
        low = (prod - high.astype(f32)).astype(bf16)
        head = lax.broadcasted_iota(jnp.int32, (2 * npair, npair * PAIR), 0)
        lanes = lax.broadcasted_iota(jnp.int32, (2 * npair, npair * PAIR), 1)
        pick = jnp.where(lanes // 64 == head, 1.0, 0.0).astype(bf16)
        delta_ref[...] = lax.dot_general(pick, high, DN_NT, preferred_element_type=f32) + lax.dot_general(
            pick, low, DN_NT, preferred_element_type=f32
        )

    block = jnp.minimum(i, nblock - 1)
    start = win_ref[0, block]
    variant = jnp.where(i < nblock, win_ref[1, block], -1)
    for n, size in enumerate(allowed):
        width = size * BLK

        @pl.when(variant == n)
        def _(width=width):
            fill_bias(bias_ref, segcol_ref, segrow_ref, i, start, width)
            rows = pl.ds(pl.multiple_of(start * BLK, BLK), width)

            def pair(h, u):
                cols = pl.ds(pl.multiple_of(h * PAIR, PAIR), PAIR)
                qbd = halves(q_ref[:, cols])
                dobd = halves(do_ref[:, cols])
                lse = lse_ref[0, pl.ds(h, 1), :]
                delta = jnp.concatenate([delta_ref[pl.ds(2 * h, 1), :], delta_ref[pl.ds(2 * h + 1, 1), :]], axis=1)
                for c in range(width // CH):
                    crow = pl.ds(pl.multiple_of(start * BLK + c * CH, CH), CH)
                    span = slice(c * CH, (c + 1) * CH)
                    s = lax.dot_general(k_ref[crow, cols], qbd, DN_NT, preferred_element_type=f32)
                    dp = lax.dot_general(v_ref[crow, cols], dobd, DN_NT, preferred_element_type=f32)
                    b = bias_ref[span, :]
                    p = jnp.exp(s + jnp.concatenate([b, b], axis=1) - lse)
                    p_ref[u, span, :] = p.astype(bf16)
                    ds_ref[u, span, :] = (p * (dp - delta)).astype(bf16)
                nn = (((1,), (0,)), ((), ()))
                dv_ref[rows, cols] += lax.dot_general(p_ref[u, :width, :], dobd, nn, preferred_element_type=f32)
                dk_ref[rows, cols] += lax.dot_general(ds_ref[u, :width, :], qbd, nn, preferred_element_type=f32)
                dq = lax.dot_general(ds_ref[u, :width, :], k_ref[rows, cols], DN_TN, preferred_element_type=f32)
                lane = lax.broadcasted_iota(jnp.int32, (BLK, PAIR), 1)
                dq = 0.125 * jnp.where(lane < 64, dq[:BLK], dq[BLK:])
                dq_ref[pl.ds(pl.multiple_of(i * BLK, BLK), BLK), cols] = dq.astype(bf16)
                qsum_ref[:, cols] += jnp.sum(dq.reshape(BLK // 8, 8, PAIR), axis=0)

            def body(t, c):
                for u in range(unroll):
                    pair(t * unroll + u, u)
                return c

            lax.fori_loop(0, npair // unroll, body, 0)

    @pl.when(i == nblock)
    def _():
        for load in loads:
            load.wait()

    @pl.when(i >= nblock)
    def _():
        span = grad_ref.shape[0]
        rows = pl.ds(pl.multiple_of((i - nblock) * span, span), span)
        total = lax.dot_general(dq_ref[rows, :], w_ref[0], DN_NT, preferred_element_type=f32)
        total += lax.dot_general(dk_ref[rows, :].astype(bf16), w_ref[1], DN_NT, preferred_element_type=f32)
        total += lax.dot_general(dv_ref[rows, :].astype(bf16), w_ref[2], DN_NT, preferred_element_type=f32)
        grad_ref[...] = dr1_ref[...] + total


def attn_bwd(q, k, v, o, do, lse, win, segcol, segrow, dr1, wq, wk, wv, allowed=ALLOWED, unroll=8, span=512):
    length, d = q.shape
    nb, npair = length // BLK, d // PAIR
    one = pl.Buffered(1)
    full = lambda: pl.BlockSpec((length, d), lambda i, w: (0, 0), pipeline_mode=one)
    row = lambda: pl.BlockSpec((BLK, d), lambda i, w: (jnp.minimum(i, nb - 1), 0))
    wide = lambda: pl.BlockSpec((span, d), lambda i, w: (jnp.maximum(i - nb, 0), 0))
    hbm = lambda: pl.BlockSpec(memory_space=pl.ANY)
    return pl.pallas_call(
        functools.partial(bwd_kernel, allowed, npair, unroll),
        out_shape=(jax.ShapeDtypeStruct((length, d), f32), jax.ShapeDtypeStruct((8, d), f32)),
        grid_spec=pltpu.PrefetchScalarGridSpec(
            num_scalar_prefetch=1, grid=(nb + length // span,),
            in_specs=[row(), full(), full(), row(), row(),
                      pl.BlockSpec((1, npair, 2 * BLK), lambda i, w: (jnp.minimum(i, nb - 1), 0, 0)),
                      pl.BlockSpec((length, 1), lambda i, w: (0, 0)), pl.BlockSpec((1, length), lambda i, w: (0, 0)),
                      wide(), hbm(), hbm(), hbm()],
            out_specs=[wide(), pl.BlockSpec((8, d), lambda i, w: (0, 0))],
            scratch_shapes=[pltpu.VMEM((length, BLK), f32), pltpu.VMEM((unroll, length, 2 * BLK), bf16),
                            pltpu.VMEM((unroll, length, 2 * BLK), bf16), pltpu.VMEM((2 * npair, BLK), f32),
                            pltpu.VMEM((length, d), bf16), pltpu.VMEM((length, d), f32), pltpu.VMEM((length, d), f32),
                            pltpu.VMEM((3, d, d), bf16), pltpu.SemaphoreType.DMA((3,))]),
        compiler_params=pltpu.CompilerParams(vmem_limit_bytes=60 << 20),
        cost_estimate=pl.CostEstimate(flops=5 * length * length * d, bytes_accessed=14 * length * d, transcendentals=length * length * npair),
        name="attend_back",
    )(win, q, k, v, o, do, lse, segcol, segrow, dr1, wq, wk, wv)
def dot(a, b, dims=NN):
    return lax.dot_general(a, b, dims, preferred_element_type=f32)


def gelu_both(z):
    x = jnp.abs(z) * 0.7071067811865476
    e = jnp.exp(-0.5 * z * z)
    t = 1.0 / (1.0 + 0.3275911 * x)
    poly = t * (0.254829592 + t * (-0.284496736 + t * (1.421413741 + t * (-1.453152027 + t * 1.061405429))))
    tail = 0.5 * poly * e
    phi = jnp.where(z >= 0, 1.0 - tail, tail)
    return z * phi, phi + z * (0.3989422804014327 * e)


def normed(r):
    center = r - jnp.mean(r, axis=-1, keepdims=True)
    factor = lax.rsqrt(jnp.mean(center * center, axis=-1, keepdims=True) + 1e-05)
    return center * factor, factor


def norm_back(normal, factor, dn):
    return factor * (
        dn - jnp.mean(dn, axis=-1, keepdims=True) - normal * jnp.mean(dn * normal, axis=-1, keepdims=True)
    )


def out_kernel(a_ref, x_ref, wout_ref, pm_ref, n1_ref, rs1_ref, low_ref):
    r = x_ref[...].astype(f32) + dot(a_ref[...], wout_ref[...]) + pm_ref[2:3, :]
    n1, rs1 = normed(r)
    n1_ref[...] = n1
    rs1_ref[...] = rs1
    low_ref[...] = (n1 * pm_ref[3:4, :] + pm_ref[4:5, :]).astype(bf16)


def out_norm(a, x, wout, pm, block=512):
    rows, d = x.shape
    r = lambda: pl.BlockSpec((block, d), lambda i: (i, 0))
    once = lambda s: pl.BlockSpec(s, lambda i: (0,) * len(s), pipeline_mode=pl.Buffered(1))
    return pl.pallas_call(
        out_kernel,
        out_shape=(jax.ShapeDtypeStruct((rows, d), f32), jax.ShapeDtypeStruct((rows, 1), f32),
                   jax.ShapeDtypeStruct((rows, d), bf16)),
        grid=(rows // block,),
        in_specs=[r(), r(), once((d, d)), once((8, d))],
        out_specs=[r(), pl.BlockSpec((block, 1), lambda i: (i, 0)), r()],
        compiler_params=pltpu.CompilerParams(vmem_limit_bytes=60 << 20),
        cost_estimate=pl.CostEstimate(flops=rows * d, bytes_accessed=8 * d, transcendentals=0),
        name="join",
    )(a, x, wout, pm)


def chunk_copies(plan, src, j, win_ref, wback_ref, sem):
    d, width = win_ref.shape[1:]
    piece, at, row = plan[j][0]
    moves = [
        (src[piece].at[at, pl.ds(row, width), pl.ds(g * width, width)], win_ref.at[j, pl.ds(g * width, width)])
        for g in range(d // width)
    ]
    piece, at, row = plan[j][1]
    moves.append((src[piece].at[at, pl.ds(row, width + 16)], wback_ref.at[j]))
    return [pltpu.make_async_copy(s, t, sem.at[n, j]) for n, (s, t) in enumerate(moves)]


def wait_chunk(plan, src, j, win_ref, wback_ref, sem):
    for n in range(len(plan)):

        @pl.when(j == n)
        def _(n=n):
            for copy in chunk_copies(plan, src, n, win_ref, wback_ref, sem):
                copy.wait()


def up_kernel(plan, nsrc, carry, span, *refs):
    low_ref, refs = refs[0], refs[1:]
    if carry:
        start_ref, refs = refs[0], refs[1:]
    src = refs[:nsrc]
    sum_ref, slope_ref, win_ref, wback_ref, sem = refs[nsrc:]
    j = pl.program_id(0)
    width = win_ref.shape[2]
    rows_all = low_ref.shape[0]

    @pl.when(j == 0)
    def _():
        if carry:
            sum_ref[...] = start_ref[...]
        else:
            sum_ref[...] = jnp.zeros_like(sum_ref)

    for n in range(len(plan)):

        @pl.when(j == max(n - 2, 0))
        def _(n=n):
            for copy in chunk_copies(plan, src, n, win_ref, wback_ref, sem):
                copy.start()

    wait_chunk(plan, src, j, win_ref, wback_ref, sem)
    parts = wback_ref[j, width : width + 16, :width].astype(f32)
    bias = parts[0:1] + parts[1:2] + parts[2:3]
    for r in range(rows_all // span):
        rows = slice(r * span, (r + 1) * span)
        u, slope = gelu_both(dot(low_ref[rows, :], win_ref[j]) + bias)
        slope_ref[0, rows, :] = slope.astype(bf16)
        sum_ref[rows, :] += dot(u.astype(bf16), wback_ref[j, :width, :])


def feed_up(low, start, src, plan, width, span=512):
    rows, d = low.shape
    n = len(plan)
    carry = start is not None
    once = lambda: pl.BlockSpec((rows, d), lambda j: (0, 0), pipeline_mode=pl.Buffered(1))
    return pl.pallas_call(
        functools.partial(up_kernel, plan, len(src), carry, min(span, rows)),
        out_shape=(jax.ShapeDtypeStruct((rows, d), f32), jax.ShapeDtypeStruct((n, rows, width), bf16)),
        grid=(n,),
        in_specs=[once()] * (1 + carry) + [pl.BlockSpec(memory_space=pl.ANY) for _ in src],
        out_specs=[pl.BlockSpec((rows, d), lambda j: (0, 0)), pl.BlockSpec((1, rows, width), lambda j: (j, 0, 0))],
        scratch_shapes=[pltpu.VMEM((n, d, width), bf16), pltpu.VMEM((n, width + 16, d), bf16),
                        pltpu.SemaphoreType.DMA((d // width + 1, n))],
        compiler_params=pltpu.CompilerParams(vmem_limit_bytes=60 << 20),
        cost_estimate=pl.CostEstimate(flops=rows * d, bytes_accessed=8 * d, transcendentals=0),
        name="feed_up",
    )(low, *([start] if carry else []), *src)


def down_kernel(plan, nsrc, slopes_at, nslope, nr, span, ahead, *refs):
    n1_ref, rs1_ref, f_ref, cot_ref, pad_ref, wout_ref, pm_ref = refs[:7]
    src = refs[7 : 7 + nsrc]
    slope_src = refs[7 + nsrc : 7 + nsrc + nslope]
    (act_ref, dr1_ref, da_ref, stat_ref, db1_ref,
     win_ref, wback_ref, sem, slope_ref, slope_sem, low_ref, sum_ref) = refs[7 + nsrc + nslope :]
    i = pl.program_id(0)
    nchunk, _, width = win_ref.shape
    block = act_ref.shape[0]
    rows_all = low_ref.shape[0]

    def slope_copy(j):
        piece, at = slopes_at[j]
        return pltpu.make_async_copy(slope_src[piece].at[at], slope_ref.at[j], slope_sem.at[j])

    @pl.when(i == 0)
    def _():
        stat_ref[...] = jnp.zeros_like(stat_ref)
        db1_ref[...] = jnp.zeros_like(db1_ref)

    for j in range(nchunk):

        @pl.when(i == max(j - ahead, 0))
        def _(j=j):
            for copy in chunk_copies(plan, src, j, win_ref, wback_ref, sem):
                copy.start()
            slope_copy(j).start()

    row = lambda n: pm_ref[n : n + 1, :]

    def add_stat(n, v):
        stat_ref[n : n + 1, :] += jnp.sum(v, axis=0, keepdims=True)

    @pl.when(i < nr)
    def _():
        h1 = n1_ref[...] * row(3) + row(4)
        n2, rs2 = normed(h1 + (f_ref[...] + row(5)))
        act_ref[...] = n2 * row(6) + row(7)
        dy = cot_ref[...].astype(f32) * pad_ref[...]
        add_stat(6, dy * n2)
        add_stat(7, dy)
        dr2 = norm_back(n2, rs2, dy * row(6))
        add_stat(5, dr2)
        rows = pl.ds(pl.multiple_of(i * block, block), block)
        sum_ref[rows, :] = dr2
        low_ref[rows, :] = dr2.astype(bf16)

    @pl.when((i >= nr) & (i < nr + nchunk))
    def _():
        j = i - nr
        for n in range(nchunk):

            @pl.when(j == n)
            def _(n=n):
                for copy in chunk_copies(plan, src, n, win_ref, wback_ref, sem):
                    copy.wait()
                slope_copy(n).wait()

        for r in range(rows_all // span):
            rows = slice(r * span, (r + 1) * span)
            dz = dot(low_ref[rows, :], wback_ref[j, :width, :], NT) * slope_ref[j, rows, :].astype(f32)
            db1_ref[j] += jnp.sum(dz, axis=0, keepdims=True)
            sum_ref[rows, :] += dot(dz.astype(bf16), win_ref[j], NT)

    @pl.when(i >= nr + nchunk)
    def _():
        rows = pl.ds(pl.multiple_of((i - nr - nchunk) * block, block), block)
        n1 = n1_ref[...]
        dh1 = sum_ref[rows, :]
        add_stat(3, dh1 * n1)
        add_stat(4, dh1)
        dr1 = norm_back(n1, rs1_ref[rows, :], dh1 * row(3))
        add_stat(2, dr1)
        dr1_ref[...] = dr1
        da = dot(dr1.astype(bf16), wout_ref[...], NT).astype(bf16)
        da_ref[...] = da
        add_stat(1, da.astype(f32))


def feed_down(n1, rs1, f, cot, padcol, wout, pm, src, plan, slopes, slopes_at, width, block=512, span=256, ahead=1):
    rows, d = n1.shape
    nchunk = len(plan)
    nr = rows // block
    once = lambda s: pl.BlockSpec(s, lambda i: (0,) * len(s), pipeline_mode=pl.Buffered(1))
    early = lambda w: pl.BlockSpec((block, w), lambda i: (jnp.minimum(i, nr - 1), 0))
    late = lambda: pl.BlockSpec((block, d), lambda i: (jnp.maximum(i - nr - nchunk, 0), 0))
    both = pl.BlockSpec(
        (block, d), lambda i: (jnp.where(i < nr + nchunk - 1, jnp.minimum(i, nr - 1), jnp.maximum(i - nr - nchunk, 0)), 0)
    )
    hbm = lambda: pl.BlockSpec(memory_space=pl.ANY)
    return pl.pallas_call(
        functools.partial(down_kernel, plan, len(src), slopes_at, len(slopes), nr, min(span, rows), ahead),
        out_shape=(jax.ShapeDtypeStruct((rows, d), f32), jax.ShapeDtypeStruct((rows, d), f32),
                   jax.ShapeDtypeStruct((rows, d), bf16), jax.ShapeDtypeStruct((8, d), f32),
                   jax.ShapeDtypeStruct((nchunk, 1, width), f32)),
        grid=(2 * nr + nchunk,),
        in_specs=[both, once((rows, 1)), early(d), early(d), early(1), once((d, d)), once((8, d))]
        + [hbm() for _ in src] + [hbm() for _ in slopes],
        out_specs=[early(d), late(), late(), pl.BlockSpec((8, d), lambda i: (0, 0)),
                   pl.BlockSpec((nchunk, 1, width), lambda i: (0, 0, 0))],
        scratch_shapes=[pltpu.VMEM((nchunk, d, width), bf16), pltpu.VMEM((nchunk, width + 16, d), bf16),
                        pltpu.SemaphoreType.DMA((d // width + 1, nchunk)), pltpu.VMEM((nchunk, rows, width), bf16),
                        pltpu.SemaphoreType.DMA((nchunk,)), pltpu.VMEM((rows, d), bf16), pltpu.VMEM((rows, d), f32)],
        compiler_params=pltpu.CompilerParams(vmem_limit_bytes=60 << 20),
        cost_estimate=pl.CostEstimate(flops=rows * d, bytes_accessed=8 * d, transcendentals=0),
        name="feed_down",
    )(n1, rs1, f, cot, padcol, wout, pm, *src, *slopes)


def adam_step(grad, first, second, param, average):
    first_new = 0.5 * first + 0.5 * grad
    second_new = 0.5 * second + 0.5 * grad * grad
    corr = 1.0 - 0.5**STEP
    param_new = param - 0.25 * (
        first_new / corr / (jnp.sqrt(second_new / corr) + 1e-08) + 0.01 * param
    )
    return (
        first_new,
        second_new,
        param_new,
        param_new.astype(jnp.bfloat16),
        0.8 * average + 0.2 * param_new,
    )


def exchange(v, axis, bit):
    size = lax.axis_size(axis)
    return lax.ppermute(v, axis, [(i, i ^ bit) for i in range(size)])


def bits(size):
    return [1 << b for b in range(size.bit_length() - 1)]


def total_sum(v):
    if lax.axis_size("mp") == 8 and lax.axis_size("dp") == 4:
        v = v + exchange(v, "mp", 1)
        v = (v + exchange(v, "mp", 2)) + (exchange(v, "mp", 4) + exchange(v, "mp", 6))
        return (v + exchange(v, "dp", 1)) + (exchange(v, "dp", 2) + exchange(v, "dp", 3))
    for axis in ("mp", "dp"):
        for bit in bits(lax.axis_size(axis)):
            v = v + exchange(v, axis, bit)
    return v


def on_device(
    tokens,
    segment_ids,
    pad_mask,
    cotangent,
    w_query,
    w_key,
    w_value,
    w_out,
    w_in,
    w_back,
    params_main,
    params_hidden,
    first_main,
    second_main,
    first_hidden,
    second_hidden,
    average_main,
    average_hidden,
):
    rows_all, d = tokens.shape
    width = params_hidden.shape[0]
    devices = lax.axis_size("mp")
    me = lax.axis_index("mp")
    total_hidden = width * devices
    seg, pad = segment_ids[0], pad_mask[0]

    rounded = lambda v: lax.reduce_precision(v, 8, 7)
    high = rounded(params_hidden)
    middle = rounded(params_hidden - high)
    rows = jnp.stack([high, middle, rounded(params_hidden - high - middle)]).astype(bf16)
    packed = jnp.concatenate([w_in[g * width : (g + 1) * width] for g in range(d // width)], axis=1)
    own = jnp.concatenate([packed, w_back, jnp.pad(rows, ((0, 13), (0, d - width)))], axis=0)
    cube = devices == 8
    hop = lambda v, bit: exchange(v, "mp", bit)
    core, along_x, along_y = 1, 2, 4
    if cube:
        by_x, by_y, by_core = hop(own, along_x), hop(own, along_y), hop(own, core)

    win = windows(seg, BLK, ALLOWED)
    segcol = jnp.where(pad == 1, seg, -1)[:, None]
    segrow = seg[None, :]
    query = (0.125 * (dot(tokens, w_query) + params_main[0])).astype(bf16)
    keys = dot(tokens, w_key).astype(bf16)
    values = (dot(tokens, w_value) + params_main[1]).astype(bf16)
    mixed, lse = attn_fwd(query, keys, values, win, segcol, segrow, (0, d // PAIR))
    padcol = pad.astype(f32)[:, None]
    if cube:
        by_x, by_y, by_core, mixed = lax.optimization_barrier((by_x, by_y, by_core, mixed))
        far_in, far_back = hop(by_y[:width], along_x), hop(by_x[width:], along_y)
        near = [own, by_core, by_x, hop(by_x, core), by_y, hop(by_y, core)]
        normal_one, factor_one, low = out_norm(mixed, tokens, w_out, params_main)
        plan = tuple(((n, 0, 0), (n, 0, width)) for n in range(6))
        first = [p[None] for p in near]
        partial, slope_near = feed_up(low, None, first, plan, width)
        far_in, far_back, partial = lax.optimization_barrier((far_in, far_back, partial))
        rest = [p[None] for p in (far_in, far_back, hop(far_in, core), hop(far_back, core))]
        far_plan = (((0, 0, 0), (1, 0, 0)), ((2, 0, 0), (3, 0, 0)))
        partial, slope_far = feed_up(low, partial, rest, far_plan, width)
        sources, slopes = first + rest, [slope_near, slope_far]
        plan = plan + tuple(((6 + i[0],) + i[1:], (6 + b[0],) + b[1:]) for i, b in far_plan)
        slopes_at = tuple((0, n) for n in range(6)) + ((1, 0), (1, 1))
    else:
        sources = [lax.all_gather(own, "mp", axis=0)]
        plan = tuple(((0, j, 0), (0, j, width)) for j in range(devices))
        normal_one, factor_one, low = out_norm(mixed, tokens, w_out, params_main)
        partial, slope = feed_up(low, None, sources, plan, width)
        slopes, slopes_at = [slope], tuple((0, j) for j in range(devices))
    activations, dresid_one, dmixed, stats, hidden_grad = feed_down(
        normal_one, factor_one, partial, cotangent, padcol, w_out, params_main, sources, plan, slopes, slopes_at, width
    )
    input_grad, query_sum = attn_bwd(
        query, keys, values, mixed, dmixed, lse, win, segcol, segrow, dresid_one, w_query, w_key, w_value
    )
    if cube:
        hidden_grad = hidden_grad.reshape(2, 2, 2, width)
        for n in range(3):
            hidden_grad = jnp.where((me & (4 >> n)) > 0, jnp.flip(hidden_grad, n), hidden_grad)
    local = jnp.concatenate(
        [jnp.sum(query_sum, axis=0)[None], stats[1:], hidden_grad.reshape(total_hidden // d, d)], axis=0
    )
    total = total_sum(local)
    grad_norm = jnp.sqrt(jnp.sum(total * total))
    grad_main = total[:8]
    grad_hid = lax.dynamic_slice_in_dim(total[8:].reshape(total_hidden), me * width, width, 0)
    tokens_all = rows_all * lax.axis_size("dp") * devices
    limit = 0.01 * math.sqrt(tokens_all * (8 * d + total_hidden))
    scale_factor = jnp.minimum(1.0, limit / (grad_norm + 1e-06))
    grad_main = grad_main * scale_factor
    grad_hid = grad_hid * scale_factor
    fm, sm, pm, cm, am = adam_step(grad_main, first_main, second_main, params_main, average_main)
    fh, sh, ph, ch, ah = adam_step(grad_hid, first_hidden, second_hidden, params_hidden, average_hidden)
    return (
        activations,
        input_grad,
        grad_norm,
        grad_main,
        grad_hid,
        fm,
        sm,
        fh,
        sh,
        pm,
        ph,
        cm,
        ch,
        am,
        ah,
    )


def solution(mesh):
    placed = (
        P(("dp", "mp"), None),
        P(("dp", "mp"), None),
        P(("dp", "mp"), None),
        P(("dp", "mp"), None),
        P(),
        P(),
        P(),
        P(),
        P(None, "mp"),
        P("mp", None),
        P(),
        P("mp"),
        P(),
        P(),
        P("mp"),
        P("mp"),
        P(),
        P("mp"),
    )
    return jax.shard_map(
        on_device,
        mesh=mesh,
        in_specs=placed,
        out_specs=(
            P(("dp", "mp"), None),
            P(("dp", "mp"), None),
            P(),
            P(),
            P("mp"),
            P(),
            P(),
            P("mp"),
            P("mp"),
            P(),
            P("mp"),
            P(),
            P("mp"),
            P(),
            P("mp"),
        ),
        check_vma=False,
    )
```

```python
import functools
import math

import jax
import jax.numpy as jnp
from jax import lax
from jax.experimental import pallas as pl
from jax.experimental.pallas import tpu as pltpu
from jax.sharding import PartitionSpec as P

STEP = 5
f32, bf16 = jnp.float32, jnp.bfloat16
NN = (((1,), (0,)), ((), ()))
NT = (((1,), (1,)), ((), ()))
DN_NT = NT
DN_TN = (((0,), (0,)), ((), ()))

BLK = 128
PAIR = 128
CH = 128
NEG = -1e9
ALLOWED = (2, 3, 4, 5, 6, 8)


def windows(seg_row, blk, allowed):
    length = seg_row.shape[0]
    nb = length // blk
    first = seg_row[::blk]
    last = seg_row[blk - 1 :: blk]
    lo = jnp.sum(seg_row[None, :] < first[:, None], axis=1)
    hi = jnp.sum(seg_row[None, :] <= last[:, None], axis=1)
    start = lo // blk
    count = (hi + blk - 1) // blk - start
    allowed_arr = jnp.array(allowed)
    variant = jnp.sum(allowed_arr[None, :] < count[:, None], axis=1)
    size = allowed_arr[variant]
    start = jnp.minimum(start, nb - size)
    return jnp.stack([start, variant]).astype(jnp.int32)


def halves(x):
    lane = lax.broadcasted_iota(jnp.int32, x.shape, 1)
    zero = jnp.zeros_like(x)
    return jnp.concatenate([jnp.where(lane < 64, x, zero), jnp.where(lane >= 64, x, zero)], axis=0)


def fill_bias(bias_ref, segcol_ref, segrow_ref, i, start, width):
    rows = pl.ds(start * BLK, width)
    kcode = segcol_ref[rows, :]
    qseg = segrow_ref[:, pl.ds(pl.multiple_of(i * BLK, BLK), BLK)]
    kpos = start * BLK + lax.broadcasted_iota(jnp.int32, (width, BLK), 0)
    qpos = i * BLK + lax.broadcasted_iota(jnp.int32, (width, BLK), 1)
    vis = (kcode == qseg) | (kpos == qpos)
    bias_ref[pl.ds(0, width), :] = jnp.where(vis, 0.0, NEG).astype(f32)


def fwd_kernel(allowed, npair, unroll, win_ref, q_ref, k_ref, v_ref, segcol_ref, segrow_ref, o_ref, lse_ref, bias_ref):
    i = pl.program_id(0)
    start = win_ref[0, i]
    variant = win_ref[1, i]
    for n, size in enumerate(allowed):
        width = size * BLK

        @pl.when(variant == n)
        def _(width=width):
            fill_bias(bias_ref, segcol_ref, segrow_ref, i, start, width)
            rows = pl.ds(pl.multiple_of(start * BLK, BLK), width)

            def pair(h):
                cols = pl.ds(pl.multiple_of(h * PAIR, PAIR), PAIR)
                qbd = halves(q_ref[:, cols])
                s = lax.dot_general(k_ref[rows, cols], qbd, DN_NT, preferred_element_type=f32)
                b = bias_ref[pl.ds(0, width), :]
                s = s + jnp.concatenate([b, b], axis=1)
                top = jnp.max(s, axis=0, keepdims=True)
                p = jnp.exp(s - top)
                tot = jnp.sum(p, axis=0, keepdims=True)
                o = lax.dot_general(p.astype(bf16), v_ref[rows, cols], DN_TN, preferred_element_type=f32)
                inv = jnp.broadcast_to(1.0 / tot, (8, 2 * BLK)).T[:, :1]
                o = o * inv
                lane = lax.broadcasted_iota(jnp.int32, (BLK, PAIR), 1)
                o_ref[:, cols] = jnp.where(lane < 64, o[:BLK], o[BLK:]).astype(bf16)
                lse_ref[0, pl.ds(h, 1), :] = top + jnp.log(tot)

            def body(t, c):
                for u in range(unroll):
                    pair(t * unroll + u)
                return c

            lax.fori_loop(0, npair // unroll, body, 0)


def attn_fwd(q, k, v, win, segcol, segrow, pairs, allowed=ALLOWED, unroll=8):
    length = q.shape[0]
    npair = pairs[1] - pairs[0]
    d, part = npair * PAIR, pairs[0] // npair
    nb = length // BLK
    unroll = min(unroll, npair)
    full = lambda: pl.BlockSpec((length, d), lambda i, w: (0, part))
    return pl.pallas_call(
        functools.partial(fwd_kernel, allowed, npair, unroll),
        out_shape=(jax.ShapeDtypeStruct((length, d), bf16), jax.ShapeDtypeStruct((nb, npair, 2 * BLK), f32)),
        grid_spec=pltpu.PrefetchScalarGridSpec(
            num_scalar_prefetch=1, grid=(nb,),
            in_specs=[pl.BlockSpec((BLK, d), lambda i, w: (i, part)), full(), full(),
                      pl.BlockSpec((length, 1), lambda i, w: (0, 0)), pl.BlockSpec((1, length), lambda i, w: (0, 0))],
            out_specs=[pl.BlockSpec((BLK, d), lambda i, w: (i, 0)), pl.BlockSpec((1, npair, 2 * BLK), lambda i, w: (i, 0, 0))],
            scratch_shapes=[pltpu.VMEM((length, BLK), f32)]),
        compiler_params=pltpu.CompilerParams(vmem_limit_bytes=60 << 20),
        cost_estimate=pl.CostEstimate(flops=length * d, bytes_accessed=8 * d, transcendentals=0),
        name="attend",
    )(win, q, k, v, segcol, segrow)


def bwd_kernel(allowed, npair, unroll, win_ref, q_ref, k_ref, v_ref, o_ref, do_ref, lse_ref, segcol_ref, segrow_ref,
               dr1_ref, wq_hbm, wk_hbm, wv_hbm, grad_ref, qsum_ref,
               bias_ref, p_ref, ds_ref, delta_ref, dq_ref, dk_ref, dv_ref, w_ref, sem):
    i = pl.program_id(0)
    nblock = k_ref.shape[0] // BLK
    loads = [pltpu.make_async_copy(w, w_ref.at[n], sem.at[n]) for n, w in enumerate((wq_hbm, wk_hbm, wv_hbm))]

    @pl.when(i == 0)
    def _():
        for load in loads:
            load.start()
        dk_ref[...] = jnp.zeros_like(dk_ref)
        dv_ref[...] = jnp.zeros_like(dv_ref)
        qsum_ref[...] = jnp.zeros_like(qsum_ref)

    @pl.when(i < nblock)
    def _():
        prod = do_ref[...].astype(f32) * o_ref[...].astype(f32)
        high = prod.astype(bf16)
        low = (prod - high.astype(f32)).astype(bf16)
        head = lax.broadcasted_iota(jnp.int32, (2 * npair, npair * PAIR), 0)
        lanes = lax.broadcasted_iota(jnp.int32, (2 * npair, npair * PAIR), 1)
        pick = jnp.where(lanes // 64 == head, 1.0, 0.0).astype(bf16)
        delta_ref[...] = lax.dot_general(pick, high, DN_NT, preferred_element_type=f32) + lax.dot_general(
            pick, low, DN_NT, preferred_element_type=f32
        )

    block = jnp.minimum(i, nblock - 1)
    start = win_ref[0, block]
    variant = jnp.where(i < nblock, win_ref[1, block], -1)
    for n, size in enumerate(allowed):
        width = size * BLK

        @pl.when(variant == n)
        def _(width=width):
            fill_bias(bias_ref, segcol_ref, segrow_ref, i, start, width)
            rows = pl.ds(pl.multiple_of(start * BLK, BLK), width)

            def pair(h, u):
                cols = pl.ds(pl.multiple_of(h * PAIR, PAIR), PAIR)
                qbd = halves(q_ref[:, cols])
                dobd = halves(do_ref[:, cols])
                lse = lse_ref[0, pl.ds(h, 1), :]
                delta = jnp.concatenate([delta_ref[pl.ds(2 * h, 1), :], delta_ref[pl.ds(2 * h + 1, 1), :]], axis=1)
                for c in range(width // CH):
                    crow = pl.ds(pl.multiple_of(start * BLK + c * CH, CH), CH)
                    span = slice(c * CH, (c + 1) * CH)
                    s = lax.dot_general(k_ref[crow, cols], qbd, DN_NT, preferred_element_type=f32)
                    dp = lax.dot_general(v_ref[crow, cols], dobd, DN_NT, preferred_element_type=f32)
                    b = bias_ref[span, :]
                    p = jnp.exp(s + jnp.concatenate([b, b], axis=1) - lse)
                    p_ref[u, span, :] = p.astype(bf16)
                    ds_ref[u, span, :] = (p * (dp - delta)).astype(bf16)
                nn = (((1,), (0,)), ((), ()))
                dv_ref[rows, cols] += lax.dot_general(p_ref[u, :width, :], dobd, nn, preferred_element_type=f32)
                dk_ref[rows, cols] += lax.dot_general(ds_ref[u, :width, :], qbd, nn, preferred_element_type=f32)
                dq = lax.dot_general(ds_ref[u, :width, :], k_ref[rows, cols], DN_TN, preferred_element_type=f32)
                lane = lax.broadcasted_iota(jnp.int32, (BLK, PAIR), 1)
                dq = 0.125 * jnp.where(lane < 64, dq[:BLK], dq[BLK:])
                dq_ref[pl.ds(pl.multiple_of(i * BLK, BLK), BLK), cols] = dq.astype(bf16)
                qsum_ref[:, cols] += jnp.sum(dq.reshape(BLK // 8, 8, PAIR), axis=0)

            def body(t, c):
                for u in range(unroll):
                    pair(t * unroll + u, u)
                return c

            lax.fori_loop(0, npair // unroll, body, 0)

    @pl.when(i == nblock)
    def _():
        for load in loads:
            load.wait()

    @pl.when(i >= nblock)
    def _():
        span = grad_ref.shape[0]
        rows = pl.ds(pl.multiple_of((i - nblock) * span, span), span)
        total = lax.dot_general(dq_ref[rows, :], w_ref[0], DN_NT, preferred_element_type=f32)
        total += lax.dot_general(dk_ref[rows, :].astype(bf16), w_ref[1], DN_NT, preferred_element_type=f32)
        total += lax.dot_general(dv_ref[rows, :].astype(bf16), w_ref[2], DN_NT, preferred_element_type=f32)
        grad_ref[...] = dr1_ref[...] + total


def attn_bwd(q, k, v, o, do, lse, win, segcol, segrow, dr1, wq, wk, wv, allowed=ALLOWED, unroll=8, span=512):
    length, d = q.shape
    nb, npair = length // BLK, d // PAIR
    one = pl.Buffered(1)
    full = lambda: pl.BlockSpec((length, d), lambda i, w: (0, 0), pipeline_mode=one)
    row = lambda: pl.BlockSpec((BLK, d), lambda i, w: (jnp.minimum(i, nb - 1), 0))
    wide = lambda: pl.BlockSpec((span, d), lambda i, w: (jnp.maximum(i - nb, 0), 0))
    hbm = lambda: pl.BlockSpec(memory_space=pl.ANY)
    return pl.pallas_call(
        functools.partial(bwd_kernel, allowed, npair, unroll),
        out_shape=(jax.ShapeDtypeStruct((length, d), f32), jax.ShapeDtypeStruct((8, d), f32)),
        grid_spec=pltpu.PrefetchScalarGridSpec(
            num_scalar_prefetch=1, grid=(nb + length // span,),
            in_specs=[row(), full(), full(), row(), row(),
                      pl.BlockSpec((1, npair, 2 * BLK), lambda i, w: (jnp.minimum(i, nb - 1), 0, 0)),
                      pl.BlockSpec((length, 1), lambda i, w: (0, 0)), pl.BlockSpec((1, length), lambda i, w: (0, 0)),
                      wide(), hbm(), hbm(), hbm()],
            out_specs=[wide(), pl.BlockSpec((8, d), lambda i, w: (0, 0))],
            scratch_shapes=[pltpu.VMEM((length, BLK), f32), pltpu.VMEM((unroll, length, 2 * BLK), bf16),
                            pltpu.VMEM((unroll, length, 2 * BLK), bf16), pltpu.VMEM((2 * npair, BLK), f32),
                            pltpu.VMEM((length, d), bf16), pltpu.VMEM((length, d), f32), pltpu.VMEM((length, d), f32),
                            pltpu.VMEM((3, d, d), bf16), pltpu.SemaphoreType.DMA((3,))]),
        compiler_params=pltpu.CompilerParams(vmem_limit_bytes=60 << 20),
        cost_estimate=pl.CostEstimate(flops=5 * length * length * d, bytes_accessed=14 * length * d, transcendentals=length * length * npair),
        name="attend_back",
    )(win, q, k, v, o, do, lse, segcol, segrow, dr1, wq, wk, wv)
def dot(a, b, dims=NN):
    return lax.dot_general(a, b, dims, preferred_element_type=f32)


def gelu_both(z):
    e = jnp.exp2(z * z * -0.7213475204444817)
    t = 1.0 / (1.0 + 0.23164189 * jnp.abs(z))
    poly = t * (0.127414796 + t * (-0.142248368 + t * (0.7107068705 + t * (-0.7265760135 + t * 0.5307027145))))
    tail = poly * e
    phi = jnp.where(z >= 0, 1.0 - tail, tail)
    return z * phi, phi + z * e * 0.3989422804014327


def normed(r):
    center = r - jnp.mean(r, axis=-1, keepdims=True)
    factor = lax.rsqrt(jnp.mean(center * center, axis=-1, keepdims=True) + 1e-05)
    return center * factor, factor


def norm_back(normal, factor, dn):
    return factor * (
        dn - jnp.mean(dn, axis=-1, keepdims=True) - normal * jnp.mean(dn * normal, axis=-1, keepdims=True)
    )


def out_kernel(a_ref, x_ref, wout_ref, pm_ref, n1_ref, rs1_ref, low_ref):
    r = x_ref[...].astype(f32) + dot(a_ref[...], wout_ref[...]) + pm_ref[2:3, :]
    n1, rs1 = normed(r)
    n1_ref[...] = n1
    rs1_ref[...] = rs1
    low_ref[...] = (n1 * pm_ref[3:4, :] + pm_ref[4:5, :]).astype(bf16)


def out_norm(a, x, wout, pm, block=512):
    rows, d = x.shape
    r = lambda: pl.BlockSpec((block, d), lambda i: (i, 0))
    once = lambda s: pl.BlockSpec(s, lambda i: (0,) * len(s), pipeline_mode=pl.Buffered(1))
    return pl.pallas_call(
        out_kernel,
        out_shape=(jax.ShapeDtypeStruct((rows, d), f32), jax.ShapeDtypeStruct((rows, 1), f32),
                   jax.ShapeDtypeStruct((rows, d), bf16)),
        grid=(rows // block,),
        in_specs=[r(), r(), once((d, d)), once((8, d))],
        out_specs=[r(), pl.BlockSpec((block, 1), lambda i: (i, 0)), r()],
        compiler_params=pltpu.CompilerParams(vmem_limit_bytes=60 << 20),
        cost_estimate=pl.CostEstimate(flops=rows * d, bytes_accessed=8 * d, transcendentals=0),
        name="join",
    )(a, x, wout, pm)


def chunk_copies(plan, src, j, win_ref, wback_ref, sem):
    d, width = win_ref.shape[1:]
    piece, at, row = plan[j][0]
    moves = [
        (src[piece].at[at, pl.ds(row, width), pl.ds(g * width, width)], win_ref.at[j, pl.ds(g * width, width)])
        for g in range(d // width)
    ]
    piece, at, row = plan[j][1]
    moves.append((src[piece].at[at, pl.ds(row, width + 16)], wback_ref.at[j]))
    return [pltpu.make_async_copy(s, t, sem.at[n, j]) for n, (s, t) in enumerate(moves)]


def wait_chunk(plan, src, j, win_ref, wback_ref, sem):
    for n in range(len(plan)):

        @pl.when(j == n)
        def _(n=n):
            for copy in chunk_copies(plan, src, n, win_ref, wback_ref, sem):
                copy.wait()


def up_kernel(plan, nsrc, span, *refs):
    low_ref, refs = refs[0], refs[1:]
    src = refs[:nsrc]
    sum_ref, slope_ref, win_ref, wback_ref, sem = refs[nsrc:]
    j = pl.program_id(0)
    width = win_ref.shape[2]
    rows_all = low_ref.shape[0]

    @pl.when(j == 0)
    def _():
        sum_ref[...] = jnp.zeros_like(sum_ref)

    for n in range(len(plan)):

        @pl.when(j == max(n - 2, 0))
        def _(n=n):
            for copy in chunk_copies(plan, src, n, win_ref, wback_ref, sem):
                copy.start()

    wait_chunk(plan, src, j, win_ref, wback_ref, sem)
    parts = wback_ref[j, width : width + 16, :width].astype(f32)
    bias = parts[0:1] + parts[1:2] + parts[2:3]
    def up(r, t):
        rows = pl.ds(pl.multiple_of(r * span, span), span)
        u, slope = gelu_both(dot(low_ref[rows, :], win_ref[j]) + bias)
        slope_ref[0, rows, :] = slope.astype(bf16)
        sum_ref[rows, :] += dot(u.astype(bf16), wback_ref[j, :width, :])
        return t

    lax.fori_loop(0, rows_all // span, up, 0)


def feed_up(low, src, plan, width, span=512):
    rows, d = low.shape
    n = len(plan)
    once = lambda: pl.BlockSpec((rows, d), lambda j: (0, 0), pipeline_mode=pl.Buffered(1))
    return pl.pallas_call(
        functools.partial(up_kernel, plan, len(src), min(span, rows)),
        out_shape=(jax.ShapeDtypeStruct((rows, d), f32), jax.ShapeDtypeStruct((n, rows, width), bf16)),
        grid=(n,),
        in_specs=[once()] + [pl.BlockSpec(memory_space=pl.ANY) for _ in src],
        out_specs=[pl.BlockSpec((rows, d), lambda j: (0, 0)), pl.BlockSpec((1, rows, width), lambda j: (j, 0, 0))],
        scratch_shapes=[pltpu.VMEM((n, d, width), bf16), pltpu.VMEM((n, width + 16, d), bf16),
                        pltpu.SemaphoreType.DMA((d // width + 1, n))],
        compiler_params=pltpu.CompilerParams(vmem_limit_bytes=60 << 20),
        cost_estimate=pl.CostEstimate(flops=rows * d, bytes_accessed=8 * d, transcendentals=0),
        name="feed_up",
    )(low, *src)


def down_kernel(plan, nsrc, nfar, nr, span, *refs):
    low_in, n1_in, f_in, rs1_ref, cot_ref, pad_ref, wout_ref, pm_ref = refs[:8]
    src = refs[8 : 8 + nsrc]
    slope_src = refs[8 + nsrc]
    (act_ref, dr1_ref, da_ref, stat_ref, db1_ref,
     win_ref, wback_ref, sem, slope_ref, slope_sem, low_ref, sum_ref, n1_ref, row_sem) = refs[9 + nsrc :]
    i = pl.program_id(0)
    nchunk, _, width = win_ref.shape
    block = act_ref.shape[0]
    rows_all = low_ref.shape[0]
    get_low = pltpu.make_async_copy(low_in, low_ref, row_sem.at[0])
    get_f = pltpu.make_async_copy(f_in, sum_ref, row_sem.at[1])
    get_n1 = pltpu.make_async_copy(n1_in, n1_ref, row_sem.at[2])

    def copies(j):
        moves = chunk_copies(plan, src, j, win_ref, wback_ref, sem)
        if j >= nfar:
            moves.append(pltpu.make_async_copy(slope_src.at[j - nfar], slope_ref.at[j], slope_sem.at[j]))
        return moves

    def start(j):
        for copy in copies(j):
            copy.start()

    def wait(j):
        for copy in copies(j):
            copy.wait()

    @pl.when(i == 0)
    def _():
        get_low.start()
        for j in range(nfar):
            start(j)
        get_f.start()
        get_n1.start()
        stat_ref[...] = jnp.zeros_like(stat_ref)
        db1_ref[...] = jnp.zeros_like(db1_ref)
        get_low.wait()
        if not nfar:
            get_f.wait()

    for j in range(nfar, nchunk):

        @pl.when(i == 1 + (j - nfar) // 2)
        def _(j=j):
            start(j)

    row = lambda n: pm_ref[n : n + 1, :]

    def add_stat(n, v):
        stat_ref[n : n + 1, :] += jnp.sum(v, axis=0, keepdims=True)

    for j in range(nfar):

        @pl.when(i == j)
        def _(j=j):
            wait(j)
            if j == 0:
                get_f.wait()

    @pl.when(i < nfar)
    def _():
        parts = wback_ref[i, width : width + 16, :width].astype(f32)
        bias = parts[0:1] + parts[1:2] + parts[2:3]

        def up(r, t):
            rows = pl.ds(pl.multiple_of(r * block, block), block)
            u, slope = gelu_both(dot(low_ref[rows, :], win_ref[i]) + bias)
            slope_ref[i, rows, :] = slope.astype(bf16)
            sum_ref[rows, :] += dot(u.astype(bf16), wback_ref[i, :width, :])
            return t

        lax.fori_loop(0, rows_all // block, up, 0)

    @pl.when(i == nfar)
    def _():
        get_n1.wait()

    @pl.when((i >= nfar) & (i < nfar + nr))
    def _():
        rows = pl.ds(pl.multiple_of((i - nfar) * block, block), block)
        h1 = n1_ref[rows, :] * row(3) + row(4)
        n2, rs2 = normed(h1 + (sum_ref[rows, :] + row(5)))
        act_ref[...] = n2 * row(6) + row(7)
        dy = cot_ref[...].astype(f32) * pad_ref[...]
        add_stat(6, dy * n2)
        add_stat(7, dy)
        dr2 = norm_back(n2, rs2, dy * row(6))
        add_stat(5, dr2)
        sum_ref[rows, :] = dr2
        low_ref[rows, :] = dr2.astype(bf16)

    last = nfar + nr + nchunk

    @pl.when((i >= nfar + nr) & (i < last))
    def _():
        j = i - nfar - nr
        for n in range(nfar, nchunk):

            @pl.when(j == n)
            def _(n=n):
                wait(n)

        for r in range(rows_all // span):
            rows = slice(r * span, (r + 1) * span)
            dz = dot(low_ref[rows, :], wback_ref[j, :width, :], NT) * slope_ref[j, rows, :].astype(f32)
            db1_ref[j] += jnp.sum(dz, axis=0, keepdims=True)
            sum_ref[rows, :] += dot(dz.astype(bf16), win_ref[j], NT)

    @pl.when(i >= last)
    def _():
        rows = pl.ds(pl.multiple_of((i - last) * block, block), block)
        n1 = n1_ref[rows, :]
        dh1 = sum_ref[rows, :]
        add_stat(3, dh1 * n1)
        add_stat(4, dh1)
        dr1 = norm_back(n1, rs1_ref[rows, :], dh1 * row(3))
        add_stat(2, dr1)
        dr1_ref[...] = dr1
        da = dot(dr1.astype(bf16), wout_ref[...], NT).astype(bf16)
        da_ref[...] = da
        add_stat(1, da.astype(f32))


def feed_down(low, n1, f, rs1, cot, padcol, wout, pm, src, plan, slopes, nfar, width, block=512, span=512):
    rows, d = low.shape
    nchunk = len(plan)
    block, span = min(block, rows), min(span, rows)
    nr = rows // block
    last = nfar + nr + nchunk
    once = lambda s: pl.BlockSpec(s, lambda i: (0,) * len(s), pipeline_mode=pl.Buffered(1))
    early = lambda w: pl.BlockSpec((block, w), lambda i: (jnp.clip(i - nfar, 0, nr - 1), 0))
    late = lambda: pl.BlockSpec((block, d), lambda i: (jnp.maximum(i - last, 0), 0))
    hbm = lambda: pl.BlockSpec(memory_space=pl.ANY)
    return pl.pallas_call(
        functools.partial(down_kernel, plan, len(src), nfar, nr, span),
        out_shape=(jax.ShapeDtypeStruct((rows, d), f32), jax.ShapeDtypeStruct((rows, d), f32),
                   jax.ShapeDtypeStruct((rows, d), bf16), jax.ShapeDtypeStruct((8, d), f32),
                   jax.ShapeDtypeStruct((nchunk, 1, width), f32)),
        grid=(last + nr,),
        in_specs=[hbm(), hbm(), hbm(), once((rows, 1)), early(d), early(1), once((d, d)), once((8, d))]
        + [hbm() for _ in src] + [hbm()],
        out_specs=[early(d), late(), late(), pl.BlockSpec((8, d), lambda i: (0, 0)),
                   pl.BlockSpec((nchunk, 1, width), lambda i: (0, 0, 0))],
        scratch_shapes=[pltpu.VMEM((nchunk, d, width), bf16), pltpu.VMEM((nchunk, width + 16, d), bf16),
                        pltpu.SemaphoreType.DMA((d // width + 1, nchunk)), pltpu.VMEM((nchunk, rows, width), bf16),
                        pltpu.SemaphoreType.DMA((nchunk,)), pltpu.VMEM((rows, d), bf16), pltpu.VMEM((rows, d), f32),
                        pltpu.VMEM((rows, d), f32), pltpu.SemaphoreType.DMA((3,))],
        compiler_params=pltpu.CompilerParams(vmem_limit_bytes=62 << 20),
        cost_estimate=pl.CostEstimate(flops=rows * d, bytes_accessed=8 * d, transcendentals=0),
        name="feed_down",
    )(low, n1, f, rs1, cot, padcol, wout, pm, *src, slopes)


def adam_step(grad, first, second, param, average):
    first_new = 0.5 * first + 0.5 * grad
    second_new = 0.5 * second + 0.5 * grad * grad
    corr = 1.0 - 0.5**STEP
    param_new = param - 0.25 * (
        first_new / corr / (jnp.sqrt(second_new / corr) + 1e-08) + 0.01 * param
    )
    return (
        first_new,
        second_new,
        param_new,
        param_new.astype(jnp.bfloat16),
        0.8 * average + 0.2 * param_new,
    )


def exchange(v, axis, bit):
    size = lax.axis_size(axis)
    return lax.ppermute(v, axis, [(i, i ^ bit) for i in range(size)])


def bits(size):
    return [1 << b for b in range(size.bit_length() - 1)]


def total_sum(v):
    if lax.axis_size("mp") == 8 and lax.axis_size("dp") == 4:
        v = v + exchange(v, "mp", 1)
        v = (v + exchange(v, "mp", 2)) + (exchange(v, "mp", 4) + exchange(v, "mp", 6))
        return (v + exchange(v, "dp", 1)) + (exchange(v, "dp", 2) + exchange(v, "dp", 3))
    for axis in ("mp", "dp"):
        for bit in bits(lax.axis_size(axis)):
            v = v + exchange(v, axis, bit)
    return v


def on_device(
    tokens,
    segment_ids,
    pad_mask,
    cotangent,
    w_query,
    w_key,
    w_value,
    w_out,
    w_in,
    w_back,
    params_main,
    params_hidden,
    first_main,
    second_main,
    first_hidden,
    second_hidden,
    average_main,
    average_hidden,
):
    rows_all, d = tokens.shape
    width = params_hidden.shape[0]
    devices = lax.axis_size("mp")
    me = lax.axis_index("mp")
    total_hidden = width * devices
    seg, pad = segment_ids[0], pad_mask[0]

    rounded = lambda v: lax.reduce_precision(v, 8, 7)
    high = rounded(params_hidden)
    middle = rounded(params_hidden - high)
    rows = jnp.stack([high, middle, rounded(params_hidden - high - middle)]).astype(bf16)
    packed = jnp.concatenate([w_in[g * width : (g + 1) * width] for g in range(d // width)], axis=1)
    own = jnp.concatenate([packed, w_back, jnp.pad(rows, ((0, 13), (0, d - width)))], axis=0)
    cube = devices == 8
    hop = lambda v, bit: exchange(v, "mp", bit)
    core, along_x, along_y = 1, 2, 4
    if cube:
        by_x, by_y, by_core = hop(own, along_x), hop(own, along_y), hop(own, core)

    win = windows(seg, BLK, ALLOWED)
    segcol = jnp.where(pad == 1, seg, -1)[:, None]
    segrow = seg[None, :]
    query = (0.125 * (dot(tokens, w_query) + params_main[0])).astype(bf16)
    keys = dot(tokens, w_key).astype(bf16)
    values = (dot(tokens, w_value) + params_main[1]).astype(bf16)
    mixed, lse = attn_fwd(query, keys, values, win, segcol, segrow, (0, d // PAIR))
    padcol = pad.astype(f32)[:, None]
    if cube:
        by_x, by_y, by_core, mixed = lax.optimization_barrier((by_x, by_y, by_core, mixed))
        far_in, far_back = hop(by_y[:width], along_x), hop(by_x[width:], along_y)
        near = [own, by_core, by_x, hop(by_x, core), by_y, hop(by_y, core)]
        normal_one, factor_one, low = out_norm(mixed, tokens, w_out, params_main)
        plan = tuple(((n, 0, 0), (n, 0, width)) for n in range(6))
        first = [p[None] for p in near]
        partial, slopes = feed_up(low, first, plan, width)
        far_in, far_back, partial = lax.optimization_barrier((far_in, far_back, partial))
        rest = [p[None] for p in (far_in, far_back, hop(far_in, core), hop(far_back, core))]
        far_plan = (((0, 0, 0), (1, 0, 0)), ((2, 0, 0), (3, 0, 0)))
        sources = first + rest
        plan = tuple(((6 + n[0],) + n[1:], (6 + m[0],) + m[1:]) for n, m in far_plan) + plan
        far = 2
    else:
        sources = [lax.all_gather(own, "mp", axis=0)]
        plan = tuple(((0, j, 0), (0, j, width)) for j in range(devices))
        normal_one, factor_one, low = out_norm(mixed, tokens, w_out, params_main)
        partial, slopes = feed_up(low, sources, plan, width)
        far = 0
    activations, dresid_one, dmixed, stats, hidden_grad = feed_down(
        low, normal_one, partial, factor_one, cotangent, padcol, w_out, params_main, sources, plan, slopes, far, width
    )
    input_grad, query_sum = attn_bwd(
        query, keys, values, mixed, dmixed, lse, win, segcol, segrow, dresid_one, w_query, w_key, w_value
    )
    if cube:
        hidden_grad = jnp.roll(hidden_grad, 6, axis=0).reshape(2, 2, 2, width)
        for n in range(3):
            hidden_grad = jnp.where((me & (4 >> n)) > 0, jnp.flip(hidden_grad, n), hidden_grad)
    local = jnp.concatenate(
        [jnp.sum(query_sum, axis=0)[None], stats[1:], hidden_grad.reshape(total_hidden // d, d)], axis=0
    )
    total = total_sum(local)
    grad_norm = jnp.sqrt(jnp.sum(total * total))
    grad_main = total[:8]
    grad_hid = lax.dynamic_slice_in_dim(total[8:].reshape(total_hidden), me * width, width, 0)
    tokens_all = rows_all * lax.axis_size("dp") * devices
    limit = 0.01 * math.sqrt(tokens_all * (8 * d + total_hidden))
    scale_factor = jnp.minimum(1.0, limit / (grad_norm + 1e-06))
    grad_main = grad_main * scale_factor
    grad_hid = grad_hid * scale_factor
    fm, sm, pm, cm, am = adam_step(grad_main, first_main, second_main, params_main, average_main)
    fh, sh, ph, ch, ah = adam_step(grad_hid, first_hidden, second_hidden, params_hidden, average_hidden)
    return (
        activations,
        input_grad,
        grad_norm,
        grad_main,
        grad_hid,
        fm,
        sm,
        fh,
        sh,
        pm,
        ph,
        cm,
        ch,
        am,
        ah,
    )


def solution(mesh):
    placed = (
        P(("dp", "mp"), None),
        P(("dp", "mp"), None),
        P(("dp", "mp"), None),
        P(("dp", "mp"), None),
        P(),
        P(),
        P(),
        P(),
        P(None, "mp"),
        P("mp", None),
        P(),
        P("mp"),
        P(),
        P(),
        P("mp"),
        P("mp"),
        P(),
        P("mp"),
    )
    return jax.shard_map(
        on_device,
        mesh=mesh,
        in_specs=placed,
        out_specs=(
            P(("dp", "mp"), None),
            P(("dp", "mp"), None),
            P(),
            P(),
            P("mp"),
            P(),
            P(),
            P("mp"),
            P("mp"),
            P(),
            P("mp"),
            P(),
            P("mp"),
            P(),
            P("mp"),
        ),
        check_vma=False,
    )
```

```python
import functools
import math

import jax
import jax.numpy as jnp
from jax import lax
from jax.experimental import pallas as pl
from jax.experimental.pallas import tpu as pltpu
from jax.sharding import PartitionSpec as P

STEP = 5
f32, bf16 = jnp.float32, jnp.bfloat16
NN = (((1,), (0,)), ((), ()))
NT = (((1,), (1,)), ((), ()))
DN_NT = NT
DN_TN = (((0,), (0,)), ((), ()))

BLK = 128
PAIR = 128
CH = 128
NEG = -1e9
ALLOWED = (2, 3, 4, 5, 6, 8)


def windows(seg_row, blk, allowed):
    length = seg_row.shape[0]
    nb = length // blk
    first = seg_row[::blk]
    last = seg_row[blk - 1 :: blk]
    lo = jnp.sum(seg_row[None, :] < first[:, None], axis=1)
    hi = jnp.sum(seg_row[None, :] <= last[:, None], axis=1)
    start = lo // blk
    count = (hi + blk - 1) // blk - start
    variant = jnp.zeros_like(count)
    size = jnp.full_like(count, allowed[0])
    for small, large in zip(allowed, allowed[1:]):
        over = (count > small).astype(count.dtype)
        variant = variant + over
        size = size + over * (large - small)
    start = jnp.minimum(start, nb - size)
    return jnp.stack([start, variant]).astype(jnp.int32)


def halves(x):
    lane = lax.broadcasted_iota(jnp.int32, x.shape, 1)
    zero = jnp.zeros_like(x)
    return jnp.concatenate([jnp.where(lane < 64, x, zero), jnp.where(lane >= 64, x, zero)], axis=0)


def fill_bias(bias_ref, segcol_ref, segrow_ref, i, start, width):
    rows = pl.ds(start * BLK, width)
    kcode = segcol_ref[rows, :]
    qseg = segrow_ref[:, pl.ds(pl.multiple_of(i * BLK, BLK), BLK)]
    kpos = start * BLK + lax.broadcasted_iota(jnp.int32, (width, BLK), 0)
    qpos = i * BLK + lax.broadcasted_iota(jnp.int32, (width, BLK), 1)
    vis = (kcode == qseg) | (kpos == qpos)
    bias_ref[pl.ds(0, width), :] = jnp.where(vis, 0.0, NEG).astype(f32)


def fwd_kernel(allowed, npair, unroll, win_ref, q_ref, k_ref, v_ref, segcol_ref, segrow_ref, o_ref, lse_ref, bias_ref):
    i = pl.program_id(0)
    start = win_ref[0, i]
    variant = win_ref[1, i]
    for n, size in enumerate(allowed):
        width = size * BLK

        @pl.when(variant == n)
        def _(width=width):
            fill_bias(bias_ref, segcol_ref, segrow_ref, i, start, width)
            rows = pl.ds(pl.multiple_of(start * BLK, BLK), width)

            def pair(h):
                cols = pl.ds(pl.multiple_of(h * PAIR, PAIR), PAIR)
                qbd = halves(q_ref[:, cols])
                s = lax.dot_general(k_ref[rows, cols], qbd, DN_NT, preferred_element_type=f32)
                b = bias_ref[pl.ds(0, width), :]
                s = s + jnp.concatenate([b, b], axis=1)
                top = jnp.max(s, axis=0, keepdims=True)
                p = jnp.exp(s - top)
                tot = jnp.sum(p, axis=0, keepdims=True)
                o = lax.dot_general(p.astype(bf16), v_ref[rows, cols], DN_TN, preferred_element_type=f32)
                inv = jnp.broadcast_to(1.0 / tot, (8, 2 * BLK)).T[:, :1]
                o = o * inv
                lane = lax.broadcasted_iota(jnp.int32, (BLK, PAIR), 1)
                o_ref[:, cols] = jnp.where(lane < 64, o[:BLK], o[BLK:]).astype(bf16)
                lse_ref[0, pl.ds(h, 1), :] = top + jnp.log(tot)

            def body(t, c):
                for u in range(unroll):
                    pair(t * unroll + u)
                return c

            lax.fori_loop(0, npair // unroll, body, 0)


def attn_fwd(q, k, v, win, segcol, segrow, pairs, allowed=ALLOWED, unroll=8):
    length = q.shape[0]
    npair = pairs[1] - pairs[0]
    d, part = npair * PAIR, pairs[0] // npair
    nb = length // BLK
    unroll = min(unroll, npair)
    full = lambda: pl.BlockSpec((length, d), lambda i, w: (0, part))
    return pl.pallas_call(
        functools.partial(fwd_kernel, allowed, npair, unroll),
        out_shape=(jax.ShapeDtypeStruct((length, d), bf16), jax.ShapeDtypeStruct((nb, npair, 2 * BLK), f32)),
        grid_spec=pltpu.PrefetchScalarGridSpec(
            num_scalar_prefetch=1, grid=(nb,),
            in_specs=[pl.BlockSpec((BLK, d), lambda i, w: (i, part)), full(), full(),
                      pl.BlockSpec((length, 1), lambda i, w: (0, 0)), pl.BlockSpec((1, length), lambda i, w: (0, 0))],
            out_specs=[pl.BlockSpec((BLK, d), lambda i, w: (i, 0)), pl.BlockSpec((1, npair, 2 * BLK), lambda i, w: (i, 0, 0))],
            scratch_shapes=[pltpu.VMEM((length, BLK), f32)]),
        compiler_params=pltpu.CompilerParams(vmem_limit_bytes=60 << 20),
        cost_estimate=pl.CostEstimate(flops=length * d, bytes_accessed=8 * d, transcendentals=0),
        name="attend",
    )(win, q, k, v, segcol, segrow)


def bwd_kernel(allowed, npair, unroll, win_ref, q_ref, k_ref, v_ref, o_ref, do_ref, lse_ref, segcol_ref, segrow_ref,
               dr1_ref, stat_in, wq_hbm, wk_hbm, wv_hbm, grad_ref, stat_ref,
               bias_ref, p_ref, ds_ref, delta_ref, dq_ref, dk_ref, dv_ref, qsum_ref, w_ref, sem):
    i = pl.program_id(0)
    nblock = k_ref.shape[0] // BLK
    loads = [pltpu.make_async_copy(w, w_ref.at[n], sem.at[n]) for n, w in enumerate((wq_hbm, wk_hbm, wv_hbm))]

    @pl.when(i == 0)
    def _():
        for load in loads:
            load.start()
        dk_ref[...] = jnp.zeros_like(dk_ref)
        dv_ref[...] = jnp.zeros_like(dv_ref)
        stat_ref[...] = stat_in[...]
        qsum_ref[...] = jnp.zeros_like(qsum_ref)

    @pl.when(i < nblock)
    def _():
        prod = do_ref[...].astype(f32) * o_ref[...].astype(f32)
        high = prod.astype(bf16)
        low = (prod - high.astype(f32)).astype(bf16)
        head = lax.broadcasted_iota(jnp.int32, (2 * npair, npair * PAIR), 0)
        lanes = lax.broadcasted_iota(jnp.int32, (2 * npair, npair * PAIR), 1)
        pick = jnp.where(lanes // 64 == head, 1.0, 0.0).astype(bf16)
        delta_ref[...] = lax.dot_general(pick, high, DN_NT, preferred_element_type=f32) + lax.dot_general(
            pick, low, DN_NT, preferred_element_type=f32
        )

    block = jnp.minimum(i, nblock - 1)
    start = win_ref[0, block]
    variant = jnp.where(i < nblock, win_ref[1, block], -1)
    for n, size in enumerate(allowed):
        width = size * BLK

        @pl.when(variant == n)
        def _(width=width):
            fill_bias(bias_ref, segcol_ref, segrow_ref, i, start, width)
            rows = pl.ds(pl.multiple_of(start * BLK, BLK), width)

            def pair(h, u):
                cols = pl.ds(pl.multiple_of(h * PAIR, PAIR), PAIR)
                qbd = halves(q_ref[:, cols])
                dobd = halves(do_ref[:, cols])
                lse = lse_ref[0, pl.ds(h, 1), :]
                delta = jnp.concatenate([delta_ref[pl.ds(2 * h, 1), :], delta_ref[pl.ds(2 * h + 1, 1), :]], axis=1)
                for c in range(width // CH):
                    crow = pl.ds(pl.multiple_of(start * BLK + c * CH, CH), CH)
                    span = slice(c * CH, (c + 1) * CH)
                    s = lax.dot_general(k_ref[crow, cols], qbd, DN_NT, preferred_element_type=f32)
                    dp = lax.dot_general(v_ref[crow, cols], dobd, DN_NT, preferred_element_type=f32)
                    b = bias_ref[span, :]
                    p = jnp.exp(s + jnp.concatenate([b, b], axis=1) - lse)
                    p_ref[u, span, :] = p.astype(bf16)
                    ds_ref[u, span, :] = (p * (dp - delta)).astype(bf16)
                nn = (((1,), (0,)), ((), ()))
                dv_ref[rows, cols] += lax.dot_general(p_ref[u, :width, :], dobd, nn, preferred_element_type=f32)
                dk_ref[rows, cols] += lax.dot_general(ds_ref[u, :width, :], qbd, nn, preferred_element_type=f32)
                dq = lax.dot_general(ds_ref[u, :width, :], k_ref[rows, cols], DN_TN, preferred_element_type=f32)
                lane = lax.broadcasted_iota(jnp.int32, (BLK, PAIR), 1)
                dq = 0.125 * jnp.where(lane < 64, dq[:BLK], dq[BLK:])
                dq_ref[pl.ds(pl.multiple_of(i * BLK, BLK), BLK), cols] = dq.astype(bf16)
                qsum_ref[:, cols] += jnp.sum(dq.reshape(BLK // 8, 8, PAIR), axis=0)

            def body(t, c):
                for u in range(unroll):
                    pair(t * unroll + u, u)
                return c

            lax.fori_loop(0, npair // unroll, body, 0)

    @pl.when(i == nblock)
    def _():
        for load in loads:
            load.wait()
        stat_ref[0:1, :] = jnp.sum(qsum_ref[...], axis=0, keepdims=True)

    @pl.when(i >= nblock)
    def _():
        span = grad_ref.shape[0]
        rows = pl.ds(pl.multiple_of((i - nblock) * span, span), span)
        total = lax.dot_general(dq_ref[rows, :], w_ref[0], DN_NT, preferred_element_type=f32)
        total += lax.dot_general(dk_ref[rows, :].astype(bf16), w_ref[1], DN_NT, preferred_element_type=f32)
        total += lax.dot_general(dv_ref[rows, :].astype(bf16), w_ref[2], DN_NT, preferred_element_type=f32)
        grad_ref[...] = dr1_ref[...] + total


def attn_bwd(q, k, v, o, do, lse, win, segcol, segrow, dr1, stat, wq, wk, wv, allowed=ALLOWED, unroll=8, span=512):
    length, d = q.shape
    nb, npair = length // BLK, d // PAIR
    one = pl.Buffered(1)
    full = lambda: pl.BlockSpec((length, d), lambda i, w: (0, 0), pipeline_mode=one)
    row = lambda: pl.BlockSpec((BLK, d), lambda i, w: (jnp.minimum(i, nb - 1), 0))
    wide = lambda: pl.BlockSpec((span, d), lambda i, w: (jnp.maximum(i - nb, 0), 0))
    hbm = lambda: pl.BlockSpec(memory_space=pl.ANY)
    return pl.pallas_call(
        functools.partial(bwd_kernel, allowed, npair, unroll),
        out_shape=(jax.ShapeDtypeStruct((length, d), f32), jax.ShapeDtypeStruct(stat.shape, f32)),
        grid_spec=pltpu.PrefetchScalarGridSpec(
            num_scalar_prefetch=1, grid=(nb + length // span,),
            in_specs=[row(), full(), full(), row(), row(),
                      pl.BlockSpec((1, npair, 2 * BLK), lambda i, w: (jnp.minimum(i, nb - 1), 0, 0)),
                      pl.BlockSpec((length, 1), lambda i, w: (0, 0)), pl.BlockSpec((1, length), lambda i, w: (0, 0)),
                      wide(), pl.BlockSpec(stat.shape, lambda i, w: (0, 0)), hbm(), hbm(), hbm()],
            out_specs=[wide(), pl.BlockSpec(stat.shape, lambda i, w: (0, 0))],
            scratch_shapes=[pltpu.VMEM((length, BLK), f32), pltpu.VMEM((unroll, length, 2 * BLK), bf16),
                            pltpu.VMEM((unroll, length, 2 * BLK), bf16), pltpu.VMEM((2 * npair, BLK), f32),
                            pltpu.VMEM((length, d), bf16), pltpu.VMEM((length, d), f32), pltpu.VMEM((length, d), f32),
                            pltpu.VMEM((8, d), f32), pltpu.VMEM((3, d, d), bf16), pltpu.SemaphoreType.DMA((3,))]),
        compiler_params=pltpu.CompilerParams(vmem_limit_bytes=60 << 20),
        cost_estimate=pl.CostEstimate(flops=5 * length * length * d, bytes_accessed=14 * length * d, transcendentals=length * length * npair),
        name="attend_back",
    )(win, q, k, v, o, do, lse, segcol, segrow, dr1, stat, wq, wk, wv)
def dot(a, b, dims=NN):
    return lax.dot_general(a, b, dims, preferred_element_type=f32)


def gelu_both(z):
    e = jnp.exp2(z * z * -0.7213475204444817)
    t = 1.0 / (1.0 + 0.23164189 * jnp.abs(z))
    poly = t * (0.127414796 + t * (-0.142248368 + t * (0.7107068705 + t * (-0.7265760135 + t * 0.5307027145))))
    tail = poly * e
    phi = jnp.where(z >= 0, 1.0 - tail, tail)
    return z * phi, phi + z * e * 0.3989422804014327


def normed(r):
    center = r - jnp.mean(r, axis=-1, keepdims=True)
    factor = lax.rsqrt(jnp.mean(center * center, axis=-1, keepdims=True) + 1e-05)
    return center * factor, factor


def norm_back(normal, factor, dn):
    return factor * (
        dn - jnp.mean(dn, axis=-1, keepdims=True) - normal * jnp.mean(dn * normal, axis=-1, keepdims=True)
    )


def out_kernel(a_ref, x_ref, wout_ref, pm_ref, n1_ref, rs1_ref, low_ref):
    r = x_ref[...].astype(f32) + dot(a_ref[...], wout_ref[...]) + pm_ref[2:3, :]
    n1, rs1 = normed(r)
    n1_ref[...] = n1
    rs1_ref[...] = rs1
    low_ref[...] = (n1 * pm_ref[3:4, :] + pm_ref[4:5, :]).astype(bf16)


def out_norm(a, x, wout, pm, block=512):
    rows, d = x.shape
    r = lambda: pl.BlockSpec((block, d), lambda i: (i, 0))
    once = lambda s: pl.BlockSpec(s, lambda i: (0,) * len(s), pipeline_mode=pl.Buffered(1))
    return pl.pallas_call(
        out_kernel,
        out_shape=(jax.ShapeDtypeStruct((rows, d), f32), jax.ShapeDtypeStruct((rows, 1), f32),
                   jax.ShapeDtypeStruct((rows, d), bf16)),
        grid=(rows // block,),
        in_specs=[r(), r(), once((d, d)), once((8, d))],
        out_specs=[r(), pl.BlockSpec((block, 1), lambda i: (i, 0)), r()],
        compiler_params=pltpu.CompilerParams(vmem_limit_bytes=24 << 20),
        cost_estimate=pl.CostEstimate(flops=rows * d, bytes_accessed=8 * d, transcendentals=0),
        name="join",
    )(a, x, wout, pm)


def chunk_copies(plan, src, j, win_ref, wback_ref, sem):
    d, width = win_ref.shape[1:]
    piece, at, row = plan[j][0]
    moves = [
        (src[piece].at[at, pl.ds(row, width), pl.ds(g * width, width)], win_ref.at[j, pl.ds(g * width, width)])
        for g in range(d // width)
    ]
    piece, at, row = plan[j][1]
    moves.append((src[piece].at[at, pl.ds(row, width + 16)], wback_ref.at[j]))
    return [pltpu.make_async_copy(s, t, sem.at[n, j]) for n, (s, t) in enumerate(moves)]


def wait_chunk(plan, src, j, win_ref, wback_ref, sem):
    for n in range(len(plan)):

        @pl.when(j == n)
        def _(n=n):
            for copy in chunk_copies(plan, src, n, win_ref, wback_ref, sem):
                copy.wait()


def up_kernel(plan, nsrc, span, *refs):
    low_ref, refs = refs[0], refs[1:]
    src = refs[:nsrc]
    sum_ref, slope_ref, win_ref, wback_ref, sem = refs[nsrc:]
    j = pl.program_id(0)
    width = win_ref.shape[2]
    rows_all = low_ref.shape[0]

    @pl.when(j == 0)
    def _():
        sum_ref[...] = jnp.zeros_like(sum_ref)

    for n in range(len(plan)):

        @pl.when(j == max(n - 2, 0))
        def _(n=n):
            for copy in chunk_copies(plan, src, n, win_ref, wback_ref, sem):
                copy.start()

    wait_chunk(plan, src, j, win_ref, wback_ref, sem)
    parts = wback_ref[j, width : width + 16, :width].astype(f32)
    bias = parts[0:1] + parts[1:2] + parts[2:3]
    def up(r, t):
        rows = pl.ds(pl.multiple_of(r * span, span), span)
        u, slope = gelu_both(dot(low_ref[rows, :], win_ref[j]) + bias)
        slope_ref[0, rows, :] = slope.astype(bf16)
        sum_ref[rows, :] += dot(u.astype(bf16), wback_ref[j, :width, :])
        return t

    lax.fori_loop(0, rows_all // span, up, 0)


def feed_up(low, src, plan, width, span=512):
    rows, d = low.shape
    n = len(plan)
    once = lambda: pl.BlockSpec((rows, d), lambda j: (0, 0), pipeline_mode=pl.Buffered(1))
    return pl.pallas_call(
        functools.partial(up_kernel, plan, len(src), min(span, rows)),
        out_shape=(jax.ShapeDtypeStruct((rows, d), f32), jax.ShapeDtypeStruct((n, rows, width), bf16)),
        grid=(n,),
        in_specs=[once()] + [pl.BlockSpec(memory_space=pl.ANY) for _ in src],
        out_specs=[pl.BlockSpec((rows, d), lambda j: (0, 0)), pl.BlockSpec((1, rows, width), lambda j: (j, 0, 0))],
        scratch_shapes=[pltpu.VMEM((n, d, width), bf16), pltpu.VMEM((n, width + 16, d), bf16),
                        pltpu.SemaphoreType.DMA((d // width + 1, n))],
        compiler_params=pltpu.CompilerParams(vmem_limit_bytes=44 << 20 if n < 8 else 60 << 20),
        cost_estimate=pl.CostEstimate(flops=rows * d, bytes_accessed=8 * d, transcendentals=0),
        name="feed_up",
    )(low, *src)


def down_kernel(plan, nsrc, nfar, nr, span, me_ref, *refs):
    low_in, n1_in, f_in, rs1_ref, cot_ref, pad_ref, wout_ref, pm_ref = refs[:8]
    src = refs[8 : 8 + nsrc]
    slope_src = refs[8 + nsrc]
    (act_ref, dr1_ref, da_ref, stat_ref,
     win_ref, wback_ref, sem, slope_ref, slope_sem, low_ref, sum_ref, n1_ref, row_sem) = refs[9 + nsrc :]
    i = pl.program_id(0)
    nchunk, _, width = win_ref.shape
    block = act_ref.shape[0]
    rows_all = low_ref.shape[0]
    get_low = pltpu.make_async_copy(low_in, low_ref, row_sem.at[0])
    get_f = pltpu.make_async_copy(f_in, sum_ref, row_sem.at[1])
    get_n1 = pltpu.make_async_copy(n1_in, n1_ref, row_sem.at[2])

    def copies(j):
        moves = chunk_copies(plan, src, j, win_ref, wback_ref, sem)
        if j >= nfar:
            moves.append(pltpu.make_async_copy(slope_src.at[j - nfar], slope_ref.at[j], slope_sem.at[j]))
        return moves

    def start(j):
        for copy in copies(j):
            copy.start()

    def wait(j):
        for copy in copies(j):
            copy.wait()

    @pl.when(i == 0)
    def _():
        get_low.start()
        for j in range(nfar):
            start(j)
        get_f.start()
        get_n1.start()
        stat_ref[...] = jnp.zeros_like(stat_ref)
        get_low.wait()
        if not nfar:
            get_f.wait()

    for j in range(nfar, nchunk):

        @pl.when(i == 1 + (j - nfar) // 2)
        def _(j=j):
            start(j)

    row = lambda n: pm_ref[n : n + 1, :]

    def add_stat(n, v):
        stat_ref[n : n + 1, :] += jnp.sum(v, axis=0, keepdims=True)

    for j in range(nfar):

        @pl.when(i == j)
        def _(j=j):
            wait(j)
            if j == 0:
                get_f.wait()

    @pl.when(i < nfar)
    def _():
        parts = wback_ref[i, width : width + 16, :width].astype(f32)
        bias = parts[0:1] + parts[1:2] + parts[2:3]

        def up(r, t):
            rows = pl.ds(pl.multiple_of(r * block, block), block)
            u, slope = gelu_both(dot(low_ref[rows, :], win_ref[i]) + bias)
            slope_ref[i, rows, :] = slope.astype(bf16)
            sum_ref[rows, :] += dot(u.astype(bf16), wback_ref[i, :width, :])
            return t

        lax.fori_loop(0, rows_all // block, up, 0)

    @pl.when(i == nfar)
    def _():
        get_n1.wait()

    @pl.when((i >= nfar) & (i < nfar + nr))
    def _():
        rows = pl.ds(pl.multiple_of((i - nfar) * block, block), block)
        h1 = n1_ref[rows, :] * row(3) + row(4)
        n2, rs2 = normed(h1 + (sum_ref[rows, :] + row(5)))
        act_ref[...] = n2 * row(6) + row(7)
        dy = cot_ref[...].astype(f32) * jnp.where(pad_ref[...] >= 0, 1.0, 0.0)
        add_stat(6, dy * n2)
        add_stat(7, dy)
        dr2 = norm_back(n2, rs2, dy * row(6))
        add_stat(5, dr2)
        sum_ref[rows, :] = dr2
        low_ref[rows, :] = dr2.astype(bf16)

    last = nfar + nr + nchunk

    @pl.when((i >= nfar + nr) & (i < last))
    def _():
        j = i - nfar - nr
        for n in range(nfar, nchunk):

            @pl.when(j == n)
            def _(n=n):
                wait(n)

        owner = lax.rem(j + nchunk - nfar, nchunk) ^ me_ref[0]
        each = low_ref.shape[1] // width
        place = (pl.ds(8 + owner // each, 1), pl.ds(pl.multiple_of(lax.rem(owner, each) * width, width), width))
        for r in range(rows_all // span):
            rows = slice(r * span, (r + 1) * span)
            dz = dot(low_ref[rows, :], wback_ref[j, :width, :], NT) * slope_ref[j, rows, :].astype(f32)
            grad = jnp.sum(dz, axis=0, keepdims=True)
            if nfar:
                stat_ref[place] += grad
            else:
                for n in range(nchunk):

                    @pl.when(j == n)
                    def _(n=n, grad=grad):
                        stat_ref[8 + n // each : 9 + n // each, n % each * width : (n % each + 1) * width] += grad

            sum_ref[rows, :] += dot(dz.astype(bf16), win_ref[j], NT)

    @pl.when(i >= last)
    def _():
        rows = pl.ds(pl.multiple_of((i - last) * block, block), block)
        n1 = n1_ref[rows, :]
        dh1 = sum_ref[rows, :]
        add_stat(3, dh1 * n1)
        add_stat(4, dh1)
        dr1 = norm_back(n1, rs1_ref[rows, :], dh1 * row(3))
        add_stat(2, dr1)
        dr1_ref[...] = dr1
        da = dot(dr1.astype(bf16), wout_ref[...], NT).astype(bf16)
        da_ref[...] = da
        add_stat(1, da.astype(f32))


def feed_down(me, low, n1, f, rs1, cot, padcol, wout, pm, src, plan, slopes, nfar, width, block=512, span=512):
    rows, d = low.shape
    nchunk = len(plan)
    block, span = min(block, rows), min(span, rows)
    nr = rows // block
    last = nfar + nr + nchunk
    once = lambda s: pl.BlockSpec(s, lambda i, me: (0,) * len(s), pipeline_mode=pl.Buffered(1))
    early = lambda w: pl.BlockSpec((block, w), lambda i, me: (jnp.clip(i - nfar, 0, nr - 1), 0))
    late = lambda: pl.BlockSpec((block, d), lambda i, me: (jnp.maximum(i - last, 0), 0))
    hbm = lambda: pl.BlockSpec(memory_space=pl.ANY)
    return pl.pallas_call(
        functools.partial(down_kernel, plan, len(src), nfar, nr, span),
        out_shape=(jax.ShapeDtypeStruct((rows, d), f32), jax.ShapeDtypeStruct((rows, d), f32),
                   jax.ShapeDtypeStruct((rows, d), bf16), jax.ShapeDtypeStruct((8 + nchunk * width // d, d), f32)),
        grid_spec=pltpu.PrefetchScalarGridSpec(
        num_scalar_prefetch=1,
        grid=(last + nr,),
        in_specs=[hbm(), hbm(), hbm(), once((rows, 1)), early(d), early(1), once((d, d)), once((8, d))]
        + [hbm() for _ in src] + [hbm()],
        out_specs=[early(d), late(), late(), pl.BlockSpec((8 + nchunk * width // d, d), lambda i, me: (0, 0))],
        scratch_shapes=[pltpu.VMEM((nchunk, d, width), bf16), pltpu.VMEM((nchunk, width + 16, d), bf16),
                        pltpu.SemaphoreType.DMA((d // width + 1, nchunk)), pltpu.VMEM((nchunk, rows, width), bf16),
                        pltpu.SemaphoreType.DMA((nchunk,)), pltpu.VMEM((rows, d), bf16), pltpu.VMEM((rows, d), f32),
                        pltpu.VMEM((rows, d), f32), pltpu.SemaphoreType.DMA((3,))]),
        compiler_params=pltpu.CompilerParams(vmem_limit_bytes=57 << 20 if nfar else 62 << 20),
        cost_estimate=pl.CostEstimate(flops=rows * d, bytes_accessed=8 * d, transcendentals=0),
        name="feed_down",
    )(me, low, n1, f, rs1, cot, padcol, wout, pm, *src, slopes)


def adam_step(grad, first, second, param, average):
    first_new = 0.5 * first + 0.5 * grad
    second_new = 0.5 * second + 0.5 * grad * grad
    corr = 1.0 - 0.5**STEP
    param_new = param - 0.25 * (
        first_new / corr / (jnp.sqrt(second_new / corr) + 1e-08) + 0.01 * param
    )
    return (
        first_new,
        second_new,
        param_new,
        param_new.astype(jnp.bfloat16),
        0.8 * average + 0.2 * param_new,
    )


def exchange(v, axis, bit):
    size = lax.axis_size(axis)
    return lax.ppermute(v, axis, [(i, i ^ bit) for i in range(size)])


def bits(size):
    return [1 << b for b in range(size.bit_length() - 1)]


def total_sum(v):
    if lax.axis_size("mp") == 8 and lax.axis_size("dp") == 4:
        v = v + exchange(v, "mp", 1)
        v = (v + exchange(v, "mp", 2)) + (exchange(v, "mp", 4) + exchange(v, "mp", 6))
        return (v + exchange(v, "dp", 1)) + (exchange(v, "dp", 2) + exchange(v, "dp", 3))
    for axis in ("mp", "dp"):
        for bit in bits(lax.axis_size(axis)):
            v = v + exchange(v, axis, bit)
    return v


def on_device(
    tokens,
    segment_ids,
    pad_mask,
    cotangent,
    w_query,
    w_key,
    w_value,
    w_out,
    w_in,
    w_back,
    params_main,
    params_hidden,
    first_main,
    second_main,
    first_hidden,
    second_hidden,
    average_main,
    average_hidden,
):
    rows_all, d = tokens.shape
    width = params_hidden.shape[0]
    devices = lax.axis_size("mp")
    me = lax.axis_index("mp")
    total_hidden = width * devices
    seg, pad = segment_ids[0], pad_mask[0]

    rounded = lambda v: lax.reduce_precision(v, 8, 7)
    high = rounded(params_hidden)
    middle = rounded(params_hidden - high)
    rows = jnp.stack([high, middle, rounded(params_hidden - high - middle)]).astype(bf16)
    packed = jnp.concatenate([w_in[g * width : (g + 1) * width] for g in range(d // width)], axis=1)
    own = jnp.concatenate([packed, w_back, jnp.pad(rows, ((0, 13), (0, d - width)))], axis=0)
    cube = devices == 8
    hop = lambda v, bit: exchange(v, "mp", bit)
    core, along_x, along_y = 1, 2, 4
    if cube:
        by_x, by_y, by_core = hop(own, along_x), hop(own, along_y), hop(own, core)

    win = windows(seg, BLK, ALLOWED)
    segcol = jnp.where(pad == 1, seg, -1)[:, None]
    segrow = seg[None, :]
    query = (0.125 * (dot(tokens, w_query) + params_main[0])).astype(bf16)
    keys = dot(tokens, w_key).astype(bf16)
    values = (dot(tokens, w_value) + params_main[1]).astype(bf16)
    mixed, lse = attn_fwd(query, keys, values, win, segcol, segrow, (0, d // PAIR))
    if cube:
        by_x, by_y, by_core, mixed = lax.optimization_barrier((by_x, by_y, by_core, mixed))
        far_in, far_back = hop(by_y[:width], along_x), hop(by_x[width:], along_y)
        near = [own, by_core, by_x, hop(by_x, core), by_y, hop(by_y, core)]
        normal_one, factor_one, low = out_norm(mixed, tokens, w_out, params_main)
        plan = tuple(((n, 0, 0), (n, 0, width)) for n in range(6))
        first = [p[None] for p in near]
        partial, slopes = feed_up(low, first, plan, width)
        far_in, far_back, partial = lax.optimization_barrier((far_in, far_back, partial))
        rest = [p[None] for p in (far_in, far_back, hop(far_in, core), hop(far_back, core))]
        far_plan = (((0, 0, 0), (1, 0, 0)), ((2, 0, 0), (3, 0, 0)))
        sources = first + rest
        plan = tuple(((6 + n[0],) + n[1:], (6 + m[0],) + m[1:]) for n, m in far_plan) + plan
        far, order = 2, me
    else:
        sources = [lax.all_gather(own, "mp", axis=0)]
        plan = tuple(((0, j, 0), (0, j, width)) for j in range(devices))
        normal_one, factor_one, low = out_norm(mixed, tokens, w_out, params_main)
        partial, slopes = feed_up(low, sources, plan, width)
        far, order = 0, jnp.zeros_like(me)
    activations, dresid_one, dmixed, stats = feed_down(
        order[None].astype(jnp.int32), low, normal_one, partial, factor_one, cotangent, segcol, w_out, params_main, sources, plan, slopes, far, width
    )
    input_grad, local = attn_bwd(
        query, keys, values, mixed, dmixed, lse, win, segcol, segrow, dresid_one, stats, w_query, w_key, w_value
    )
    total = total_sum(local)
    grad_norm = jnp.sqrt(jnp.sum(total * total))
    grad_main = total[:8]
    grad_hid = lax.dynamic_slice_in_dim(total[8:].reshape(total_hidden), me * width, width, 0)
    tokens_all = rows_all * lax.axis_size("dp") * devices
    limit = 0.01 * math.sqrt(tokens_all * (8 * d + total_hidden))
    scale_factor = jnp.minimum(1.0, limit / (grad_norm + 1e-06))
    grad_main = grad_main * scale_factor
    grad_hid = grad_hid * scale_factor
    fm, sm, pm, cm, am = adam_step(grad_main, first_main, second_main, params_main, average_main)
    fh, sh, ph, ch, ah = adam_step(grad_hid, first_hidden, second_hidden, params_hidden, average_hidden)
    return (
        activations,
        input_grad,
        grad_norm,
        grad_main,
        grad_hid,
        fm,
        sm,
        fh,
        sh,
        pm,
        ph,
        cm,
        ch,
        am,
        ah,
    )


def solution(mesh):
    placed = (
        P(("dp", "mp"), None),
        P(("dp", "mp"), None),
        P(("dp", "mp"), None),
        P(("dp", "mp"), None),
        P(),
        P(),
        P(),
        P(),
        P(None, "mp"),
        P("mp", None),
        P(),
        P("mp"),
        P(),
        P(),
        P("mp"),
        P("mp"),
        P(),
        P("mp"),
    )
    return jax.shard_map(
        on_device,
        mesh=mesh,
        in_specs=placed,
        out_specs=(
            P(("dp", "mp"), None),
            P(("dp", "mp"), None),
            P(),
            P(),
            P("mp"),
            P(),
            P(),
            P("mp"),
            P("mp"),
            P(),
            P("mp"),
            P(),
            P("mp"),
            P(),
            P("mp"),
        ),
        check_vma=False,
    )
```

```python
import functools
import math

import jax
import jax.numpy as jnp
from jax import lax
from jax.experimental import pallas as pl
from jax.experimental.pallas import tpu as pltpu
from jax.sharding import PartitionSpec as P

STEP = 5
f32, bf16 = jnp.float32, jnp.bfloat16
NN = (((1,), (0,)), ((), ()))
NT = (((1,), (1,)), ((), ()))
DN_NT = NT
DN_TN = (((0,), (0,)), ((), ()))

BLK = 128
PAIR = 128
CH = 128
NEG = -1e9
ALLOWED = (2, 3, 4, 5, 6, 8)


def windows(seg_row, blk, allowed):
    length = seg_row.shape[0]
    nb = length // blk
    first = seg_row[::blk]
    last = seg_row[blk - 1 :: blk]
    lo = jnp.sum(seg_row[None, :] < first[:, None], axis=1)
    hi = jnp.sum(seg_row[None, :] <= last[:, None], axis=1)
    start = lo // blk
    count = (hi + blk - 1) // blk - start
    variant = jnp.zeros_like(count)
    size = jnp.full_like(count, allowed[0])
    for small, large in zip(allowed, allowed[1:]):
        over = (count > small).astype(count.dtype)
        variant = variant + over
        size = size + over * (large - small)
    start = jnp.minimum(start, nb - size)
    return jnp.stack([start, variant]).astype(jnp.int32)


def halves(x):
    lane = lax.broadcasted_iota(jnp.int32, x.shape, 1)
    zero = jnp.zeros_like(x)
    return jnp.concatenate([jnp.where(lane < 64, x, zero), jnp.where(lane >= 64, x, zero)], axis=0)


def fill_bias(bias_ref, segcol_ref, segrow_ref, i, start, width):
    rows = pl.ds(start * BLK, width)
    kcode = segcol_ref[rows, :]
    qseg = segrow_ref[:, pl.ds(pl.multiple_of(i * BLK, BLK), BLK)]
    kpos = start * BLK + lax.broadcasted_iota(jnp.int32, (width, BLK), 0)
    qpos = i * BLK + lax.broadcasted_iota(jnp.int32, (width, BLK), 1)
    vis = (kcode == qseg) | (kpos == qpos)
    bias_ref[pl.ds(0, width), :] = jnp.where(vis, 0.0, NEG).astype(f32)


def fwd_kernel(allowed, npair, unroll, win_ref, q_ref, k_ref, v_ref, segcol_ref, segrow_ref, o_ref, lse_ref, bias_ref):
    i = pl.program_id(0)
    start = win_ref[0, i]
    variant = win_ref[1, i]
    for n, size in enumerate(allowed):
        width = size * BLK

        @pl.when(variant == n)
        def _(width=width):
            fill_bias(bias_ref, segcol_ref, segrow_ref, i, start, width)
            rows = pl.ds(pl.multiple_of(start * BLK, BLK), width)

            def pair(h):
                cols = pl.ds(pl.multiple_of(h * PAIR, PAIR), PAIR)
                qbd = halves(q_ref[:, cols])
                s = lax.dot_general(k_ref[rows, cols], qbd, DN_NT, preferred_element_type=f32)
                b = bias_ref[pl.ds(0, width), :]
                s = s + jnp.concatenate([b, b], axis=1)
                top = jnp.max(s, axis=0, keepdims=True)
                p = jnp.exp(s - top)
                tot = jnp.sum(p, axis=0, keepdims=True)
                o = lax.dot_general(p.astype(bf16), v_ref[rows, cols], DN_TN, preferred_element_type=f32)
                inv = jnp.broadcast_to(1.0 / tot, (8, 2 * BLK)).T[:, :1]
                o = o * inv
                lane = lax.broadcasted_iota(jnp.int32, (BLK, PAIR), 1)
                o_ref[:, cols] = jnp.where(lane < 64, o[:BLK], o[BLK:]).astype(bf16)
                lse_ref[0, pl.ds(h, 1), :] = top + jnp.log(tot)

            def body(t, c):
                for u in range(unroll):
                    pair(t * unroll + u)
                return c

            lax.fori_loop(0, npair // unroll, body, 0)


def attn_fwd(q, k, v, win, segcol, segrow, pairs, allowed=ALLOWED, unroll=8):
    length = q.shape[0]
    npair = pairs[1] - pairs[0]
    d, part = npair * PAIR, pairs[0] // npair
    nb = length // BLK
    unroll = min(unroll, npair)
    full = lambda: pl.BlockSpec((length, d), lambda i, w: (0, part))
    return pl.pallas_call(
        functools.partial(fwd_kernel, allowed, npair, unroll),
        out_shape=(jax.ShapeDtypeStruct((length, d), bf16), jax.ShapeDtypeStruct((nb, npair, 2 * BLK), f32)),
        grid_spec=pltpu.PrefetchScalarGridSpec(
            num_scalar_prefetch=1, grid=(nb,),
            in_specs=[pl.BlockSpec((BLK, d), lambda i, w: (i, part)), full(), full(),
                      pl.BlockSpec((length, 1), lambda i, w: (0, 0)), pl.BlockSpec((1, length), lambda i, w: (0, 0))],
            out_specs=[pl.BlockSpec((BLK, d), lambda i, w: (i, 0)), pl.BlockSpec((1, npair, 2 * BLK), lambda i, w: (i, 0, 0))],
            scratch_shapes=[pltpu.VMEM((length, BLK), f32)]),
        compiler_params=pltpu.CompilerParams(vmem_limit_bytes=60 << 20),
        cost_estimate=pl.CostEstimate(flops=length * d, bytes_accessed=8 * d, transcendentals=0),
        name="attend",
    )(win, q, k, v, segcol, segrow)


def bwd_kernel(allowed, npair, unroll, win_ref, q_ref, k_ref, v_ref, o_ref, do_ref, lse_ref, segcol_ref, segrow_ref,
               dr1_ref, stat_in, wq_hbm, wk_hbm, wv_hbm, grad_ref, stat_ref,
               bias_ref, p_ref, ds_ref, delta_ref, dq_ref, dk_ref, dv_ref, qsum_ref, w_ref, sem):
    i = pl.program_id(0)
    nblock = k_ref.shape[0] // BLK
    loads = [pltpu.make_async_copy(w, w_ref.at[n], sem.at[n]) for n, w in enumerate((wq_hbm, wk_hbm, wv_hbm))]

    @pl.when(i == 0)
    def _():
        for load in loads:
            load.start()
        dk_ref[...] = jnp.zeros_like(dk_ref)
        dv_ref[...] = jnp.zeros_like(dv_ref)
        stat_ref[...] = stat_in[...]
        qsum_ref[...] = jnp.zeros_like(qsum_ref)

    @pl.when(i < nblock)
    def _():
        prod = do_ref[...].astype(f32) * o_ref[...].astype(f32)
        high = prod.astype(bf16)
        low = (prod - high.astype(f32)).astype(bf16)
        head = lax.broadcasted_iota(jnp.int32, (2 * npair, npair * PAIR), 0)
        lanes = lax.broadcasted_iota(jnp.int32, (2 * npair, npair * PAIR), 1)
        pick = jnp.where(lanes // 64 == head, 1.0, 0.0).astype(bf16)
        delta_ref[...] = lax.dot_general(pick, high, DN_NT, preferred_element_type=f32) + lax.dot_general(
            pick, low, DN_NT, preferred_element_type=f32
        )

    block = jnp.minimum(i, nblock - 1)
    start = win_ref[0, block]
    variant = jnp.where(i < nblock, win_ref[1, block], -1)
    for n, size in enumerate(allowed):
        width = size * BLK

        @pl.when(variant == n)
        def _(width=width):
            fill_bias(bias_ref, segcol_ref, segrow_ref, i, start, width)
            rows = pl.ds(pl.multiple_of(start * BLK, BLK), width)

            def pair(h, u):
                cols = pl.ds(pl.multiple_of(h * PAIR, PAIR), PAIR)
                qbd = halves(q_ref[:, cols])
                dobd = halves(do_ref[:, cols])
                lse = lse_ref[0, pl.ds(h, 1), :]
                delta = jnp.concatenate([delta_ref[pl.ds(2 * h, 1), :], delta_ref[pl.ds(2 * h + 1, 1), :]], axis=1)
                for c in range(width // CH):
                    crow = pl.ds(pl.multiple_of(start * BLK + c * CH, CH), CH)
                    span = slice(c * CH, (c + 1) * CH)
                    s = lax.dot_general(k_ref[crow, cols], qbd, DN_NT, preferred_element_type=f32)
                    dp = lax.dot_general(v_ref[crow, cols], dobd, DN_NT, preferred_element_type=f32)
                    b = bias_ref[span, :]
                    p = jnp.exp(s + jnp.concatenate([b, b], axis=1) - lse)
                    p_ref[u, span, :] = p.astype(bf16)
                    ds_ref[u, span, :] = (p * (dp - delta)).astype(bf16)
                nn = (((1,), (0,)), ((), ()))
                dv_ref[rows, cols] += lax.dot_general(p_ref[u, :width, :], dobd, nn, preferred_element_type=f32)
                dk_ref[rows, cols] += lax.dot_general(ds_ref[u, :width, :], qbd, nn, preferred_element_type=f32)
                dq = lax.dot_general(ds_ref[u, :width, :], k_ref[rows, cols], DN_TN, preferred_element_type=f32)
                lane = lax.broadcasted_iota(jnp.int32, (BLK, PAIR), 1)
                dq = 0.125 * jnp.where(lane < 64, dq[:BLK], dq[BLK:])
                dq_ref[pl.ds(pl.multiple_of(i * BLK, BLK), BLK), cols] = dq.astype(bf16)
                qsum_ref[:, cols] += jnp.sum(dq.reshape(BLK // 8, 8, PAIR), axis=0)

            def body(t, c):
                for u in range(unroll):
                    pair(t * unroll + u, u)
                return c

            lax.fori_loop(0, npair // unroll, body, 0)

    @pl.when(i == nblock)
    def _():
        for load in loads:
            load.wait()
        stat_ref[0:1, :] = jnp.sum(qsum_ref[...], axis=0, keepdims=True)

    @pl.when(i >= nblock)
    def _():
        span = grad_ref.shape[0]
        rows = pl.ds(pl.multiple_of((i - nblock) * span, span), span)
        total = lax.dot_general(dq_ref[rows, :], w_ref[0], DN_NT, preferred_element_type=f32)
        total += lax.dot_general(dk_ref[rows, :].astype(bf16), w_ref[1], DN_NT, preferred_element_type=f32)
        total += lax.dot_general(dv_ref[rows, :].astype(bf16), w_ref[2], DN_NT, preferred_element_type=f32)
        grad_ref[...] = dr1_ref[...] + total


def attn_bwd(q, k, v, o, do, lse, win, segcol, segrow, dr1, stat, wq, wk, wv, allowed=ALLOWED, unroll=8, span=512):
    length, d = q.shape
    nb, npair = length // BLK, d // PAIR
    one = pl.Buffered(1)
    full = lambda: pl.BlockSpec((length, d), lambda i, w: (0, 0), pipeline_mode=one)
    row = lambda: pl.BlockSpec((BLK, d), lambda i, w: (jnp.minimum(i, nb - 1), 0))
    wide = lambda: pl.BlockSpec((span, d), lambda i, w: (jnp.maximum(i - nb, 0), 0))
    hbm = lambda: pl.BlockSpec(memory_space=pl.ANY)
    return pl.pallas_call(
        functools.partial(bwd_kernel, allowed, npair, unroll),
        out_shape=(jax.ShapeDtypeStruct((length, d), f32), jax.ShapeDtypeStruct(stat.shape, f32)),
        grid_spec=pltpu.PrefetchScalarGridSpec(
            num_scalar_prefetch=1, grid=(nb + length // span,),
            in_specs=[row(), full(), full(), row(), row(),
                      pl.BlockSpec((1, npair, 2 * BLK), lambda i, w: (jnp.minimum(i, nb - 1), 0, 0)),
                      pl.BlockSpec((length, 1), lambda i, w: (0, 0)), pl.BlockSpec((1, length), lambda i, w: (0, 0)),
                      wide(), pl.BlockSpec(stat.shape, lambda i, w: (0, 0)), hbm(), hbm(), hbm()],
            out_specs=[wide(), pl.BlockSpec(stat.shape, lambda i, w: (0, 0))],
            scratch_shapes=[pltpu.VMEM((length, BLK), f32), pltpu.VMEM((unroll, length, 2 * BLK), bf16),
                            pltpu.VMEM((unroll, length, 2 * BLK), bf16), pltpu.VMEM((2 * npair, BLK), f32),
                            pltpu.VMEM((length, d), bf16), pltpu.VMEM((length, d), f32), pltpu.VMEM((length, d), f32),
                            pltpu.VMEM((8, d), f32), pltpu.VMEM((3, d, d), bf16), pltpu.SemaphoreType.DMA((3,))]),
        compiler_params=pltpu.CompilerParams(vmem_limit_bytes=60 << 20),
        cost_estimate=pl.CostEstimate(flops=5 * length * length * d, bytes_accessed=14 * length * d, transcendentals=length * length * npair),
        name="attend_back",
    )(win, q, k, v, o, do, lse, segcol, segrow, dr1, stat, wq, wk, wv)
def dot(a, b, dims=NN):
    return lax.dot_general(a, b, dims, preferred_element_type=f32)


def gelu_both(z):
    e = jnp.exp2(z * z * -0.7213475204444817)
    t = 1.0 / (1.0 + 0.23164189 * jnp.abs(z))
    poly = t * (0.127414796 + t * (-0.142248368 + t * (0.7107068705 + t * (-0.7265760135 + t * 0.5307027145))))
    tail = poly * e
    phi = jnp.where(z >= 0, 1.0 - tail, tail)
    return z * phi, phi + z * e * 0.3989422804014327


def normed(r):
    center = r - jnp.mean(r, axis=-1, keepdims=True)
    factor = lax.rsqrt(jnp.mean(center * center, axis=-1, keepdims=True) + 1e-05)
    return center * factor, factor


def norm_back(normal, factor, dn):
    return factor * (
        dn - jnp.mean(dn, axis=-1, keepdims=True) - normal * jnp.mean(dn * normal, axis=-1, keepdims=True)
    )


def out_kernel(a_ref, x_ref, wout_ref, pm_ref, n1_ref, rs1_ref, low_ref):
    r = x_ref[...].astype(f32) + dot(a_ref[...], wout_ref[...]) + pm_ref[2:3, :]
    n1, rs1 = normed(r)
    n1_ref[...] = n1
    rs1_ref[...] = rs1
    low_ref[...] = (n1 * pm_ref[3:4, :] + pm_ref[4:5, :]).astype(bf16)


def out_norm(a, x, wout, pm, block=512):
    rows, d = x.shape
    r = lambda: pl.BlockSpec((block, d), lambda i: (i, 0))
    once = lambda s: pl.BlockSpec(s, lambda i: (0,) * len(s), pipeline_mode=pl.Buffered(1))
    return pl.pallas_call(
        out_kernel,
        out_shape=(jax.ShapeDtypeStruct((rows, d), f32), jax.ShapeDtypeStruct((rows, 1), f32),
                   jax.ShapeDtypeStruct((rows, d), bf16)),
        grid=(rows // block,),
        in_specs=[r(), r(), once((d, d)), once((8, d))],
        out_specs=[r(), pl.BlockSpec((block, 1), lambda i: (i, 0)), r()],
        compiler_params=pltpu.CompilerParams(vmem_limit_bytes=24 << 20),
        cost_estimate=pl.CostEstimate(flops=rows * d, bytes_accessed=8 * d, transcendentals=0),
        name="join",
    )(a, x, wout, pm)


def chunk_copies(plan, src, j, win_ref, wback_ref, sem):
    d, width = win_ref.shape[1:]
    piece, at, row = plan[j][0]
    moves = [
        (src[piece].at[at, pl.ds(row, width), pl.ds(g * width, width)], win_ref.at[j, pl.ds(g * width, width)])
        for g in range(d // width)
    ]
    piece, at, row = plan[j][1]
    moves.append((src[piece].at[at, pl.ds(row, width + 16)], wback_ref.at[j]))
    return [pltpu.make_async_copy(s, t, sem.at[n, j]) for n, (s, t) in enumerate(moves)]


def wait_chunk(plan, src, j, win_ref, wback_ref, sem):
    for n in range(len(plan)):

        @pl.when(j == n)
        def _(n=n):
            for copy in chunk_copies(plan, src, n, win_ref, wback_ref, sem):
                copy.wait()


def up_kernel(plan, nsrc, span, *refs):
    low_ref, refs = refs[0], refs[1:]
    src = refs[:nsrc]
    sum_ref, slope_ref, win_ref, wback_ref, sem = refs[nsrc:]
    j = pl.program_id(0)
    width = win_ref.shape[2]
    rows_all = low_ref.shape[0]

    @pl.when(j == 0)
    def _():
        sum_ref[...] = jnp.zeros_like(sum_ref)

    for n in range(len(plan)):

        @pl.when(j == max(n - 2, 0))
        def _(n=n):
            for copy in chunk_copies(plan, src, n, win_ref, wback_ref, sem):
                copy.start()

    wait_chunk(plan, src, j, win_ref, wback_ref, sem)
    parts = wback_ref[j, width : width + 16, :width].astype(f32)
    bias = parts[0:1] + parts[1:2] + parts[2:3]
    def up(r, t):
        rows = pl.ds(pl.multiple_of(r * span, span), span)
        u, slope = gelu_both(dot(low_ref[rows, :], win_ref[j]) + bias)
        slope_ref[0, rows, :] = slope.astype(bf16)
        sum_ref[rows, :] += dot(u.astype(bf16), wback_ref[j, :width, :])
        return t

    lax.fori_loop(0, rows_all // span, up, 0)


def feed_up(low, src, plan, width, span=512):
    rows, d = low.shape
    n = len(plan)
    once = lambda: pl.BlockSpec((rows, d), lambda j: (0, 0), pipeline_mode=pl.Buffered(1))
    return pl.pallas_call(
        functools.partial(up_kernel, plan, len(src), min(span, rows)),
        out_shape=(jax.ShapeDtypeStruct((rows, d), f32), jax.ShapeDtypeStruct((n, rows, width), bf16)),
        grid=(n,),
        in_specs=[once()] + [pl.BlockSpec(memory_space=pl.ANY) for _ in src],
        out_specs=[pl.BlockSpec((rows, d), lambda j: (0, 0)), pl.BlockSpec((1, rows, width), lambda j: (j, 0, 0))],
        scratch_shapes=[pltpu.VMEM((n, d, width), bf16), pltpu.VMEM((n, width + 16, d), bf16),
                        pltpu.SemaphoreType.DMA((d // width + 1, n))],
        compiler_params=pltpu.CompilerParams(vmem_limit_bytes=44 << 20 if n < 8 else 60 << 20),
        cost_estimate=pl.CostEstimate(flops=rows * d, bytes_accessed=8 * d, transcendentals=0),
        name="feed_up",
    )(low, *src)


def down_kernel(plan, nsrc, nfar, nr, span, me_ref, *refs):
    low_in, n1_in, f_in, rs1_ref, cot_ref, pad_ref, wout_ref, pm_ref = refs[:8]
    src = refs[8 : 8 + nsrc]
    slope_src = refs[8 + nsrc]
    (act_ref, dr1_ref, da_ref, stat_ref,
     win_ref, wback_ref, sem, slope_ref, slope_sem, low_ref, sum_ref, n1_ref, row_sem) = refs[9 + nsrc :]
    i = pl.program_id(0)
    nchunk, _, width = win_ref.shape
    block = act_ref.shape[0]
    rows_all = low_ref.shape[0]
    get_low = pltpu.make_async_copy(low_in, low_ref, row_sem.at[0])
    get_f = pltpu.make_async_copy(f_in, sum_ref, row_sem.at[1])
    get_n1 = pltpu.make_async_copy(n1_in, n1_ref, row_sem.at[2])

    def copies(j):
        moves = chunk_copies(plan, src, j, win_ref, wback_ref, sem)
        if j >= nfar:
            moves.append(pltpu.make_async_copy(slope_src.at[j - nfar], slope_ref.at[j], slope_sem.at[j]))
        return moves

    def start(j):
        for copy in copies(j):
            copy.start()

    def wait(j):
        for copy in copies(j):
            copy.wait()

    @pl.when(i == 0)
    def _():
        get_low.start()
        for j in range(nfar):
            start(j)
        get_f.start()
        get_n1.start()
        stat_ref[...] = jnp.zeros_like(stat_ref)
        get_low.wait()
        if not nfar:
            get_f.wait()

    for j in range(nfar, nchunk):

        @pl.when(i == 1 + (j - nfar) // 2)
        def _(j=j):
            start(j)

    row = lambda n: pm_ref[n : n + 1, :]

    def add_stat(n, v):
        stat_ref[n : n + 1, :] += jnp.sum(v, axis=0, keepdims=True)

    for j in range(nfar):

        @pl.when(i == j)
        def _(j=j):
            wait(j)
            if j == 0:
                get_f.wait()

    @pl.when(i < nfar)
    def _():
        parts = wback_ref[i, width : width + 16, :width].astype(f32)
        bias = parts[0:1] + parts[1:2] + parts[2:3]

        def up(r, t):
            rows = pl.ds(pl.multiple_of(r * block, block), block)
            u, slope = gelu_both(dot(low_ref[rows, :], win_ref[i]) + bias)
            slope_ref[i, rows, :] = slope.astype(bf16)
            sum_ref[rows, :] += dot(u.astype(bf16), wback_ref[i, :width, :])
            return t

        lax.fori_loop(0, rows_all // block, up, 0)

    @pl.when(i == nfar)
    def _():
        get_n1.wait()

    @pl.when((i >= nfar) & (i < nfar + nr))
    def _():
        rows = pl.ds(pl.multiple_of((i - nfar) * block, block), block)
        h1 = n1_ref[rows, :] * row(3) + row(4)
        n2, rs2 = normed(h1 + (sum_ref[rows, :] + row(5)))
        act_ref[...] = n2 * row(6) + row(7)
        dy = cot_ref[...].astype(f32) * jnp.where(pad_ref[...] >= 0, 1.0, 0.0)
        add_stat(6, dy * n2)
        add_stat(7, dy)
        dr2 = norm_back(n2, rs2, dy * row(6))
        add_stat(5, dr2)
        sum_ref[rows, :] = dr2
        low_ref[rows, :] = dr2.astype(bf16)

    last = nfar + nr + nchunk

    @pl.when((i >= nfar + nr) & (i < last))
    def _():
        j = i - nfar - nr
        for n in range(nfar, nchunk):

            @pl.when(j == n)
            def _(n=n):
                wait(n)

        owner = lax.rem(j + nchunk - nfar, nchunk) ^ me_ref[0]
        each = low_ref.shape[1] // width
        place = (pl.ds(8 + owner // each, 1), pl.ds(pl.multiple_of(lax.rem(owner, each) * width, width), width))
        for r in range(rows_all // span):
            rows = slice(r * span, (r + 1) * span)
            dz = dot(low_ref[rows, :], wback_ref[j, :width, :], NT) * slope_ref[j, rows, :].astype(f32)
            grad = jnp.sum(dz, axis=0, keepdims=True)
            if nfar:
                stat_ref[place] += grad
            else:
                for n in range(nchunk):

                    @pl.when(j == n)
                    def _(n=n, grad=grad):
                        stat_ref[8 + n // each : 9 + n // each, n % each * width : (n % each + 1) * width] += grad

            sum_ref[rows, :] += dot(dz.astype(bf16), win_ref[j], NT)

    @pl.when(i >= last)
    def _():
        rows = pl.ds(pl.multiple_of((i - last) * block, block), block)
        n1 = n1_ref[rows, :]
        dh1 = sum_ref[rows, :]
        add_stat(3, dh1 * n1)
        add_stat(4, dh1)
        dr1 = norm_back(n1, rs1_ref[rows, :], dh1 * row(3))
        add_stat(2, dr1)
        dr1_ref[...] = dr1
        da = dot(dr1.astype(bf16), wout_ref[...], NT).astype(bf16)
        da_ref[...] = da
        add_stat(1, da.astype(f32))


def feed_down(me, low, n1, f, rs1, cot, padcol, wout, pm, src, plan, slopes, nfar, width, block=512, span=512):
    rows, d = low.shape
    nchunk = len(plan)
    block, span = min(block, rows), min(span, rows)
    nr = rows // block
    last = nfar + nr + nchunk
    once = lambda s: pl.BlockSpec(s, lambda i, me: (0,) * len(s), pipeline_mode=pl.Buffered(1))
    early = lambda w: pl.BlockSpec((block, w), lambda i, me: (jnp.clip(i - nfar, 0, nr - 1), 0))
    late = lambda: pl.BlockSpec((block, d), lambda i, me: (jnp.maximum(i - last, 0), 0))
    hbm = lambda: pl.BlockSpec(memory_space=pl.ANY)
    return pl.pallas_call(
        functools.partial(down_kernel, plan, len(src), nfar, nr, span),
        out_shape=(jax.ShapeDtypeStruct((rows, d), f32), jax.ShapeDtypeStruct((rows, d), f32),
                   jax.ShapeDtypeStruct((rows, d), bf16), jax.ShapeDtypeStruct((8 + nchunk * width // d, d), f32)),
        grid_spec=pltpu.PrefetchScalarGridSpec(
        num_scalar_prefetch=1,
        grid=(last + nr,),
        in_specs=[hbm(), hbm(), hbm(), once((rows, 1)), early(d), early(1), once((d, d)), once((8, d))]
        + [hbm() for _ in src] + [hbm()],
        out_specs=[early(d), late(), late(), pl.BlockSpec((8 + nchunk * width // d, d), lambda i, me: (0, 0))],
        scratch_shapes=[pltpu.VMEM((nchunk, d, width), bf16), pltpu.VMEM((nchunk, width + 16, d), bf16),
                        pltpu.SemaphoreType.DMA((d // width + 1, nchunk)), pltpu.VMEM((nchunk, rows, width), bf16),
                        pltpu.SemaphoreType.DMA((nchunk,)), pltpu.VMEM((rows, d), bf16), pltpu.VMEM((rows, d), f32),
                        pltpu.VMEM((rows, d), f32), pltpu.SemaphoreType.DMA((3,))]),
        compiler_params=pltpu.CompilerParams(vmem_limit_bytes=57 << 20 if nfar else 62 << 20),
        cost_estimate=pl.CostEstimate(flops=rows * d, bytes_accessed=8 * d, transcendentals=0),
        name="feed_down",
    )(me, low, n1, f, rs1, cot, padcol, wout, pm, *src, slopes)


def adam_step(grad, first, second, param, average):
    first_new = 0.5 * first + 0.5 * grad
    second_new = 0.5 * second + 0.5 * grad * grad
    corr = 1.0 - 0.5**STEP
    param_new = param - 0.25 * (
        first_new / corr / (jnp.sqrt(second_new / corr) + 1e-08) + 0.01 * param
    )
    return (
        first_new,
        second_new,
        param_new,
        param_new.astype(jnp.bfloat16),
        0.8 * average + 0.2 * param_new,
    )


def exchange(v, axis, bit):
    size = lax.axis_size(axis)
    return lax.ppermute(v, axis, [(i, i ^ bit) for i in range(size)])


def bits(size):
    return [1 << b for b in range(size.bit_length() - 1)]


def total_sum(v):
    if lax.axis_size("mp") == 8 and lax.axis_size("dp") == 4:
        v = v + exchange(v, "mp", 1)
        v = (v + exchange(v, "mp", 2)) + (exchange(v, "mp", 4) + exchange(v, "mp", 6))
        v = v + exchange(v, "dp", 1)
        return v + exchange(v, "dp", 2)
    for axis in ("mp", "dp"):
        for bit in bits(lax.axis_size(axis)):
            v = v + exchange(v, axis, bit)
    return v


def on_device(
    tokens,
    segment_ids,
    pad_mask,
    cotangent,
    w_query,
    w_key,
    w_value,
    w_out,
    w_in,
    w_back,
    params_main,
    params_hidden,
    first_main,
    second_main,
    first_hidden,
    second_hidden,
    average_main,
    average_hidden,
):
    rows_all, d = tokens.shape
    width = params_hidden.shape[0]
    devices = lax.axis_size("mp")
    me = lax.axis_index("mp")
    total_hidden = width * devices
    seg, pad = segment_ids[0], pad_mask[0]

    rounded = lambda v: lax.reduce_precision(v, 8, 7)
    high = rounded(params_hidden)
    middle = rounded(params_hidden - high)
    rows = jnp.stack([high, middle, rounded(params_hidden - high - middle)]).astype(bf16)
    packed = jnp.concatenate([w_in[g * width : (g + 1) * width] for g in range(d // width)], axis=1)
    own = jnp.concatenate([packed, w_back, jnp.pad(rows, ((0, 13), (0, d - width)))], axis=0)
    cube = devices == 8
    hop = lambda v, bit: exchange(v, "mp", bit)
    core, along_x, along_y = 1, 2, 4
    if cube:
        by_x, by_y, by_core = hop(own, along_x), hop(own, along_y), hop(own, core)

    win = windows(seg, BLK, ALLOWED)
    segcol = jnp.where(pad == 1, seg, -1)[:, None]
    segrow = seg[None, :]
    query = (0.125 * (dot(tokens, w_query) + params_main[0])).astype(bf16)
    keys = dot(tokens, w_key).astype(bf16)
    values = (dot(tokens, w_value) + params_main[1]).astype(bf16)
    mixed, lse = attn_fwd(query, keys, values, win, segcol, segrow, (0, d // PAIR))
    if cube:
        by_x, by_y, by_core, mixed = lax.optimization_barrier((by_x, by_y, by_core, mixed))
        far_in, far_back = hop(by_y[:width], along_x), hop(by_x[width:], along_y)
        near = [own, by_core, by_x, hop(by_x, core), by_y, hop(by_y, core)]
        normal_one, factor_one, low = out_norm(mixed, tokens, w_out, params_main)
        plan = tuple(((n, 0, 0), (n, 0, width)) for n in range(6))
        first = [p[None] for p in near]
        partial, slopes = feed_up(low, first, plan, width)
        far_in, far_back, partial = lax.optimization_barrier((far_in, far_back, partial))
        rest = [p[None] for p in (far_in, far_back, hop(far_in, core), hop(far_back, core))]
        far_plan = (((0, 0, 0), (1, 0, 0)), ((2, 0, 0), (3, 0, 0)))
        sources = first + rest
        plan = tuple(((6 + n[0],) + n[1:], (6 + m[0],) + m[1:]) for n, m in far_plan) + plan
        far, order = 2, me
    else:
        sources = [lax.all_gather(own, "mp", axis=0)]
        plan = tuple(((0, j, 0), (0, j, width)) for j in range(devices))
        normal_one, factor_one, low = out_norm(mixed, tokens, w_out, params_main)
        partial, slopes = feed_up(low, sources, plan, width)
        far, order = 0, jnp.zeros_like(me)
    activations, dresid_one, dmixed, stats = feed_down(
        order[None].astype(jnp.int32), low, normal_one, partial, factor_one, cotangent, segcol, w_out, params_main, sources, plan, slopes, far, width
    )
    input_grad, local = attn_bwd(
        query, keys, values, mixed, dmixed, lse, win, segcol, segrow, dresid_one, stats, w_query, w_key, w_value
    )
    total = total_sum(local)
    grad_norm = jnp.sqrt(jnp.sum(total * total))
    grad_main = total[:8]
    grad_hid = lax.dynamic_slice_in_dim(total[8:].reshape(total_hidden), me * width, width, 0)
    tokens_all = rows_all * lax.axis_size("dp") * devices
    limit = 0.01 * math.sqrt(tokens_all * (8 * d + total_hidden))
    scale_factor = jnp.minimum(1.0, limit / (grad_norm + 1e-06))
    grad_main = grad_main * scale_factor
    grad_hid = grad_hid * scale_factor
    fm, sm, pm, cm, am = adam_step(grad_main, first_main, second_main, params_main, average_main)
    fh, sh, ph, ch, ah = adam_step(grad_hid, first_hidden, second_hidden, params_hidden, average_hidden)
    return (
        activations,
        input_grad,
        grad_norm,
        grad_main,
        grad_hid,
        fm,
        sm,
        fh,
        sh,
        pm,
        ph,
        cm,
        ch,
        am,
        ah,
    )


def solution(mesh):
    placed = (
        P(("dp", "mp"), None),
        P(("dp", "mp"), None),
        P(("dp", "mp"), None),
        P(("dp", "mp"), None),
        P(),
        P(),
        P(),
        P(),
        P(None, "mp"),
        P("mp", None),
        P(),
        P("mp"),
        P(),
        P(),
        P("mp"),
        P("mp"),
        P(),
        P("mp"),
    )
    return jax.shard_map(
        on_device,
        mesh=mesh,
        in_specs=placed,
        out_specs=(
            P(("dp", "mp"), None),
            P(("dp", "mp"), None),
            P(),
            P(),
            P("mp"),
            P(),
            P(),
            P("mp"),
            P("mp"),
            P(),
            P("mp"),
            P(),
            P("mp"),
            P(),
            P("mp"),
        ),
        check_vma=False,
    )
```
